32 devices in a mesh: fsdp: 16 (over z, y, x), rep: 2 (over core).
Axes of the slice: x: 2, y: 2, z: 4, core: 2. Of those that a mesh axis runs over, the one named last changes fastest.
Arguments:
- tokens: bfloat16 [32, 512, 768], P(('fsdp', 'rep')), may hold values from -6 to 6
- boxes: int32 [32, 2, 512], P(('fsdp', 'rep')), may hold values from 0 to 999
- lengths: int32 [32], P(('fsdp', 'rep')), may hold values from 40 to 512, as said below
- cotangent: bfloat16 [32, 512, 768], P(('fsdp', 'rep')), may hold values from -6 to 6
- attn_weight: float32 [5, 768, 768], P(None, 'fsdp')
- up_weight: float32 [768, 3072], P('fsdp'), may hold values from -0.21875 to 0.21875
- down_weight: float32 [3072, 768], P('fsdp'), may hold values from -0.109375 to 0.109375
- vectors: float32 [12, 768], P(None, 'fsdp')
- attn_first: float32 [5, 768, 768], P(None, 'fsdp')
- up_first: float32 [768, 3072], P('fsdp')
- down_first: float32 [3072, 768], P('fsdp')
- vector_first: float32 [12, 768], P(None, 'fsdp')
- attn_second: float32 [5, 768, 768], P(None, 'fsdp')
- up_second: float32 [768, 3072], P('fsdp')
- down_second: float32 [3072, 768], P('fsdp')
- vector_second: float32 [12, 768], P(None, 'fsdp')
Outputs:
- layer_out: bfloat16 [32, 512, 768], P(('fsdp', 'rep'))
- token_grad: float32 [32, 512, 768], P(('fsdp', 'rep'))
- attn_new: float32 [5, 768, 768], P(None, 'fsdp')
- up_new: float32 [768, 3072], P('fsdp')
- down_new: float32 [3072, 768], P('fsdp')
- vectors_new: float32 [12, 768], P(None, 'fsdp')
- attn_first_new: float32 [5, 768, 768], P(None, 'fsdp')
- up_first_new: float32 [768, 3072], P('fsdp')
- down_first_new: float32 [3072, 768], P('fsdp')
- vector_first_new: float32 [12, 768], P(None, 'fsdp')
- attn_second_new: float32 [5, 768, 768], P(None, 'fsdp')
- up_second_new: float32 [768, 3072], P('fsdp')
- down_second_new: float32 [3072, 768], P('fsdp')
- vector_second_new: float32 [12, 768], P(None, 'fsdp')
- attn_copy: bfloat16 [5, 768, 768], P(None, 'fsdp')
- up_copy: bfloat16 [768, 3072], P('fsdp')
- down_copy: bfloat16 [3072, 768], P('fsdp')
- vector_copy: bfloat16 [12, 768], P(None, 'fsdp')
The draws below stay inside these ranges and needn't reach their ends.
Inputs may be any that keep to these rules, and one draw needn't show every extreme that they name: `lengths`: some page has exactly 512 real tokens and another exactly 40.
All inputs are finite; a program needn't handle non-finite values.
Results may differ from the reference program's by a relative error of at most 0.014.
The reference program's roundings to bfloat16 on the way count: a program that leaves them out, or rounds other values in their place, can miss the bound.
Values may be sent and summed in bfloat16 or wider, within the bound.
No kernel may reach another device: no remote copies, remote signals or barrier semaphores. Data moves between devices by JAX's collectives and lax.ppermute only.
A program may use at most 192 MiB of HBM per device.

```python
import math
import jax
import jax.numpy as jnp
from jax import lax

HEADS = 12
HEAD_DIM = 64
FF = 3072
D = 768
PAGE = 512
MIN_LEN = 40
PAGES = 32
STEP = 7


ATTN_KINDS = (0.5, 0.5, 0.33, 0.3, 0.35)


VECTOR_KINDS = (0.9, 0.9, 1.0, 1.0, 0.5, 0.33, 0.65, 0.8)


UP_BIAS_KIND = 0.22


UP_WEIGHT_TYPE = 0.22


DOWN_KIND = 0.52


def summed_rows():
    return math.sqrt(PAGES * (PAGE + MIN_LEN) / 2.0)


def attn_scales():
    return jnp.array(ATTN_KINDS, jnp.float32)[:, None, None] * summed_rows()


def vector_scales():
    kinds = jnp.concatenate([jnp.array(VECTOR_KINDS, jnp.float32), jnp.full((FF // D,), UP_BIAS_KIND, jnp.float32)])
    return kinds[:, None] * summed_rows()


def moment_first(key, shape, scale):
    base = jax.random.normal(key, shape, jnp.float32)
    return base * scale


def moment_second(key, shape, scale):
    factor = jnp.exp(jax.random.uniform(key, shape, jnp.float32, math.log(0.5), math.log(8.0)))
    return factor * scale * scale


def draw_lengths(key, part):
    drawn = jax.random.randint(jax.random.fold_in(key, 11), (PAGES,), MIN_LEN, PAGE + 1)
    longest = jax.random.randint(jax.random.fold_in(key, 12), (), 0, PAGES)
    offset = jax.random.randint(jax.random.fold_in(key, 13), (), 1, PAGES)
    shortest = (longest + offset) % PAGES
    position = jnp.arange(PAGES)
    drawn = jnp.where(position == longest, PAGE, drawn)
    return jnp.where(position == shortest, MIN_LEN, drawn).astype(jnp.int32)


def draw_attn_weight(key, part):
    spread_row = jnp.array([1.0, 1.0, 3.0, 2.0, 1.0], jnp.float32)[:, None, None] * D ** (-0.5)
    base = jax.random.normal(key, (5, D, D), jnp.float32)
    return base * spread_row


def draw_vectors(key, part):
    row_total = 8 + FF // D
    base = jax.random.normal(key, (row_total, D), jnp.float32)
    position = jnp.arange(row_total)[:, None]
    gain_rows = (position == 0) | (position == 2)
    shift_scale = jnp.where(position == 5, 0.9, 0.3)
    return jnp.where(gain_rows, 1.0 + 0.15 * base, shift_scale * base)


def draw_attn_first(key, part):
    return moment_first(key, (5, D, D), attn_scales())


def draw_up_first(key, part):
    return moment_first(key, (D, FF), UP_WEIGHT_TYPE * summed_rows())


def draw_down_first(key, part):
    return moment_first(key, (FF, D), DOWN_KIND * summed_rows())


def draw_vector_first(key, part):
    return moment_first(key, (8 + FF // D, D), vector_scales())


def draw_attn_second(key, part):
    return moment_second(key, (5, D, D), attn_scales())


def draw_up_second(key, part):
    return moment_second(key, (D, FF), UP_WEIGHT_TYPE * summed_rows())


def draw_down_second(key, part):
    return moment_second(key, (FF, D), DOWN_KIND * summed_rows())


def draw_vector_second(key, part):
    return moment_second(key, (8 + FF // D, D), vector_scales())


def plant(entries, stream_key, smallest, high):
    index_at = [jax.random.randint(jax.random.fold_in(stream_key, axis), (), 0, length) for axis, length in enumerate(entries.shape)]
    widest = entries.shape.index(max(entries.shape))
    next_to = index_at[:widest] + [(index_at[widest] + 1) % entries.shape[widest]] + index_at[widest + 1:]
    return entries.at[tuple(index_at)].set(smallest).at[tuple(next_to)].set(high)


def level_of(rng, shape, split, smallest, top_value):
    level, own = 1.0, jax.random.fold_in(rng, 6)
    for dim, parts in split:
        draws = jnp.exp(jax.random.uniform(jax.random.fold_in(own, dim), (parts,), jnp.float32, smallest / len(split), top_value / len(split)))
        level = level * jnp.repeat(draws, shape[dim] // parts).reshape([-1 if axis == dim else 1 for axis in range(len(shape))])
    return level


def gaussian(key, dims, deviation, bound, split=(), dtype=jnp.bfloat16):
    level = level_of(key, dims, split, -0.22, 0.18) if split else 1.0
    values = jax.random.normal(key, dims, jnp.float32) * deviation * level
    return jnp.minimum(jnp.maximum(values, -bound), bound).astype(dtype)


def setup_inputs(seed: int = 0) -> dict:
    seeds = jax.random.split(jax.random.key(seed), 17)
    return {
        "tokens": gaussian(seeds[0], (PAGES, PAGE, D), 1.0, 6.0, ((0, 32),)),
        "boxes": plant(jax.random.randint(seeds[1], (PAGES, 2, PAGE), 0, 1000), jax.random.fold_in(seeds[1], 1), 0, 999).astype(jnp.int32),
        "lengths": draw_lengths(jax.random.fold_in(seeds[16], 71), 0),
        "cotangent": gaussian(seeds[3], (PAGES, PAGE, D), 1.0, 6.0, ((0, 32),)),
        "attn_weight": draw_attn_weight(jax.random.fold_in(seeds[16], 71), 0),
        "up_weight": gaussian(seeds[5], (D, FF), D ** -0.5, 0.21875, ((0, 16),), jnp.float32),
        "down_weight": gaussian(seeds[6], (FF, D), FF ** -0.5, 0.109375, ((0, 16),), jnp.float32),
        "vectors": draw_vectors(jax.random.fold_in(seeds[16], 71), 0),
        "attn_first": draw_attn_first(jax.random.fold_in(seeds[16], 71), 0),
        "up_first": draw_up_first(jax.random.fold_in(seeds[16], 71), 0),
        "down_first": draw_down_first(jax.random.fold_in(seeds[16], 71), 0),
        "vector_first": draw_vector_first(jax.random.fold_in(seeds[16], 71), 0),
        "attn_second": draw_attn_second(jax.random.fold_in(seeds[16], 71), 0),
        "up_second": draw_up_second(jax.random.fold_in(seeds[16], 71), 0),
        "down_second": draw_down_second(jax.random.fold_in(seeds[16], 71), 0),
        "vector_second": draw_vector_second(jax.random.fold_in(seeds[16], 71), 0),
    }


EPS_NORM = 1e-12
EPS_ADAM = 1e-08
DECAY = 0.5
MASK_FILL = -1e+30
WEIGHT_DECAY = 0.01
ATTN_RATES = (0.04, 0.04, 0.04, 0.2, 0.04)
UP_RATE = 0.04
DOWN_RATE = 0.02
VECTOR_RATE = 0.3
largest_value = lax.Precision.HIGHEST

@jax.custom_vjp
def low(v):
    return lax.optimization_barrier(v.astype(jnp.bfloat16)).astype(jnp.float32)

@jax.custom_vjp
def low_back(v):
    return v

def low_keep(v):
    return (low(v), None)

def low_pass(kept, grad):
    return (grad,)

def back_keep(v):
    return (v, None)

def back_low(kept, grad):
    return (low(grad),)
low.defvjp(low_keep, low_pass)
low_back.defvjp(back_keep, back_low)

def layer_norm(hidden, gain_row, shift_row):
    center = hidden - lax.optimization_barrier(jnp.mean(hidden, axis=-1, keepdims=True))
    spread = lax.optimization_barrier(jnp.mean(center * center, axis=-1, keepdims=True))
    return center * lax.rsqrt(spread + EPS_NORM) * gain_row + shift_row

def box_tables(box_rows, model_width):
    quarter = model_width // 4
    frequency = jnp.exp(jnp.arange(quarter).astype(jnp.float32) * (-math.log(10000.0) / quarter))
    angles = box_rows.astype(jnp.float32)[:, :, None] * frequency
    return (jnp.sin(angles), jnp.cos(angles))

def encode(sine_rows, cosine_rows):
    return jnp.concatenate([sine_rows[0], cosine_rows[0], sine_rows[1], cosine_rows[1]], axis=-1)

def rotate(pos_table, sine_rows, cosine_rows):
    quarter = sine_rows.shape[-1]
    pieces = []
    for coord in range(2):
        sine_part = pos_table[..., 2 * coord * quarter:(2 * coord + 1) * quarter]
        cosine_part = pos_table[..., (2 * coord + 1) * quarter:(2 * coord + 2) * quarter]
        pieces.append(cosine_part * sine_rows[coord] - sine_part * cosine_rows[coord])
        pieces.append(sine_part * sine_rows[coord] + cosine_part * cosine_rows[coord])
    return jnp.concatenate(pieces, axis=-1)

def page_forward(weights, token_row_block, box_rows, page_length):
    attention_matrices, up_mat, down_mat, vector_rows = weights
    row_count, model_width = token_row_block.shape
    page_live = jnp.arange(row_count) < page_length
    projected_rows = jnp.einsum('tb,mby->mty', token_row_block, attention_matrices[:3], precision=largest_value)
    query_rows = low(low_back(projected_rows[0] + vector_rows[4])).reshape(row_count, HEADS, HEAD_DIM)
    key_rows = low(low_back(projected_rows[1])).reshape(row_count, HEADS, HEAD_DIM)
    value_rows = low(low_back(projected_rows[2] + vector_rows[5])).reshape(row_count, HEADS, HEAD_DIM)
    sine_rows, cosine_rows = box_tables(box_rows, model_width)
    encoded = low(encode(sine_rows, cosine_rows))
    rel_heads = attention_matrices[4].reshape(model_width, HEADS, HEAD_DIM)
    pos_table = low_back(jnp.einsum('ihd,ehd->hie', query_rows, rel_heads, precision=largest_value))
    left_rows = low(rotate(pos_table, sine_rows, cosine_rows))
    text_part = jnp.einsum('ihd,jhd->hij', query_rows, key_rows, precision=largest_value)
    place_part = jnp.einsum('hie,je->hij', left_rows, encoded, precision=largest_value)
    score_rows = low_back((text_part + place_part) * HEAD_DIM ** (-0.5))
    score_rows = jnp.where(page_live[None, None, :], score_rows, MASK_FILL)
    row_top = lax.optimization_barrier(jnp.max(score_rows, axis=-1, keepdims=True))
    exponent = jnp.exp(score_rows - row_top)
    prob_rows = exponent / lax.optimization_barrier(jnp.sum(exponent, axis=-1, keepdims=True))
    mixed_rows = jnp.einsum('hij,jhd->ihd', low(prob_rows), value_rows, precision=largest_value)
    context = low(low_back(mixed_rows.reshape(row_count, model_width)))
    attn_out = low_back(jnp.dot(context, attention_matrices[3], precision=largest_value) + vector_rows[6])
    first_sum = token_row_block + attn_out
    normed = layer_norm(first_sum, vector_rows[0], vector_rows[1])
    pre_act = low_back(jnp.dot(low(normed), up_mat, precision=largest_value) + vector_rows[8:].reshape(-1))
    act_rows = jax.nn.gelu(pre_act, approximate=False)
    ffn_out = low_back(jnp.dot(low(act_rows), down_mat, precision=largest_value) + vector_rows[7])
    second_sum = normed + ffn_out
    return layer_norm(second_sum, vector_rows[2], vector_rows[3]) * page_live[:, None]

def adam_update(weight, first, second, grad, rate, decay_weight):
    first_new = DECAY * first + (1.0 - DECAY) * grad
    second_new = DECAY * second + (1.0 - DECAY) * grad * grad
    correction = 1.0 - DECAY ** STEP
    direction = first_new / correction / (jnp.sqrt(second_new / correction) + EPS_ADAM)
    return (weight - rate * (direction + decay_weight * weight), first_new, second_new)

def reference(tokens, boxes, lengths, cotangent, attn_weight, up_weight, down_weight, vectors, attn_first, up_first, down_first, vector_first, attn_second, up_second, down_second, vector_second):

    def forward_all(token_rows_full, attn_param, up_param, down_param, vector_param):
        weights = (low(attn_param), low(up_param), low(down_param), low(vector_param))

        def page_step(carry, page):
            token_row_block, box_rows, page_length = page
            return (carry, page_forward(weights, token_row_block, box_rows, page_length))
        _, page_outs = lax.scan(jax.checkpoint(page_step), None, (token_rows_full, boxes, lengths))
        return page_outs
    layer_out, pull = jax.vjp(forward_all, tokens.astype(jnp.float32), attn_weight, up_weight, down_weight, vectors)
    token_grad, attn_grad, up_grad, down_grad, vector_grad = pull(cotangent.astype(jnp.float32))
    attn_rates = jnp.array(ATTN_RATES, jnp.float32)[:, None, None]
    attn_new, attn_first_new, attn_second_new = adam_update(attn_weight, attn_first, attn_second, attn_grad, attn_rates, WEIGHT_DECAY)
    up_new, up_first_new, up_second_new = adam_update(up_weight, up_first, up_second, up_grad, UP_RATE, WEIGHT_DECAY)
    down_new, down_first_new, down_second_new = adam_update(down_weight, down_first, down_second, down_grad, DOWN_RATE, WEIGHT_DECAY)
    vectors_new, vector_first_new, vector_second_new = adam_update(vectors, vector_first, vector_second, vector_grad, VECTOR_RATE, 0.0)
    return (layer_out.astype(jnp.bfloat16), token_grad, attn_new, up_new, down_new, vectors_new, attn_first_new, up_first_new, down_first_new, vector_first_new, attn_second_new, up_second_new, down_second_new, vector_second_new, attn_new.astype(jnp.bfloat16), up_new.astype(jnp.bfloat16), down_new.astype(jnp.bfloat16), vectors_new.astype(jnp.bfloat16))
```

```python
from functools import partial
import math

import jax
import jax.numpy as jnp
from jax import lax
from jax.sharding import PartitionSpec as P

HEADS = 12
HEAD_DIM = 64
STEP = 7


EPS_NORM = 1e-12
EPS_ADAM = 1e-08
DECAY = 0.5
MASK_FILL = -1e30
WEIGHT_DECAY = 0.01
ATTN_RATES = (0.04, 0.04, 0.04, 0.2, 0.04)
UP_RATE = 0.04
DOWN_RATE = 0.02
VECTOR_RATE = 0.3


def contract(left_op, right_op, left_dim, right_dim):
    return lax.dot_general(
        left_op,
        right_op,
        (((left_dim,), (right_dim,)), ((), ())),
        preferred_element_type=jnp.float32,
    )


def layer_norm(hidden, gain_row, shift_row):
    center = hidden - jnp.mean(hidden, axis=-1, keepdims=True)
    spread = jnp.mean(center * center, axis=-1, keepdims=True)
    return center * lax.rsqrt(spread + EPS_NORM) * gain_row + shift_row


def box_tables(box_rows, model_width):
    quarter = model_width // 4
    frequency = jnp.exp(jnp.arange(quarter).astype(jnp.float32) * (-math.log(10000.0) / quarter))
    angles = box_rows.astype(jnp.float32)[:, :, None] * frequency
    return (jnp.sin(angles), jnp.cos(angles))


def encode(sine_rows, cosine_rows):
    return jnp.concatenate([sine_rows[0], cosine_rows[0], sine_rows[1], cosine_rows[1]], axis=-1)


def rotate(pos_table, sine_rows, cosine_rows):
    quarter = sine_rows.shape[-1]
    pieces = []
    for coord in range(2):
        sine_part = pos_table[..., 2 * coord * quarter : (2 * coord + 1) * quarter]
        cosine_part = pos_table[..., (2 * coord + 1) * quarter : (2 * coord + 2) * quarter]
        pieces.append(cosine_part * sine_rows[coord] - sine_part * cosine_rows[coord])
        pieces.append(sine_part * sine_rows[coord] + cosine_part * cosine_rows[coord])
    return jnp.concatenate(pieces, axis=-1)


def scores(query_rows, key_rows, left_rows, encoded, page_live):
    text_part = jnp.einsum("ihd,jhd->hij", query_rows, key_rows, preferred_element_type=jnp.float32)
    place_part = jnp.einsum("hie,je->hij", left_rows, encoded, preferred_element_type=jnp.float32)
    score_rows = (text_part + place_part) * HEAD_DIM ** (-0.5)
    return jnp.where(page_live[None, None, :], score_rows, MASK_FILL)


def forward_page(weights, token_row_block, box_rows, page_length):
    attention_matrices, up_mat, down_mat, vector_rows = weights
    row_count, model_width = token_row_block.shape
    vector_f32 = vector_rows.astype(jnp.float32)
    page_live = jnp.arange(row_count) < page_length
    projected_rows = jnp.einsum(
        "tb,mby->mty", token_row_block, attention_matrices[:3], preferred_element_type=jnp.float32
    )
    query_rows = (
        (projected_rows[0] + vector_f32[4]).astype(jnp.bfloat16).reshape(row_count, HEADS, HEAD_DIM)
    )
    key_rows = projected_rows[1].astype(jnp.bfloat16).reshape(row_count, HEADS, HEAD_DIM)
    value_rows = (
        (projected_rows[2] + vector_f32[5]).astype(jnp.bfloat16).reshape(row_count, HEADS, HEAD_DIM)
    )
    sine_rows, cosine_rows = box_tables(box_rows, model_width)
    encoded = encode(sine_rows, cosine_rows).astype(jnp.bfloat16)
    rel_heads = attention_matrices[4].reshape(model_width, HEADS, HEAD_DIM)
    pos_table = jnp.einsum(
        "ihd,ehd->hie", query_rows, rel_heads, preferred_element_type=jnp.float32
    )
    left_rows = rotate(pos_table, sine_rows, cosine_rows).astype(jnp.bfloat16)
    score_rows = scores(query_rows, key_rows, left_rows, encoded, page_live)
    row_top = jnp.max(score_rows, axis=-1, keepdims=True)
    exponent = jnp.exp(score_rows - row_top)
    row_total = jnp.sum(exponent, axis=-1, keepdims=True)
    prob_low = (exponent / row_total).astype(jnp.bfloat16)
    logsum = row_top + jnp.log(row_total)
    mixed_rows = jnp.einsum(
        "hij,jhd->ihd", prob_low, value_rows, preferred_element_type=jnp.float32
    )
    context = mixed_rows.reshape(row_count, model_width).astype(jnp.bfloat16)
    attn_out = (
        jnp.dot(context, attention_matrices[3], preferred_element_type=jnp.float32) + vector_f32[6]
    )
    first_sum = token_row_block.astype(jnp.float32) + attn_out
    normed = layer_norm(first_sum, vector_f32[0], vector_f32[1])
    pre_act = jnp.dot(
        normed.astype(jnp.bfloat16), up_mat, preferred_element_type=jnp.float32
    ) + vector_f32[8:].reshape(-1)
    act_low = jax.nn.gelu(pre_act, approximate=False).astype(jnp.bfloat16)
    second_sum = normed + (
        jnp.dot(act_low, down_mat, preferred_element_type=jnp.float32) + vector_f32[7]
    )
    page_out = (layer_norm(second_sum, vector_f32[2], vector_f32[3]) * page_live[:, None]).astype(
        jnp.bfloat16
    )
    saved_state = (
        query_rows,
        key_rows,
        value_rows,
        left_rows,
        logsum,
        context,
        first_sum,
        pre_act,
        act_low,
        second_sum,
    )
    return (page_out, saved_state)


def backward_page(weights, token_row_block, box_rows, page_length, upstream, saved_state):
    attention_matrices, up_mat, down_mat, vector_rows = weights
    (
        query_rows,
        key_rows,
        value_rows,
        left_rows,
        logsum,
        context,
        first_sum,
        pre_act,
        act_low,
        second_sum,
    ) = saved_state
    row_count, model_width = token_row_block.shape
    vector_f32 = vector_rows.astype(jnp.float32)
    page_live = jnp.arange(row_count) < page_length
    sine_rows, cosine_rows = box_tables(box_rows, model_width)
    encoded = encode(sine_rows, cosine_rows).astype(jnp.bfloat16)
    out_grad = upstream.astype(jnp.float32) * page_live[:, None]
    _, pull_second = jax.vjp(layer_norm, second_sum, vector_f32[2], vector_f32[3])
    second_grad, gain_two, shift_two = pull_second(out_grad)
    ffn_grad = second_grad.astype(jnp.bfloat16)
    down_grad = contract(act_low, ffn_grad, 0, 0)
    act_grad = contract(ffn_grad, down_mat, 1, 1)
    _, pull_gelu = jax.vjp(partial(jax.nn.gelu, approximate=False), pre_act)
    pre_grad = pull_gelu(act_grad)[0].astype(jnp.bfloat16)
    normed, pull_first = jax.vjp(layer_norm, first_sum, vector_f32[0], vector_f32[1])
    up_grad = contract(normed.astype(jnp.bfloat16), pre_grad, 0, 0)
    normed_grad = contract(pre_grad, up_mat, 1, 1) + second_grad
    first_grad, gain_one, shift_one = pull_first(normed_grad)
    attn_grad = first_grad.astype(jnp.bfloat16)
    out_mat_grad = contract(context, attn_grad, 0, 0)
    context_grad = (
        contract(attn_grad, attention_matrices[3], 1, 1)
        .astype(jnp.bfloat16)
        .reshape(row_count, HEADS, HEAD_DIM)
    )
    score_rows = scores(query_rows, key_rows, left_rows, encoded, page_live)
    prob_rows = jnp.exp(score_rows - logsum)
    value_grad = jnp.einsum(
        "hij,ihd->jhd",
        prob_rows.astype(jnp.bfloat16),
        context_grad,
        preferred_element_type=jnp.float32,
    ).astype(jnp.bfloat16)
    prob_grad = jnp.einsum(
        "ihd,jhd->hij", context_grad, value_rows, preferred_element_type=jnp.float32
    )
    score_grad = (
        prob_rows * (prob_grad - jnp.sum(prob_rows * prob_grad, axis=-1, keepdims=True))
    ).astype(jnp.bfloat16)
    score_scale = HEAD_DIM ** (-0.5)
    left_grad = (
        jnp.einsum("hij,je->hie", score_grad, encoded, preferred_element_type=jnp.float32)
        * score_scale
    )
    table_grad = rotate(left_grad, sine_rows, cosine_rows).astype(jnp.bfloat16)
    rel_heads = attention_matrices[4].reshape(model_width, HEADS, HEAD_DIM)
    rel_grad = jnp.einsum(
        "hie,ihd->ehd", table_grad, query_rows, preferred_element_type=jnp.float32
    ).reshape(model_width, model_width)
    query_grad = (
        jnp.einsum("hij,jhd->ihd", score_grad, key_rows, preferred_element_type=jnp.float32)
        * score_scale
    )
    query_grad = query_grad + jnp.einsum(
        "hie,ehd->ihd", table_grad, rel_heads, preferred_element_type=jnp.float32
    )
    key_grad = (
        jnp.einsum("hij,ihd->jhd", score_grad, query_rows, preferred_element_type=jnp.float32)
        * score_scale
    )
    stacked_layers = jnp.stack(
        [
            query_grad.astype(jnp.bfloat16).reshape(row_count, model_width),
            key_grad.astype(jnp.bfloat16).reshape(row_count, model_width),
            value_grad.reshape(row_count, model_width),
        ]
    )
    projection_gradient = jnp.einsum(
        "cg,yca->yga", token_row_block, stacked_layers, preferred_element_type=jnp.float32
    )
    token_grad = first_grad + jnp.einsum(
        "skl,scl->kc", stacked_layers, attention_matrices[:3], preferred_element_type=jnp.float32
    )
    column_sums = jnp.sum(stacked_layers.astype(jnp.float32), axis=1)
    attn_grads = jnp.concatenate([projection_gradient, out_mat_grad[None], rel_grad[None]], axis=0)
    small_rows = jnp.stack(
        [
            gain_one,
            shift_one,
            gain_two,
            shift_two,
            column_sums[0],
            column_sums[2],
            jnp.sum(attn_grad.astype(jnp.float32), axis=0),
            jnp.sum(ffn_grad.astype(jnp.float32), axis=0),
        ]
    )
    up_bias_rows = jnp.sum(pre_grad.astype(jnp.float32), axis=0).reshape(-1, model_width)
    vector_grad = jnp.concatenate([small_rows, up_bias_rows], axis=0)
    return (token_grad, (attn_grads, up_grad, down_grad, vector_grad))


def adam_update(weight, first, second, grad, rate, decay_weight):
    first_new = DECAY * first + (1.0 - DECAY) * grad
    second_new = DECAY * second + (1.0 - DECAY) * grad * grad
    correction = 1.0 - DECAY**STEP
    direction = first_new / correction / (jnp.sqrt(second_new / correction) + EPS_ADAM)
    return (weight - rate * (direction + decay_weight * weight), first_new, second_new)


AXES = ("fsdp", "rep")
ORDERS = ((8, 4, 2, 1), (8, 4, 1, 2))


def mask_table(order):
    masks = [0]
    for bit in order:
        masks = masks + [bit ^ m for m in masks]
    return masks


MASKS = tuple(mask_table(order) for order in ORDERS)


def inverse(masks):
    places = [0] * len(masks)
    for place, mask in enumerate(masks):
        places[mask] = place
    return places


PLACES = tuple(inverse(masks) for masks in MASKS)


def step_pairs(step):
    return [
        (chip * 2 + core, (chip ^ ORDERS[core][step]) * 2 + core)
        for chip in range(16)
        for core in range(2)
    ]


CORE_PAIRS = [(chip * 2 + core, chip * 2 + 1 - core) for chip in range(16) for core in range(2)]


def swap_cores(block):
    return lax.ppermute(block, AXES, CORE_PAIRS)


def gather_blocks(own_half):
    held = own_half[None]
    for step in range(4):
        held = jnp.concatenate([held, lax.ppermute(held, AXES, step_pairs(step))], axis=0)
    return held, swap_cores(held)


def in_order(mine, other):
    chip, core = lax.axis_index("fsdp"), lax.axis_index("rep")
    places = jnp.array(PLACES, jnp.int32)
    blocks = jnp.arange(16) ^ chip
    mine = jnp.take(mine, places[core][blocks], axis=0)
    other = jnp.take(other, places[1 - core][blocks], axis=0)
    first = jnp.where(core == 0, mine, other)
    second = jnp.where(core == 0, other, mine)
    return first, second


def scatter_blocks(first, second):
    chip, core = lax.axis_index("fsdp"), lax.axis_index("rep")
    masks = jnp.array(MASKS, jnp.int32)
    keep = jnp.where(core == 0, first, second)
    send = jnp.where(core == 0, second, first)
    keep = jnp.take(keep, masks[core] ^ chip, axis=0)
    send = jnp.take(send, masks[1 - core] ^ chip, axis=0)
    held = keep + swap_cores(send)
    for step in (3, 2, 1, 0):
        half = held.shape[0] // 2
        held = held[:half] + lax.ppermute(held[half:], AXES, step_pairs(step))
    mine = held[0]
    other = swap_cores(mine)
    first = jnp.where(core == 0, mine, other)
    second = jnp.where(core == 0, other, mine)
    return first, second


def local(
    tokens,
    boxes,
    lengths,
    cotangent,
    attn_weight,
    up_weight,
    down_weight,
    vectors,
    attn_first,
    up_first,
    down_first,
    vector_first,
    attn_second,
    up_second,
    down_second,
    vector_second,
):
    core = lax.axis_index("rep")
    attn_low = attn_weight.astype(jnp.bfloat16)
    up_low = up_weight.astype(jnp.bfloat16).reshape(48, 4, 768).transpose(1, 0, 2)
    down_low = down_weight.astype(jnp.bfloat16).reshape(4, 48, 768)
    vec_low = jnp.pad(vectors.astype(jnp.bfloat16), ((0, 4), (0, 768 - 48)))
    halves_one = jnp.stack([
        jnp.concatenate([attn_low[0], attn_low[1], vec_low]),
        jnp.concatenate([attn_low[2], attn_low[4], vec_low]),
    ])
    halves_two = jnp.stack([
        jnp.concatenate([attn_low[3, :, :384].reshape(24, 768), up_low[0], up_low[1]]),
        jnp.concatenate([attn_low[3, :, 384:].reshape(24, 768), up_low[2], up_low[3]]),
    ])
    halves_three = jnp.stack([
        jnp.concatenate([down_low[0], down_low[1]]),
        jnp.concatenate([down_low[2], down_low[3]]),
    ])
    def own(halves):
        return lax.dynamic_index_in_dim(halves, core, 0, keepdims=False)
    one = in_order(*gather_blocks(own(halves_one)))
    two = in_order(*gather_blocks(own(halves_two)))
    three = in_order(*gather_blocks(own(halves_three)))
    def square(piece, start):
        return piece[:, start:start + 48].reshape(768, 768)
    w_o = jnp.concatenate([p[:, :24].reshape(768, 384) for p in two], axis=1)
    attn_full = jnp.stack([square(one[0], 0), square(one[0], 48), square(one[1], 0), w_o, square(one[1], 48)])
    up_full = jnp.concatenate([square(p, 24 + 48 * i) for p in two for i in range(2)], axis=1)
    down_full = jnp.concatenate(three, axis=1).reshape(3072, 768)
    vec_full = one[0][:, 96:108, :48].transpose(1, 0, 2).reshape(12, 768)
    weights = (attn_full, up_full, down_full, vec_full)
    page_out, saved_state = forward_page(weights, tokens[0], boxes[0], lengths[0])
    layer_out = page_out[None]
    token_grad, (attn_grads, up_grad, down_grad, vector_grad) = backward_page(
        weights, tokens[0], boxes[0], lengths[0], cotangent[0], saved_state
    )
    token_grad = token_grad[None]
    def low(v):
        return v.astype(jnp.bfloat16)
    down_blocks = low(down_grad).reshape(16, 192, 768)
    three = scatter_blocks(down_blocks[:, :96], down_blocks[:, 96:])
    up_blocks = low(up_grad).reshape(16, 48, 4, 768).transpose(0, 2, 1, 3)
    attn_blocks = low(attn_grads).reshape(5, 16, 48, 768)
    o_blocks = attn_blocks[3]
    two = scatter_blocks(
        *(jnp.concatenate([o_blocks[:, :, 384 * i:384 * i + 384].reshape(16, 24, 768), up_blocks[:, 2 * i], up_blocks[:, 2 * i + 1]], axis=1)
        for i in range(2)))
    vec_blocks = jnp.pad(low(vector_grad).reshape(12, 16, 48).transpose(1, 0, 2), ((0, 0), (0, 4), (0, 720)))
    one = scatter_blocks(
        jnp.concatenate([attn_blocks[0], attn_blocks[1], vec_blocks], axis=1),
        jnp.concatenate([attn_blocks[2], attn_blocks[4], vec_blocks], axis=1))
    wide = [v.astype(jnp.float32) for v in (*one, *two, *three)]
    o_sum = jnp.concatenate([wide[2][:24].reshape(48, 384), wide[3][:24].reshape(48, 384)], axis=1)
    reduced = (
        jnp.stack([wide[0][:48], wide[0][48:96], wide[1][:48], o_sum, wide[1][48:96]]),
        jnp.concatenate([wide[2][24:72], wide[2][72:], wide[3][24:72], wide[3][72:]], axis=1),
        jnp.concatenate([wide[4], wide[5]], axis=0),
        wide[0][96:108, :48],
    )
    attn_rates = jnp.array(ATTN_RATES, jnp.float32)[:, None, None]
    attn_new, attn_first_new, attn_second_new = adam_update(
        attn_weight, attn_first, attn_second, reduced[0], attn_rates, WEIGHT_DECAY
    )
    up_new, up_first_new, up_second_new = adam_update(
        up_weight, up_first, up_second, reduced[1], UP_RATE, WEIGHT_DECAY
    )
    down_new, down_first_new, down_second_new = adam_update(
        down_weight, down_first, down_second, reduced[2], DOWN_RATE, WEIGHT_DECAY
    )
    vectors_new, vector_first_new, vector_second_new = adam_update(
        vectors, vector_first, vector_second, reduced[3], VECTOR_RATE, 0.0
    )
    return (
        layer_out,
        token_grad,
        attn_new,
        up_new,
        down_new,
        vectors_new,
        attn_first_new,
        up_first_new,
        down_first_new,
        vector_first_new,
        attn_second_new,
        up_second_new,
        down_second_new,
        vector_second_new,
        attn_new.astype(jnp.bfloat16),
        up_new.astype(jnp.bfloat16),
        down_new.astype(jnp.bfloat16),
        vectors_new.astype(jnp.bfloat16),
    )


def local_general(
    tokens,
    boxes,
    lengths,
    cotangent,
    attn_weight,
    up_weight,
    down_weight,
    vectors,
    attn_first,
    up_first,
    down_first,
    vector_first,
    attn_second,
    up_second,
    down_second,
    vector_second,
):
    lowered = (
        attn_weight.astype(jnp.bfloat16),
        up_weight.astype(jnp.bfloat16),
        down_weight.astype(jnp.bfloat16),
        vectors.astype(jnp.bfloat16),
    )
    gathered = (
        lax.all_gather(lowered[0], "fsdp", axis=1, tiled=True),
        lax.all_gather(lowered[1], "fsdp", axis=0, tiled=True),
        lax.all_gather(lowered[2], "fsdp", axis=0, tiled=True),
        lax.all_gather(lowered[3], "fsdp", axis=1, tiled=True),
    )

    def forward_step(carry, page):
        token_row_block, box_rows, page_length = page
        return (carry, forward_page(gathered, token_row_block, box_rows, page_length))

    _, (layer_out, saved_all) = lax.scan(forward_step, None, (tokens, boxes, lengths))
    backward_weights = (
        lax.all_gather(lowered[0], "fsdp", axis=1, tiled=True),
        lax.all_gather(lowered[1], "fsdp", axis=0, tiled=True),
        lax.all_gather(lowered[2], "fsdp", axis=0, tiled=True),
        lax.all_gather(lowered[3], "fsdp", axis=1, tiled=True),
    )
    model_width = gathered[0].shape[2]
    ffn_width = gathered[1].shape[1]
    zero_grads = (
        jnp.zeros((5, model_width, model_width), jnp.float32),
        jnp.zeros((model_width, ffn_width), jnp.float32),
        jnp.zeros((ffn_width, model_width), jnp.float32),
        jnp.zeros(gathered[3].shape, jnp.float32),
    )

    def backward_step(totals, page):
        token_row_block, box_rows, page_length, upstream, saved_state = page
        token_grad, grads = backward_page(
            backward_weights, token_row_block, box_rows, page_length, upstream, saved_state
        )
        return (jax.tree.map(jnp.add, totals, grads), token_grad)

    totals, token_grad = lax.scan(
        backward_step, zero_grads, (tokens, boxes, lengths, cotangent, saved_all)
    )
    shards = (
        lax.psum_scatter(totals[0], "fsdp", scatter_dimension=1, tiled=True),
        lax.psum_scatter(totals[1], "fsdp", scatter_dimension=0, tiled=True),
        lax.psum_scatter(totals[2], "fsdp", scatter_dimension=0, tiled=True),
        lax.psum_scatter(totals[3], "fsdp", scatter_dimension=1, tiled=True),
    )
    reduced = (
        lax.psum(shards[0].astype(jnp.bfloat16), "rep").astype(jnp.float32),
        lax.psum(shards[1].astype(jnp.bfloat16), "rep").astype(jnp.float32),
        lax.psum(shards[2].astype(jnp.bfloat16), "rep").astype(jnp.float32),
        lax.psum(shards[3].astype(jnp.bfloat16), "rep").astype(jnp.float32),
    )
    attn_rates = jnp.array(ATTN_RATES, jnp.float32)[:, None, None]
    attn_new, attn_first_new, attn_second_new = adam_update(
        attn_weight, attn_first, attn_second, reduced[0], attn_rates, WEIGHT_DECAY
    )
    up_new, up_first_new, up_second_new = adam_update(
        up_weight, up_first, up_second, reduced[1], UP_RATE, WEIGHT_DECAY
    )
    down_new, down_first_new, down_second_new = adam_update(
        down_weight, down_first, down_second, reduced[2], DOWN_RATE, WEIGHT_DECAY
    )
    vectors_new, vector_first_new, vector_second_new = adam_update(
        vectors, vector_first, vector_second, reduced[3], VECTOR_RATE, 0.0
    )
    return (
        layer_out,
        token_grad,
        attn_new,
        up_new,
        down_new,
        vectors_new,
        attn_first_new,
        up_first_new,
        down_first_new,
        vector_first_new,
        attn_second_new,
        up_second_new,
        down_second_new,
        vector_second_new,
        attn_new.astype(jnp.bfloat16),
        up_new.astype(jnp.bfloat16),
        down_new.astype(jnp.bfloat16),
        vectors_new.astype(jnp.bfloat16),
    )


def solution(mesh):
    blocked = mesh.shape["fsdp"] == 16 and mesh.shape["rep"] == 2
    return jax.shard_map(
        local if blocked else local_general,
        mesh=mesh,
        in_specs=(
            P(("fsdp", "rep"), None, None),
            P(("fsdp", "rep"), None, None),
            P(("fsdp", "rep")),
            P(("fsdp", "rep"), None, None),
            P(None, "fsdp", None),
            P("fsdp", None),
            P("fsdp", None),
            P(None, "fsdp"),
            P(None, "fsdp", None),
            P("fsdp", None),
            P("fsdp", None),
            P(None, "fsdp"),
            P(None, "fsdp", None),
            P("fsdp", None),
            P("fsdp", None),
            P(None, "fsdp"),
        ),
        out_specs=(
            P(("fsdp", "rep"), None, None),
            P(("fsdp", "rep"), None, None),
            P(None, "fsdp", None),
            P("fsdp", None),
            P("fsdp", None),
            P(None, "fsdp"),
            P(None, "fsdp", None),
            P("fsdp", None),
            P("fsdp", None),
            P(None, "fsdp"),
            P(None, "fsdp", None),
            P("fsdp", None),
            P("fsdp", None),
            P(None, "fsdp"),
            P(None, "fsdp", None),
            P("fsdp", None),
            P("fsdp", None),
            P(None, "fsdp"),
        ),
        check_vma=False,
    )
```

```python
from functools import partial
import math

import jax
import jax.numpy as jnp
from jax import lax
from jax.experimental import pallas as pl
from jax.experimental.pallas import tpu as pltpu
from jax.sharding import PartitionSpec as P

HEADS = 12
HEAD_DIM = 64
STEP = 7


EPS_NORM = 1e-12
EPS_ADAM = 1e-08
DECAY = 0.5
MASK_FILL = -1e30
WEIGHT_DECAY = 0.01
ATTN_RATES = (0.04, 0.04, 0.04, 0.2, 0.04)
UP_RATE = 0.04
DOWN_RATE = 0.02
VECTOR_RATE = 0.3


def contract(left_op, right_op, left_dim, right_dim):
    return lax.dot_general(
        left_op,
        right_op,
        (((left_dim,), (right_dim,)), ((), ())),
        preferred_element_type=jnp.float32,
    )


def layer_norm(hidden, gain_row, shift_row):
    center = hidden - jnp.mean(hidden, axis=-1, keepdims=True)
    spread = jnp.mean(center * center, axis=-1, keepdims=True)
    return center * lax.rsqrt(spread + EPS_NORM) * gain_row + shift_row


def box_tables(box_rows, model_width):
    quarter = model_width // 4
    frequency = jnp.exp(jnp.arange(quarter).astype(jnp.float32) * (-math.log(10000.0) / quarter))
    angles = box_rows.astype(jnp.float32)[:, :, None] * frequency
    return (jnp.sin(angles), jnp.cos(angles))


def encode(sine_rows, cosine_rows):
    return jnp.concatenate([sine_rows[0], cosine_rows[0], sine_rows[1], cosine_rows[1]], axis=-1)


def rotate(pos_table, sine_rows, cosine_rows):
    quarter = sine_rows.shape[-1]
    pieces = []
    for coord in range(2):
        sine_part = pos_table[..., 2 * coord * quarter : (2 * coord + 1) * quarter]
        cosine_part = pos_table[..., (2 * coord + 1) * quarter : (2 * coord + 2) * quarter]
        pieces.append(cosine_part * sine_rows[coord] - sine_part * cosine_rows[coord])
        pieces.append(sine_part * sine_rows[coord] + cosine_part * cosine_rows[coord])
    return jnp.concatenate(pieces, axis=-1)


def scores(query_rows, key_rows, left_rows, encoded, page_live):
    text_part = jnp.einsum("ihd,jhd->hij", query_rows, key_rows, preferred_element_type=jnp.float32)
    place_part = jnp.einsum("hie,je->hij", left_rows, encoded, preferred_element_type=jnp.float32)
    score_rows = (text_part + place_part) * HEAD_DIM ** (-0.5)
    return jnp.where(page_live[None, None, :], score_rows, MASK_FILL)


def forward_page(weights, token_row_block, box_rows, page_length):
    attention_matrices, up_mat, down_mat, vector_rows = weights
    row_count, model_width = token_row_block.shape
    vector_f32 = vector_rows.astype(jnp.float32)
    page_live = jnp.arange(row_count) < page_length
    projected_rows = jnp.einsum(
        "tb,mby->mty", token_row_block, attention_matrices[:3], preferred_element_type=jnp.float32
    )
    query_rows = (
        (projected_rows[0] + vector_f32[4]).astype(jnp.bfloat16).reshape(row_count, HEADS, HEAD_DIM)
    )
    key_rows = projected_rows[1].astype(jnp.bfloat16).reshape(row_count, HEADS, HEAD_DIM)
    value_rows = (
        (projected_rows[2] + vector_f32[5]).astype(jnp.bfloat16).reshape(row_count, HEADS, HEAD_DIM)
    )
    sine_rows, cosine_rows = box_tables(box_rows, model_width)
    encoded = encode(sine_rows, cosine_rows).astype(jnp.bfloat16)
    rel_heads = attention_matrices[4].reshape(model_width, HEADS, HEAD_DIM)
    pos_table = jnp.einsum(
        "ihd,ehd->hie", query_rows, rel_heads, preferred_element_type=jnp.float32
    )
    left_rows = rotate(pos_table, sine_rows, cosine_rows).astype(jnp.bfloat16)
    score_rows = scores(query_rows, key_rows, left_rows, encoded, page_live)
    row_top = jnp.max(score_rows, axis=-1, keepdims=True)
    exponent = jnp.exp(score_rows - row_top)
    row_total = jnp.sum(exponent, axis=-1, keepdims=True)
    prob_low = (exponent / row_total).astype(jnp.bfloat16)
    logsum = row_top + jnp.log(row_total)
    mixed_rows = jnp.einsum(
        "hij,jhd->ihd", prob_low, value_rows, preferred_element_type=jnp.float32
    )
    context = mixed_rows.reshape(row_count, model_width).astype(jnp.bfloat16)
    attn_out = (
        jnp.dot(context, attention_matrices[3], preferred_element_type=jnp.float32) + vector_f32[6]
    )
    first_sum = token_row_block.astype(jnp.float32) + attn_out
    normed = layer_norm(first_sum, vector_f32[0], vector_f32[1])
    pre_act = jnp.dot(
        normed.astype(jnp.bfloat16), up_mat, preferred_element_type=jnp.float32
    ) + vector_f32[8:].reshape(-1)
    act_low = jax.nn.gelu(pre_act, approximate=False).astype(jnp.bfloat16)
    second_sum = normed + (
        jnp.dot(act_low, down_mat, preferred_element_type=jnp.float32) + vector_f32[7]
    )
    page_out = (layer_norm(second_sum, vector_f32[2], vector_f32[3]) * page_live[:, None]).astype(
        jnp.bfloat16
    )
    saved_state = (
        query_rows,
        key_rows,
        value_rows,
        left_rows,
        logsum,
        context,
        first_sum,
        pre_act,
        act_low,
        second_sum,
    )
    return (page_out, saved_state)


def backward_page(weights, token_row_block, box_rows, page_length, upstream, saved_state):
    attention_matrices, up_mat, down_mat, vector_rows = weights
    (
        query_rows,
        key_rows,
        value_rows,
        left_rows,
        logsum,
        context,
        first_sum,
        pre_act,
        act_low,
        second_sum,
    ) = saved_state
    row_count, model_width = token_row_block.shape
    vector_f32 = vector_rows.astype(jnp.float32)
    page_live = jnp.arange(row_count) < page_length
    sine_rows, cosine_rows = box_tables(box_rows, model_width)
    encoded = encode(sine_rows, cosine_rows).astype(jnp.bfloat16)
    out_grad = upstream.astype(jnp.float32) * page_live[:, None]
    _, pull_second = jax.vjp(layer_norm, second_sum, vector_f32[2], vector_f32[3])
    second_grad, gain_two, shift_two = pull_second(out_grad)
    ffn_grad = second_grad.astype(jnp.bfloat16)
    down_grad = contract(act_low, ffn_grad, 0, 0)
    act_grad = contract(ffn_grad, down_mat, 1, 1)
    _, pull_gelu = jax.vjp(partial(jax.nn.gelu, approximate=False), pre_act)
    pre_grad = pull_gelu(act_grad)[0].astype(jnp.bfloat16)
    normed, pull_first = jax.vjp(layer_norm, first_sum, vector_f32[0], vector_f32[1])
    up_grad = contract(normed.astype(jnp.bfloat16), pre_grad, 0, 0)
    normed_grad = contract(pre_grad, up_mat, 1, 1) + second_grad
    first_grad, gain_one, shift_one = pull_first(normed_grad)
    attn_grad = first_grad.astype(jnp.bfloat16)
    out_mat_grad = contract(context, attn_grad, 0, 0)
    context_grad = (
        contract(attn_grad, attention_matrices[3], 1, 1)
        .astype(jnp.bfloat16)
        .reshape(row_count, HEADS, HEAD_DIM)
    )
    score_rows = scores(query_rows, key_rows, left_rows, encoded, page_live)
    prob_rows = jnp.exp(score_rows - logsum)
    value_grad = jnp.einsum(
        "hij,ihd->jhd",
        prob_rows.astype(jnp.bfloat16),
        context_grad,
        preferred_element_type=jnp.float32,
    ).astype(jnp.bfloat16)
    prob_grad = jnp.einsum(
        "ihd,jhd->hij", context_grad, value_rows, preferred_element_type=jnp.float32
    )
    score_grad = (
        prob_rows * (prob_grad - jnp.sum(prob_rows * prob_grad, axis=-1, keepdims=True))
    ).astype(jnp.bfloat16)
    score_scale = HEAD_DIM ** (-0.5)
    left_grad = (
        jnp.einsum("hij,je->hie", score_grad, encoded, preferred_element_type=jnp.float32)
        * score_scale
    )
    table_grad = rotate(left_grad, sine_rows, cosine_rows).astype(jnp.bfloat16)
    rel_heads = attention_matrices[4].reshape(model_width, HEADS, HEAD_DIM)
    rel_grad = jnp.einsum(
        "hie,ihd->ehd", table_grad, query_rows, preferred_element_type=jnp.float32
    ).reshape(model_width, model_width)
    query_grad = (
        jnp.einsum("hij,jhd->ihd", score_grad, key_rows, preferred_element_type=jnp.float32)
        * score_scale
    )
    query_grad = query_grad + jnp.einsum(
        "hie,ehd->ihd", table_grad, rel_heads, preferred_element_type=jnp.float32
    )
    key_grad = (
        jnp.einsum("hij,ihd->jhd", score_grad, query_rows, preferred_element_type=jnp.float32)
        * score_scale
    )
    stacked_layers = jnp.stack(
        [
            query_grad.astype(jnp.bfloat16).reshape(row_count, model_width),
            key_grad.astype(jnp.bfloat16).reshape(row_count, model_width),
            value_grad.reshape(row_count, model_width),
        ]
    )
    projection_gradient = jnp.einsum(
        "cg,yca->yga", token_row_block, stacked_layers, preferred_element_type=jnp.float32
    )
    token_grad = first_grad + jnp.einsum(
        "skl,scl->kc", stacked_layers, attention_matrices[:3], preferred_element_type=jnp.float32
    )
    column_sums = jnp.sum(stacked_layers.astype(jnp.float32), axis=1)
    attn_grads = jnp.concatenate([projection_gradient, out_mat_grad[None], rel_grad[None]], axis=0)
    small_rows = jnp.stack(
        [
            gain_one,
            shift_one,
            gain_two,
            shift_two,
            column_sums[0],
            column_sums[2],
            jnp.sum(attn_grad.astype(jnp.float32), axis=0),
            jnp.sum(ffn_grad.astype(jnp.float32), axis=0),
        ]
    )
    up_bias_rows = jnp.sum(pre_grad.astype(jnp.float32), axis=0).reshape(-1, model_width)
    vector_grad = jnp.concatenate([small_rows, up_bias_rows], axis=0)
    return (token_grad, (attn_grads, up_grad, down_grad, vector_grad))


def adam_update(weight, first, second, grad, rate, decay_weight):
    first_new = DECAY * first + (1.0 - DECAY) * grad
    second_new = DECAY * second + (1.0 - DECAY) * grad * grad
    correction = 1.0 - DECAY**STEP
    direction = first_new / correction / (jnp.sqrt(second_new / correction) + EPS_ADAM)
    return (weight - rate * (direction + decay_weight * weight), first_new, second_new)


AXES = ("fsdp", "rep")
ORDERS = ((8, 4, 2, 1), (8, 4, 1, 2))
LOW = jnp.bfloat16
WIDE = jnp.float32
CHUNK = 256
SLAB = 128
VMEM_BYTES = 58 * 1024 * 1024
CORE_AT, LENGTH_AT, PLACE_AT = 32, 33, 34


def mask_table(order):
    masks = [0]
    for bit in order:
        masks = masks + [bit ^ mask for mask in masks]
    return masks


def inverse(masks):
    places = [0] * len(masks)
    for place, mask in enumerate(masks):
        places[mask] = place
    return places


MASKS = tuple(mask_table(order) for order in ORDERS)
PLACES = tuple(inverse(masks) for masks in MASKS)
CORE_PAIRS = [(chip * 2 + core, chip * 2 + 1 - core) for chip in range(16) for core in range(2)]


def step_pairs(step):
    return [
        (chip * 2 + core, (chip ^ ORDERS[core][step]) * 2 + core)
        for chip in range(16)
        for core in range(2)
    ]


def swap_cores(block):
    return lax.ppermute(block, AXES, CORE_PAIRS)


def gather_mine(own_half):
    held = own_half[None]
    for step in range(4):
        held = jnp.concatenate([held, lax.ppermute(held, AXES, step_pairs(step))], axis=0)
    return held


def gather_blocks(own_half):
    held = gather_mine(own_half)
    return held, swap_cores(held)


def scatter_mine(held):
    for step in (3, 2, 1, 0):
        half = held.shape[0] // 2
        arrived = lax.ppermute(held[half:], AXES, step_pairs(step))
        held = held[:half] + arrived
    return held[0]


def scatter_blocks(keep, send):
    core = lax.axis_index("rep")
    mine = scatter_mine(keep + swap_cores(send))
    other = swap_cores(mine)
    first = jnp.where(core == 0, mine, other)
    second = jnp.where(core == 0, other, mine)
    return first.astype(WIDE), second.astype(WIDE)


def dot(left_op, right_op, left_dim, right_dim):
    return lax.dot_general(
        left_op,
        right_op,
        (((left_dim,), (right_dim,)), ((), ())),
        preferred_element_type=WIDE,
    )


def each(count, size, body):
    def step(index, carry):
        body(pl.ds(pl.multiple_of(index * size, size), size))
        return carry

    lax.fori_loop(0, count // size, step, 0)


def block_at(index):
    return pl.ds(pl.multiple_of(index * 48, 16), 48)


def turned(block):
    return (block & 3) | ((block & 4) << 1) | ((block & 8) >> 1)


def run_copies(make, count):
    def start(place, carry):
        for copy in make(place):
            copy.start()
        return carry

    def wait(place, carry):
        for copy in make(place):
            copy.wait()
        return carry

    lax.fori_loop(0, count, start, 0)
    lax.fori_loop(0, count, wait, 0)


def attn_copies(scal, mine, other, mats, sem, place):
    core = scal[CORE_AT]
    copies = []
    for source, base, half in ((mine, 0, core), (other, 16, 1 - core)):
        block = scal[base + place]
        for part in range(2):
            row = block if part == 0 else jnp.where(half == 1, turned(block), block)
            copies.append(
                pltpu.make_async_copy(
                    source.at[place, pl.ds(48 * part, 48)],
                    mats.at[2 * half + part, block_at(row)],
                    sem,
                )
            )
    return copies


def head_masks(dtype):
    lane = lax.broadcasted_iota(jnp.int32, (1, 128), 1)
    first = jnp.where(lane < 64, 1.0, 0.0)
    return (first.astype(dtype), (1.0 - first).astype(dtype))


def attend_kernel(
    scal,
    tokens,
    vec,
    sines,
    cosines,
    encoded,
    mine,
    other,
    q_out,
    k_out,
    v_out,
    ctx_out,
    prob_out,
    mats,
    right,
    sem,
):
    pair = pl.program_id(0)
    width = tokens.shape[1]
    rows = tokens.shape[0]

    @pl.when(pair == 0)
    def _():
        run_copies(partial(attn_copies, scal, mine, other, mats, sem), 16)
        right[:, :width] = encoded[...]

        def project(at):
            x = tokens[at, :]
            q_out[at, :] = (dot(x, mats[0], 1, 0) + vec[4:5, :]).astype(LOW)
            k_out[at, :] = dot(x, mats[1], 1, 0).astype(LOW)
            v_out[at, :] = (dot(x, mats[2], 1, 0) + vec[5:6, :]).astype(LOW)

        each(rows, CHUNK, project)

    lanes = pl.ds(pl.multiple_of(pair * 128, 128), 128)
    right[:, width:] = k_out[:, lanes]
    rel = mats[3, :, lanes]
    live = lax.broadcasted_iota(jnp.int32, (1, rows), 1) < scal[LENGTH_AT]
    half = width // 2

    def score(at):
        q_pair = q_out[at, :] if q_out.shape[1] == 128 else q_out[at, lanes]
        sin, cos = sines[at, :], cosines[at, :]
        mixed = []
        for head, mask in enumerate(head_masks(LOW)):
            q_head = q_pair * mask
            table = dot(q_head, rel, 1, 1)
            us, uc = table[:, :half], table[:, half:]
            left = jnp.concatenate(
                [(uc * sin - us * cos).astype(LOW), (us * sin + uc * cos).astype(LOW), q_head], axis=1
            )
            s = dot(left, right[...], 1, 1) * HEAD_DIM ** (-0.5)
            s = jnp.where(live, s, MASK_FILL)
            top = jnp.max(s, axis=-1, keepdims=True)
            e = jnp.exp(s - top)
            prob = e * (1.0 / jnp.sum(e, axis=-1, keepdims=True))
            prob_out[head, at, :] = prob
            mixed.append(dot(prob.astype(LOW), v_out[:, lanes], 1, 0))
        masks = head_masks(WIDE)
        ctx_out[at, :] = (mixed[0] * masks[0] + mixed[1] * masks[1]).astype(LOW)

    each(rows, CHUNK, score)


def any_space():
    return pl.BlockSpec(memory_space=pl.ANY)


def whole(shape):
    return pl.BlockSpec(shape, lambda *_: (0,) * len(shape))


def attend(scal, tokens, vec, sines, cosines, encoded, mine, other):
    rows, width = tokens.shape
    cols = mine.shape[2]
    pairs = cols // 128
    low = jax.ShapeDtypeStruct((rows, cols), LOW)
    return pl.pallas_call(
        attend_kernel,
        out_shape=(low, low, low, low, jax.ShapeDtypeStruct((2 * pairs, rows, rows), WIDE)),
        grid_spec=pltpu.PrefetchScalarGridSpec(
            num_scalar_prefetch=1,
            grid=(pairs,),
            in_specs=[
                whole((rows, width)),
                whole((vec.shape[0], cols)),
                whole((rows, width // 2)),
                whole((rows, width // 2)),
                whole((rows, width)),
                any_space(),
                any_space(),
            ],
            out_specs=[whole((rows, cols))] * 3
            + [
                pl.BlockSpec((rows, 128), lambda p, _: (0, p)),
                pl.BlockSpec((2, rows, rows), lambda p, _: (p, 0, 0)),
            ],
            scratch_shapes=[
                pltpu.VMEM((4, width, cols), LOW),
                pltpu.VMEM((rows, width + 128), LOW),
                pltpu.SemaphoreType.DMA,
            ],
        ),
        compiler_params=pltpu.CompilerParams(
            dimension_semantics=("arbitrary",), vmem_limit_bytes=VMEM_BYTES
        ),
        cost_estimate=pl.CostEstimate(
            flops=pairs * 2 * rows * width * 3072, transcendentals=0, bytes_accessed=24 * 1024 * 1024
        ),
        name="attend",
    )(scal, tokens, vec, sines, cosines, encoded, mine, other)


CDF_POLY = (
    -0.020695917308330536,
    0.09534552693367004,
    -0.15029412508010864,
    0.07120334357023239,
    -0.011180647648870945,
    0.05997580662369728,
    0.08762594312429428,
    0.11413583159446716,
    0.12694157660007477,
    0.12694266438484192,
)
CDF_SLOPE = 0.45 / math.sqrt(2.0)


def gelu_pair(x):
    size = jnp.abs(x)
    t = 1.0 / (1.0 + CDF_SLOPE * size)
    bell = jnp.exp(-0.5 * x * x)
    poly = CDF_POLY[0]
    for value in CDF_POLY[1:]:
        poly = poly * t + value
    tail = poly * t * bell
    cdf = jnp.where(x < 0.0, tail, 1.0 - tail)
    return x * cdf, cdf + x * bell * (1.0 / math.sqrt(2.0 * math.pi))


def moments(z):
    center = z - jnp.mean(z, axis=-1, keepdims=True)
    r = lax.rsqrt(jnp.mean(center * center, axis=-1, keepdims=True) + EPS_NORM)
    return center * r, r


def norm_back(grad, xh, r, gain):
    dxh = grad * gain
    return r * (
        dxh - jnp.mean(dxh, axis=-1, keepdims=True) - xh * jnp.mean(dxh * xh, axis=-1, keepdims=True)
    )


def total(values):
    return jnp.sum(values, axis=0, keepdims=True)


def two_copies(scal, mine, other, out_mat, up_mat, sem, place):
    core = scal[CORE_AT]
    copies = []
    for source, base, half in ((mine, 0, core), (other, 16, 1 - core)):
        at = block_at(scal[base + place])
        copies.append(
            pltpu.make_async_copy(
                source.at[place, pl.ds(0, 48)],
                out_mat.at[at, pl.ds(pl.multiple_of(half * 384, 128), 384)],
                sem,
            )
        )
        for part in range(4):
            copies.append(
                pltpu.make_async_copy(
                    source.at[place, pl.ds(48 + 48 * part, 48)],
                    up_mat.at[2 * half + part // 2, at, pl.ds(384 * (part % 2), 384)],
                    sem,
                )
            )
    return copies


def three_copies(scal, mine, other, down_mat, sem, place):
    core = scal[CORE_AT]
    return [
        pltpu.make_async_copy(
            source.at[place],
            down_mat.at[pl.ds(pl.multiple_of(scal[base + place] * 192 + half * 96, 32), 96)],
            sem,
        )
        for source, base, half in ((mine, 0, core), (other, 16, 1 - core))
    ]


def route(scal, half, block, source, keep, send, sem, act):
    core = scal[CORE_AT]

    @pl.when(core == half)
    def _():
        act(pltpu.make_async_copy(source, keep(scal[PLACE_AT + block]), sem))

    @pl.when(core != half)
    def _():
        act(pltpu.make_async_copy(source, send(scal[PLACE_AT + 16 + block]), sem))


def starting(copy):
    copy.start()


def waiting(copy):
    copy.wait()


def feed_kernel(groups, *refs):
    scal, tokens, cot, vec = refs[:4]
    ctx_parts = refs[4 : 4 + groups]
    two_mine, two_other, three_mine, three_other = refs[4 + groups : 8 + groups]
    (
        page_out,
        dh1_out,
        dctx_out,
        vec_out,
        two_keep,
        two_send,
        three_keep,
        three_send,
        out_mat,
        up_mat,
        down_mat,
        ctx,
        norm_low,
        xh1,
        r1,
        act,
        slope,
        held,
        df,
        dpre,
        dattn,
        g_out,
        g_up,
        g_down,
        sem_in,
        sem_up,
        sem_down,
        sem_out,
    ) = refs[8 + groups :]
    step = pl.program_id(0)
    rows, width = tokens.shape
    length = scal[LENGTH_AT]

    @pl.when(step == 0)
    def _():
        run_copies(
            lambda place: two_copies(scal, two_mine, two_other, out_mat, up_mat, sem_in, place)
            + three_copies(scal, three_mine, three_other, down_mat, sem_in, place),
            16,
        )
        vec_out[...] = jnp.zeros_like(vec_out)
        cols = width // groups
        for g in range(groups):
            ctx[:, cols * g : cols * (g + 1)] = ctx_parts[g][...]

        def first(at):
            attn = dot(ctx[at, :], out_mat[...], 1, 0) + vec[6:7, :]
            hat, r = moments(tokens[at, :].astype(WIDE) + attn)
            normed = hat * vec[0:1, :] + vec[1:2, :]
            xh1[at, :] = hat
            r1[at, :] = jnp.broadcast_to(r, (r.shape[0], 128))
            norm_low[at, :] = normed.astype(LOW)
            held[at, :] = normed + vec[7:8, :]

        each(rows, CHUNK, first)

    @pl.when(step < 4)
    def _():
        def forward(at):
            pre = dot(norm_low[at, :], up_mat[step], 1, 0) + vec[pl.ds(8 + step, 1), :]
            value, grad = gelu_pair(pre)
            low = value.astype(LOW)
            act[step, at, :] = low
            slope[step, at, :] = grad
            held[at, :] += dot(low, down_mat[pl.ds(pl.multiple_of(step * width, width), width), :], 1, 0)

        each(rows, CHUNK, forward)

    @pl.when(step == 3)
    def _():
        def second(at):
            hat, r = moments(held[at, :])
            place = lax.broadcasted_iota(jnp.int32, (SLAB, 1), 0) + at.start
            live = jnp.where(place < length, 1.0, 0.0)
            page_out[at, :] = ((hat * vec[2:3, :] + vec[3:4, :]) * live).astype(LOW)
            dy = cot[at, :].astype(WIDE) * live
            vec_out[2:3, :] += total(dy * hat)
            vec_out[3:4, :] += total(dy)
            dh2 = norm_back(dy, hat, r, vec[2:3, :])
            low = dh2.astype(LOW)
            df[at, :] = low
            vec_out[7:8, :] += total(low.astype(WIDE))
            held[at, :] = dh2

        each(rows, SLAB, second)

    def up_route(slot, unit, act_on):
        def body(block, carry):
            for part in range(2):
                local = 2 * lax.rem(unit, 2) + part
                at = pl.ds(pl.multiple_of(48 + 48 * local, 16), 48)
                route(
                    scal,
                    unit // 2,
                    block,
                    g_up.at[slot, block_at(block), pl.ds(384 * part, 384)],
                    lambda place: two_keep.at[place, at],
                    lambda place: two_send.at[place, at],
                    sem_up.at[slot],
                    act_on,
                )
            return carry

        lax.fori_loop(0, 16, body, 0)

    def down_route(slot, unit, act_on):
        for part in range(8):
            route(
                scal,
                part % 2,
                4 * unit + part // 2,
                g_down.at[slot, pl.ds(96 * part, 96)],
                lambda place: three_keep.at[place],
                lambda place: three_send.at[place],
                sem_down.at[slot],
                act_on,
            )

    def out_route(act_on):
        def body(block, carry):
            for half in range(2):
                route(
                    scal,
                    half,
                    block,
                    g_out.at[block_at(block), pl.ds(384 * half, 384)],
                    lambda place: two_keep.at[place, pl.ds(0, 48)],
                    lambda place: two_send.at[place, pl.ds(0, 48)],
                    sem_out,
                    act_on,
                )
            return carry

        lax.fori_loop(0, 16, body, 0)

    @pl.when(step >= 4)
    def _():
        unit = step - 4
        slot = lax.rem(unit, 2)
        down_at = pl.ds(pl.multiple_of(unit * width, width), width)

        @pl.when(unit >= 2)
        def _():
            up_route(slot, unit - 2, waiting)
            down_route(slot, unit - 2, waiting)

        def backward(at):
            grad = dot(df[at, :], down_mat[down_at, :], 1, 1) * slope[unit, at, :]
            low = grad.astype(LOW)
            dpre[at, :] = low
            vec_out[pl.ds(8 + unit, 1), :] += total(low.astype(WIDE))
            held[at, :] += dot(low, up_mat[unit], 1, 1)

        each(rows, CHUNK, backward)

        def weights(at):
            g_down[slot, at, :] = dot(act[unit, :, at], df[...], 0, 0).astype(LOW)
            g_up[slot, at, :] = dot(norm_low[:, at], dpre[...], 0, 0).astype(LOW)

        each(width, CHUNK, weights)
        down_route(slot, unit, starting)
        up_route(slot, unit, starting)

    @pl.when(step == 7)
    def _():
        def last(at):
            grad, hat = held[at, :], xh1[at, :]
            vec_out[0:1, :] += total(grad * hat)
            vec_out[1:2, :] += total(grad)
            dh1 = norm_back(grad, hat, r1[at, :1], vec[0:1, :])
            dh1_out[at, :] = dh1
            low = dh1.astype(LOW)
            dattn[at, :] = low
            vec_out[6:7, :] += total(low.astype(WIDE))

        each(rows, SLAB, last)

        def context(at):
            dctx_out[at, :] = dot(dattn[at, :], out_mat[...], 1, 1).astype(LOW)

        each(rows, CHUNK, context)

        def weights(at):
            g_out[at, :] = dot(ctx[:, at], dattn[...], 0, 0).astype(LOW)

        each(width, CHUNK, weights)
        out_route(starting)
        for unit in (2, 3):
            up_route(unit % 2, unit, waiting)
            down_route(unit % 2, unit, waiting)
        out_route(waiting)


def feed(scal, tokens, cot, vec, ctx_parts, two, three):
    rows, width = tokens.shape
    groups = len(ctx_parts)
    return pl.pallas_call(
        partial(feed_kernel, groups),
        out_shape=(
            jax.ShapeDtypeStruct((rows, width), LOW),
            jax.ShapeDtypeStruct((rows, width), WIDE),
            jax.ShapeDtypeStruct((rows, width), LOW),
            jax.ShapeDtypeStruct((16, width), WIDE),
            jax.ShapeDtypeStruct((16, 240, 384), LOW),
            jax.ShapeDtypeStruct((16, 240, 384), LOW),
            jax.ShapeDtypeStruct((16, 96, width), LOW),
            jax.ShapeDtypeStruct((16, 96, width), LOW),
        ),
        grid_spec=pltpu.PrefetchScalarGridSpec(
            num_scalar_prefetch=1,
            grid=(8,),
            in_specs=[whole((rows, width)), whole((rows, width)), whole((16, width))]
            + [whole((rows, width // groups))] * groups
            + [any_space()] * 4,
            out_specs=[whole((rows, width))] * 3 + [whole((16, width))] + [any_space()] * 4,
            scratch_shapes=[
                pltpu.VMEM((width, width), LOW),
                pltpu.VMEM((4, width, width), LOW),
                pltpu.VMEM((4 * width, width), LOW),
                pltpu.VMEM((rows, width), LOW),
                pltpu.VMEM((rows, width), LOW),
                pltpu.VMEM((rows, width), WIDE),
                pltpu.VMEM((rows, 128), WIDE),
                pltpu.VMEM((4, rows, width), LOW),
                pltpu.VMEM((4, rows, width), WIDE),
                pltpu.VMEM((rows, width), WIDE),
                pltpu.VMEM((rows, width), LOW),
                pltpu.VMEM((rows, width), LOW),
                pltpu.VMEM((rows, width), LOW),
                pltpu.VMEM((width, width), LOW),
                pltpu.VMEM((2, width, width), LOW),
                pltpu.VMEM((2, width, width), LOW),
                pltpu.SemaphoreType.DMA,
                pltpu.SemaphoreType.DMA((2,)),
                pltpu.SemaphoreType.DMA((2,)),
                pltpu.SemaphoreType.DMA,
            ],
        ),
        compiler_params=pltpu.CompilerParams(
            dimension_semantics=("arbitrary",), vmem_limit_bytes=VMEM_BYTES
        ),
        cost_estimate=pl.CostEstimate(
            flops=2 * rows * width * width * 27, transcendentals=0, bytes_accessed=32 * 1024 * 1024
        ),
        name="feed",
    )(scal, tokens, cot, vec, *ctx_parts, *two, *three)


def unattend_kernel(
    scal,
    tokens,
    sines,
    cosines,
    encoded,
    q_in,
    k_in,
    v_in,
    dctx_in,
    prob,
    mine,
    other,
    dq_out,
    dk_out,
    dv_out,
    vec_out,
    keep,
    send,
    mats,
    right,
    prob_low,
    ds_low,
    du_low,
    q_heads,
    d_heads,
    dq_part,
    grads,
    sem,
    sem_out,
):
    pair = pl.program_id(0)
    rows, width = tokens.shape
    half = width // 2
    scale = HEAD_DIM ** (-0.5)

    @pl.when(pair == 0)
    def _():
        run_copies(partial(attn_copies, scal, mine, other, mats, sem), 16)
        right[:, :width] = encoded[...]

    lanes = pl.ds(pl.multiple_of(pair * 128, 128), 128)
    right[:, width:] = k_in[...]
    rel = mats[3, :, lanes]
    low_masks, wide_masks = head_masks(LOW), head_masks(WIDE)

    def score(at):
        sin, cos = sines[at, :], cosines[at, :]
        dq = None
        for head in range(2):
            spot = pl.ds(pl.multiple_of(head * rows + at.start, at.size), at.size)
            dctx = dctx_in[at, :] * low_masks[head]
            d_heads[spot, :] = dctx
            q_heads[spot, :] = q_in[at, :] * low_masks[head]
            p = prob[head, at, :]
            prob_low[spot, :] = p.astype(LOW)
            dp = dot(dctx, v_in[...], 1, 1)
            ds = (p * (dp - jnp.sum(p * dp, axis=-1, keepdims=True))).astype(LOW)
            ds_low[spot, :] = ds
            dl = dot(ds, right[...], 1, 0) * scale
            ls, lc = dl[:, :half], dl[:, half:width]
            du = jnp.concatenate(
                [(lc * sin - ls * cos).astype(LOW), (ls * sin + lc * cos).astype(LOW)], axis=1
            )
            du_low[spot, :] = du
            part = (dl[:, width:] + dot(du, rel, 1, 0)) * wide_masks[head]
            dq = part if dq is None else dq + part
        dq_out[at, lanes] = dq.astype(LOW)

    each(rows, CHUNK, score)
    dv_out[:, lanes] = dot(prob_low[...], d_heads[...], 0, 0).astype(LOW)
    dk_out[:, lanes] = (dot(ds_low[...], q_heads[...], 0, 0) * scale).astype(LOW)
    grads[3, :, lanes] = dot(du_low[...], q_heads[...], 0, 0).astype(LOW)

    @pl.when(pair == pl.num_programs(0) - 1)
    def _():
        def weights(at):
            x = tokens[:, at]
            grads[0, at, :] = dot(x, dq_out[...], 0, 0).astype(LOW)
            grads[1, at, :] = dot(x, dk_out[...], 0, 0).astype(LOW)
            grads[2, at, :] = dot(x, dv_out[...], 0, 0).astype(LOW)

        each(width, CHUNK, weights)

        def move(act_on):
            def body(block, carry):
                for slot in range(4):
                    row = turned(block) if slot == 3 else block
                    at = pl.ds(48 * (slot % 2), 48)
                    route(
                        scal,
                        slot // 2,
                        block,
                        grads.at[slot, block_at(row)],
                        lambda place: keep.at[place, at],
                        lambda place: send.at[place, at],
                        sem_out,
                        act_on,
                    )
                return carry

            lax.fori_loop(0, 16, body, 0)

        move(starting)
        vec_out[...] = jnp.zeros_like(vec_out)
        vec_out[0:1, :] = total(dq_out[...].astype(WIDE))
        vec_out[1:2, :] = total(dv_out[...].astype(WIDE))
        move(waiting)


def unattend(scal, tokens, sines, cosines, encoded, q, k, v, dctx, group, prob, mine, other):
    rows, width = tokens.shape
    cols = mine.shape[2]
    pairs = cols // 128
    low = jax.ShapeDtypeStruct((rows, cols), LOW)
    lane_block = pl.BlockSpec((rows, 128), lambda p, _: (0, p))
    return pl.pallas_call(
        unattend_kernel,
        out_shape=(low, low, low, jax.ShapeDtypeStruct((8, cols), WIDE))
        + (jax.ShapeDtypeStruct((16, 96, cols), LOW),) * 2,
        grid_spec=pltpu.PrefetchScalarGridSpec(
            num_scalar_prefetch=1,
            grid=(pairs,),
            in_specs=[
                whole((rows, width)),
                whole((rows, half_of(width))),
                whole((rows, half_of(width))),
                whole((rows, width)),
                lane_block,
                lane_block,
                lane_block,
                pl.BlockSpec((rows, 128), lambda p, _: (0, group * pairs + p)),
                pl.BlockSpec((2, rows, rows), lambda p, _: (p, 0, 0)),
                any_space(),
                any_space(),
            ],
            out_specs=[whole((rows, cols))] * 3 + [whole((8, cols))] + [any_space()] * 2,
            scratch_shapes=[
                pltpu.VMEM((4, width, cols), LOW),
                pltpu.VMEM((rows, width + 128), LOW),
                pltpu.VMEM((2 * rows, rows), LOW),
                pltpu.VMEM((2 * rows, rows), LOW),
                pltpu.VMEM((2 * rows, width), LOW),
                pltpu.VMEM((2 * rows, 128), LOW),
                pltpu.VMEM((2 * rows, 128), LOW),
                pltpu.VMEM((8, 128), WIDE),
                pltpu.VMEM((4, width, cols), LOW),
                pltpu.SemaphoreType.DMA,
                pltpu.SemaphoreType.DMA,
            ],
        ),
        compiler_params=pltpu.CompilerParams(
            dimension_semantics=("arbitrary",), vmem_limit_bytes=VMEM_BYTES
        ),
        cost_estimate=pl.CostEstimate(
            flops=pairs * 2 * rows * width * 5000, transcendentals=0, bytes_accessed=24 * 1024 * 1024
        ),
        name="unattend",
    )(scal, tokens, sines, cosines, encoded, q, k, v, dctx, prob, mine, other)


def half_of(width):
    return width // 2


def input_grad_kernel(groups, *refs):
    scal, dh1 = refs[:2]
    parts = refs[2 : 2 + 3 * groups]
    pieces = refs[2 + 3 * groups : 2 + 5 * groups]
    out, mats, sem = refs[2 + 5 * groups :]

    def copies(place):
        made = []
        for g in range(groups):
            made += attn_copies(scal, pieces[2 * g], pieces[2 * g + 1], mats.at[g], sem, place)
        return made

    run_copies(copies, 16)

    def rows_of(at):
        grad = dh1[at, :]
        for g in range(groups):
            for slot in range(3):
                grad = grad + dot(parts[3 * g + slot][at, :], mats[g, slot], 1, 1)
        out[at, :] = grad

    each(dh1.shape[0], CHUNK, rows_of)


def input_grad(scal, dh1, parts, pieces):
    rows, width = dh1.shape
    groups = len(pieces) // 2
    cols = width // groups
    return pl.pallas_call(
        partial(input_grad_kernel, groups),
        out_shape=jax.ShapeDtypeStruct((rows, width), WIDE),
        grid_spec=pltpu.PrefetchScalarGridSpec(
            num_scalar_prefetch=1,
            grid=(1,),
            in_specs=[whole((rows, width))]
            + [whole((rows, cols))] * (3 * groups)
            + [any_space()] * (2 * groups),
            out_specs=whole((rows, width)),
            scratch_shapes=[pltpu.VMEM((groups, 4, width, cols), LOW), pltpu.SemaphoreType.DMA],
        ),
        compiler_params=pltpu.CompilerParams(
            dimension_semantics=("arbitrary",), vmem_limit_bytes=VMEM_BYTES
        ),
        cost_estimate=pl.CostEstimate(
            flops=2 * rows * width * width * 3, transcendentals=0, bytes_accessed=10 * 1024 * 1024
        ),
        name="input_grad",
    )(scal, dh1, *parts, *pieces)


GROUPS = 1


def local(
    tokens,
    boxes,
    lengths,
    cotangent,
    attn_weight,
    up_weight,
    down_weight,
    vectors,
    attn_first,
    up_first,
    down_first,
    vector_first,
    attn_second,
    up_second,
    down_second,
    vector_second,
):
    chip, core = lax.axis_index("fsdp"), lax.axis_index("rep")
    width = tokens.shape[2]
    cols = width // GROUPS
    masks, places = jnp.array(MASKS, jnp.int32), jnp.array(PLACES, jnp.int32)
    lane = jnp.arange(16, dtype=jnp.int32)
    scal = jnp.concatenate(
        [
            masks[core] ^ chip,
            masks[1 - core] ^ chip,
            jnp.stack([core, lengths[0]]),
            places[core][lane ^ chip],
            places[1 - core][lane ^ chip],
        ]
    ).astype(jnp.int32)

    first = core == 0
    top = jnp.where(first, attn_weight[0], attn_weight[2]).astype(LOW)
    bottom = jnp.where(first, attn_weight[1], attn_weight[4]).astype(LOW)
    own_one = jnp.concatenate([top, bottom], axis=0)
    one = [
        gather_blocks(own_one[:, cols * g : cols * (g + 1)]) for g in range(GROUPS)
    ]
    vec_blocks = gather_mine(vectors.astype(LOW))
    vec = jnp.take(vec_blocks, places[core][lane ^ chip], axis=0)
    vec = vec.transpose(1, 0, 2).reshape(vectors.shape[0], width).astype(WIDE)
    vec = jnp.pad(vec, ((0, 16 - vec.shape[0]), (0, 0)))
    parts = [attn_weight[3]] + [up_weight[:, 768 * i : 768 * (i + 1)] for i in range(4)]
    halves = [
        [parts[0][:, 384 * h : 384 * (h + 1)]]
        + [up_weight[:, 1536 * h + 384 * i : 1536 * h + 384 * (i + 1)] for i in range(4)]
        for h in range(2)
    ]
    own_two = jnp.concatenate(
        [jnp.where(first, a, b).astype(LOW) for a, b in zip(*halves, strict=True)], axis=0
    )
    two = gather_blocks(own_two)
    own_three = jnp.where(first, down_weight[:96], down_weight[96:]).astype(LOW)
    three = gather_blocks(own_three)

    quarter = width // 4
    frequency = jnp.exp(jnp.arange(quarter).astype(WIDE) * (-math.log(10000.0) / quarter))
    place = boxes[0].astype(WIDE)
    angles = jnp.concatenate([place[0][:, None] * frequency, place[1][:, None] * frequency], axis=1)
    sines, cosines = jnp.sin(angles), jnp.cos(angles)
    encoded = jnp.concatenate([sines, cosines], axis=1).astype(LOW)

    page = tokens[0]
    kept = []
    for g in range(GROUPS):
        vec_group = vec[:, cols * g : cols * (g + 1)]
        kept.append(attend(scal, page, vec_group, sines, cosines, encoded, *one[g]))
    page_out, dh1, dctx, vec_one, two_keep, two_send, three_keep, three_send = feed(
        scal, page, cotangent[0], vec, [k[3] for k in kept], two, three
    )
    three_sum = scatter_blocks(three_keep, three_send)
    two_sum = scatter_blocks(two_keep, two_send)
    back = [
        unattend(
            scal,
            page,
            sines,
            cosines,
            encoded,
            *kept[g][:3],
            dctx,
            g,
            kept[g][4],
            *one[g],
        )
        for g in range(GROUPS)
    ]
    one_sum = [scatter_blocks(b[4], b[5]) for b in back]
    vec_two = jnp.concatenate([b[3][:2] for b in back], axis=1)
    vec_grad = jnp.concatenate([vec_one[:4], vec_two, vec_one[6:12]], axis=0)
    vec_blocks = vec_grad.reshape(12, 16, 48).transpose(1, 0, 2)
    vec_blocks = jnp.take(vec_blocks, masks[core] ^ chip, axis=0)
    vec_mine = scatter_mine(vec_blocks)
    vec_other = swap_cores(vec_mine)
    vec_sum = vec_mine + vec_other
    token_grad = input_grad(
        scal,
        dh1,
        [part for b in back for part in b[:3]],
        [piece for pieces in one for piece in pieces],
    )
    halves_one = [jnp.concatenate([s[h] for s in one_sum], axis=1) for h in range(2)]
    reduced = (
        jnp.stack(
            [
                halves_one[0][:48],
                halves_one[0][48:],
                halves_one[1][:48],
                jnp.concatenate([two_sum[0][:48], two_sum[1][:48]], axis=1),
                halves_one[1][48:],
            ]
        ),
        jnp.concatenate(
            [two_sum[h][48 + 48 * i : 96 + 48 * i] for h in range(2) for i in range(4)], axis=1
        ),
        jnp.concatenate(three_sum, axis=0),
        vec_sum,
    )
    layer_out, token_grad = page_out[None], token_grad[None]
    attn_rates = jnp.array(ATTN_RATES, jnp.float32)[:, None, None]
    attn_new, attn_first_new, attn_second_new = adam_update(
        attn_weight, attn_first, attn_second, reduced[0], attn_rates, WEIGHT_DECAY
    )
    up_new, up_first_new, up_second_new = adam_update(
        up_weight, up_first, up_second, reduced[1], UP_RATE, WEIGHT_DECAY
    )
    down_new, down_first_new, down_second_new = adam_update(
        down_weight, down_first, down_second, reduced[2], DOWN_RATE, WEIGHT_DECAY
    )
    vectors_new, vector_first_new, vector_second_new = adam_update(
        vectors, vector_first, vector_second, reduced[3], VECTOR_RATE, 0.0
    )
    return (
        layer_out,
        token_grad,
        attn_new,
        up_new,
        down_new,
        vectors_new,
        attn_first_new,
        up_first_new,
        down_first_new,
        vector_first_new,
        attn_second_new,
        up_second_new,
        down_second_new,
        vector_second_new,
        attn_new.astype(jnp.bfloat16),
        up_new.astype(jnp.bfloat16),
        down_new.astype(jnp.bfloat16),
        vectors_new.astype(jnp.bfloat16),
    )


def local_general(
    tokens,
    boxes,
    lengths,
    cotangent,
    attn_weight,
    up_weight,
    down_weight,
    vectors,
    attn_first,
    up_first,
    down_first,
    vector_first,
    attn_second,
    up_second,
    down_second,
    vector_second,
):
    lowered = (
        attn_weight.astype(jnp.bfloat16),
        up_weight.astype(jnp.bfloat16),
        down_weight.astype(jnp.bfloat16),
        vectors.astype(jnp.bfloat16),
    )
    gathered = (
        lax.all_gather(lowered[0], "fsdp", axis=1, tiled=True),
        lax.all_gather(lowered[1], "fsdp", axis=0, tiled=True),
        lax.all_gather(lowered[2], "fsdp", axis=0, tiled=True),
        lax.all_gather(lowered[3], "fsdp", axis=1, tiled=True),
    )

    def forward_step(carry, page):
        token_row_block, box_rows, page_length = page
        return (carry, forward_page(gathered, token_row_block, box_rows, page_length))

    _, (layer_out, saved_all) = lax.scan(forward_step, None, (tokens, boxes, lengths))
    backward_weights = (
        lax.all_gather(lowered[0], "fsdp", axis=1, tiled=True),
        lax.all_gather(lowered[1], "fsdp", axis=0, tiled=True),
        lax.all_gather(lowered[2], "fsdp", axis=0, tiled=True),
        lax.all_gather(lowered[3], "fsdp", axis=1, tiled=True),
    )
    model_width = gathered[0].shape[2]
    ffn_width = gathered[1].shape[1]
    zero_grads = (
        jnp.zeros((5, model_width, model_width), jnp.float32),
        jnp.zeros((model_width, ffn_width), jnp.float32),
        jnp.zeros((ffn_width, model_width), jnp.float32),
        jnp.zeros(gathered[3].shape, jnp.float32),
    )

    def backward_step(totals, page):
        token_row_block, box_rows, page_length, upstream, saved_state = page
        token_grad, grads = backward_page(
            backward_weights, token_row_block, box_rows, page_length, upstream, saved_state
        )
        return (jax.tree.map(jnp.add, totals, grads), token_grad)

    totals, token_grad = lax.scan(
        backward_step, zero_grads, (tokens, boxes, lengths, cotangent, saved_all)
    )
    shards = (
        lax.psum_scatter(totals[0], "fsdp", scatter_dimension=1, tiled=True),
        lax.psum_scatter(totals[1], "fsdp", scatter_dimension=0, tiled=True),
        lax.psum_scatter(totals[2], "fsdp", scatter_dimension=0, tiled=True),
        lax.psum_scatter(totals[3], "fsdp", scatter_dimension=1, tiled=True),
    )
    reduced = (
        lax.psum(shards[0].astype(jnp.bfloat16), "rep").astype(jnp.float32),
        lax.psum(shards[1].astype(jnp.bfloat16), "rep").astype(jnp.float32),
        lax.psum(shards[2].astype(jnp.bfloat16), "rep").astype(jnp.float32),
        lax.psum(shards[3].astype(jnp.bfloat16), "rep").astype(jnp.float32),
    )
    attn_rates = jnp.array(ATTN_RATES, jnp.float32)[:, None, None]
    attn_new, attn_first_new, attn_second_new = adam_update(
        attn_weight, attn_first, attn_second, reduced[0], attn_rates, WEIGHT_DECAY
    )
    up_new, up_first_new, up_second_new = adam_update(
        up_weight, up_first, up_second, reduced[1], UP_RATE, WEIGHT_DECAY
    )
    down_new, down_first_new, down_second_new = adam_update(
        down_weight, down_first, down_second, reduced[2], DOWN_RATE, WEIGHT_DECAY
    )
    vectors_new, vector_first_new, vector_second_new = adam_update(
        vectors, vector_first, vector_second, reduced[3], VECTOR_RATE, 0.0
    )
    return (
        layer_out,
        token_grad,
        attn_new,
        up_new,
        down_new,
        vectors_new,
        attn_first_new,
        up_first_new,
        down_first_new,
        vector_first_new,
        attn_second_new,
        up_second_new,
        down_second_new,
        vector_second_new,
        attn_new.astype(jnp.bfloat16),
        up_new.astype(jnp.bfloat16),
        down_new.astype(jnp.bfloat16),
        vectors_new.astype(jnp.bfloat16),
    )


def solution(mesh):
    blocked = mesh.shape["fsdp"] == 16 and mesh.shape["rep"] == 2
    return jax.shard_map(
        local if blocked else local_general,
        mesh=mesh,
        in_specs=(
            P(("fsdp", "rep"), None, None),
            P(("fsdp", "rep"), None, None),
            P(("fsdp", "rep")),
            P(("fsdp", "rep"), None, None),
            P(None, "fsdp", None),
            P("fsdp", None),
            P("fsdp", None),
            P(None, "fsdp"),
            P(None, "fsdp", None),
            P("fsdp", None),
            P("fsdp", None),
            P(None, "fsdp"),
            P(None, "fsdp", None),
            P("fsdp", None),
            P("fsdp", None),
            P(None, "fsdp"),
        ),
        out_specs=(
            P(("fsdp", "rep"), None, None),
            P(("fsdp", "rep"), None, None),
            P(None, "fsdp", None),
            P("fsdp", None),
            P("fsdp", None),
            P(None, "fsdp"),
            P(None, "fsdp", None),
            P("fsdp", None),
            P("fsdp", None),
            P(None, "fsdp"),
            P(None, "fsdp", None),
            P("fsdp", None),
            P("fsdp", None),
            P(None, "fsdp"),
            P(None, "fsdp", None),
            P("fsdp", None),
            P("fsdp", None),
            P(None, "fsdp"),
        ),
        check_vma=False,
    )
```

```python
from functools import partial
import math

import jax
import jax.numpy as jnp
from jax import lax
from jax.experimental import pallas as pl
from jax.experimental.pallas import tpu as pltpu
from jax.sharding import PartitionSpec as P

HEADS = 12
HEAD_DIM = 64
STEP = 7


EPS_NORM = 1e-12
EPS_ADAM = 1e-08
DECAY = 0.5
MASK_FILL = -1e30
WEIGHT_DECAY = 0.01
ATTN_RATES = (0.04, 0.04, 0.04, 0.2, 0.04)
UP_RATE = 0.04
DOWN_RATE = 0.02
VECTOR_RATE = 0.3


def contract(left_op, right_op, left_dim, right_dim):
    return lax.dot_general(
        left_op,
        right_op,
        (((left_dim,), (right_dim,)), ((), ())),
        preferred_element_type=jnp.float32,
    )


def layer_norm(hidden, gain_row, shift_row):
    center = hidden - jnp.mean(hidden, axis=-1, keepdims=True)
    spread = jnp.mean(center * center, axis=-1, keepdims=True)
    return center * lax.rsqrt(spread + EPS_NORM) * gain_row + shift_row


def box_tables(box_rows, model_width):
    quarter = model_width // 4
    frequency = jnp.exp(jnp.arange(quarter).astype(jnp.float32) * (-math.log(10000.0) / quarter))
    angles = box_rows.astype(jnp.float32)[:, :, None] * frequency
    return (jnp.sin(angles), jnp.cos(angles))


def encode(sine_rows, cosine_rows):
    return jnp.concatenate([sine_rows[0], cosine_rows[0], sine_rows[1], cosine_rows[1]], axis=-1)


def rotate(pos_table, sine_rows, cosine_rows):
    quarter = sine_rows.shape[-1]
    pieces = []
    for coord in range(2):
        sine_part = pos_table[..., 2 * coord * quarter : (2 * coord + 1) * quarter]
        cosine_part = pos_table[..., (2 * coord + 1) * quarter : (2 * coord + 2) * quarter]
        pieces.append(cosine_part * sine_rows[coord] - sine_part * cosine_rows[coord])
        pieces.append(sine_part * sine_rows[coord] + cosine_part * cosine_rows[coord])
    return jnp.concatenate(pieces, axis=-1)


def scores(query_rows, key_rows, left_rows, encoded, page_live):
    text_part = jnp.einsum("ihd,jhd->hij", query_rows, key_rows, preferred_element_type=jnp.float32)
    place_part = jnp.einsum("hie,je->hij", left_rows, encoded, preferred_element_type=jnp.float32)
    score_rows = (text_part + place_part) * HEAD_DIM ** (-0.5)
    return jnp.where(page_live[None, None, :], score_rows, MASK_FILL)


def forward_page(weights, token_row_block, box_rows, page_length):
    attention_matrices, up_mat, down_mat, vector_rows = weights
    row_count, model_width = token_row_block.shape
    vector_f32 = vector_rows.astype(jnp.float32)
    page_live = jnp.arange(row_count) < page_length
    projected_rows = jnp.einsum(
        "tb,mby->mty", token_row_block, attention_matrices[:3], preferred_element_type=jnp.float32
    )
    query_rows = (
        (projected_rows[0] + vector_f32[4]).astype(jnp.bfloat16).reshape(row_count, HEADS, HEAD_DIM)
    )
    key_rows = projected_rows[1].astype(jnp.bfloat16).reshape(row_count, HEADS, HEAD_DIM)
    value_rows = (
        (projected_rows[2] + vector_f32[5]).astype(jnp.bfloat16).reshape(row_count, HEADS, HEAD_DIM)
    )
    sine_rows, cosine_rows = box_tables(box_rows, model_width)
    encoded = encode(sine_rows, cosine_rows).astype(jnp.bfloat16)
    rel_heads = attention_matrices[4].reshape(model_width, HEADS, HEAD_DIM)
    pos_table = jnp.einsum(
        "ihd,ehd->hie", query_rows, rel_heads, preferred_element_type=jnp.float32
    )
    left_rows = rotate(pos_table, sine_rows, cosine_rows).astype(jnp.bfloat16)
    score_rows = scores(query_rows, key_rows, left_rows, encoded, page_live)
    row_top = jnp.max(score_rows, axis=-1, keepdims=True)
    exponent = jnp.exp(score_rows - row_top)
    row_total = jnp.sum(exponent, axis=-1, keepdims=True)
    prob_low = (exponent / row_total).astype(jnp.bfloat16)
    logsum = row_top + jnp.log(row_total)
    mixed_rows = jnp.einsum(
        "hij,jhd->ihd", prob_low, value_rows, preferred_element_type=jnp.float32
    )
    context = mixed_rows.reshape(row_count, model_width).astype(jnp.bfloat16)
    attn_out = (
        jnp.dot(context, attention_matrices[3], preferred_element_type=jnp.float32) + vector_f32[6]
    )
    first_sum = token_row_block.astype(jnp.float32) + attn_out
    normed = layer_norm(first_sum, vector_f32[0], vector_f32[1])
    pre_act = jnp.dot(
        normed.astype(jnp.bfloat16), up_mat, preferred_element_type=jnp.float32
    ) + vector_f32[8:].reshape(-1)
    act_low = jax.nn.gelu(pre_act, approximate=False).astype(jnp.bfloat16)
    second_sum = normed + (
        jnp.dot(act_low, down_mat, preferred_element_type=jnp.float32) + vector_f32[7]
    )
    page_out = (layer_norm(second_sum, vector_f32[2], vector_f32[3]) * page_live[:, None]).astype(
        jnp.bfloat16
    )
    saved_state = (
        query_rows,
        key_rows,
        value_rows,
        left_rows,
        logsum,
        context,
        first_sum,
        pre_act,
        act_low,
        second_sum,
    )
    return (page_out, saved_state)


def backward_page(weights, token_row_block, box_rows, page_length, upstream, saved_state):
    attention_matrices, up_mat, down_mat, vector_rows = weights
    (
        query_rows,
        key_rows,
        value_rows,
        left_rows,
        logsum,
        context,
        first_sum,
        pre_act,
        act_low,
        second_sum,
    ) = saved_state
    row_count, model_width = token_row_block.shape
    vector_f32 = vector_rows.astype(jnp.float32)
    page_live = jnp.arange(row_count) < page_length
    sine_rows, cosine_rows = box_tables(box_rows, model_width)
    encoded = encode(sine_rows, cosine_rows).astype(jnp.bfloat16)
    out_grad = upstream.astype(jnp.float32) * page_live[:, None]
    _, pull_second = jax.vjp(layer_norm, second_sum, vector_f32[2], vector_f32[3])
    second_grad, gain_two, shift_two = pull_second(out_grad)
    ffn_grad = second_grad.astype(jnp.bfloat16)
    down_grad = contract(act_low, ffn_grad, 0, 0)
    act_grad = contract(ffn_grad, down_mat, 1, 1)
    _, pull_gelu = jax.vjp(partial(jax.nn.gelu, approximate=False), pre_act)
    pre_grad = pull_gelu(act_grad)[0].astype(jnp.bfloat16)
    normed, pull_first = jax.vjp(layer_norm, first_sum, vector_f32[0], vector_f32[1])
    up_grad = contract(normed.astype(jnp.bfloat16), pre_grad, 0, 0)
    normed_grad = contract(pre_grad, up_mat, 1, 1) + second_grad
    first_grad, gain_one, shift_one = pull_first(normed_grad)
    attn_grad = first_grad.astype(jnp.bfloat16)
    out_mat_grad = contract(context, attn_grad, 0, 0)
    context_grad = (
        contract(attn_grad, attention_matrices[3], 1, 1)
        .astype(jnp.bfloat16)
        .reshape(row_count, HEADS, HEAD_DIM)
    )
    score_rows = scores(query_rows, key_rows, left_rows, encoded, page_live)
    prob_rows = jnp.exp(score_rows - logsum)
    value_grad = jnp.einsum(
        "hij,ihd->jhd",
        prob_rows.astype(jnp.bfloat16),
        context_grad,
        preferred_element_type=jnp.float32,
    ).astype(jnp.bfloat16)
    prob_grad = jnp.einsum(
        "ihd,jhd->hij", context_grad, value_rows, preferred_element_type=jnp.float32
    )
    score_grad = (
        prob_rows * (prob_grad - jnp.sum(prob_rows * prob_grad, axis=-1, keepdims=True))
    ).astype(jnp.bfloat16)
    score_scale = HEAD_DIM ** (-0.5)
    left_grad = (
        jnp.einsum("hij,je->hie", score_grad, encoded, preferred_element_type=jnp.float32)
        * score_scale
    )
    table_grad = rotate(left_grad, sine_rows, cosine_rows).astype(jnp.bfloat16)
    rel_heads = attention_matrices[4].reshape(model_width, HEADS, HEAD_DIM)
    rel_grad = jnp.einsum(
        "hie,ihd->ehd", table_grad, query_rows, preferred_element_type=jnp.float32
    ).reshape(model_width, model_width)
    query_grad = (
        jnp.einsum("hij,jhd->ihd", score_grad, key_rows, preferred_element_type=jnp.float32)
        * score_scale
    )
    query_grad = query_grad + jnp.einsum(
        "hie,ehd->ihd", table_grad, rel_heads, preferred_element_type=jnp.float32
    )
    key_grad = (
        jnp.einsum("hij,ihd->jhd", score_grad, query_rows, preferred_element_type=jnp.float32)
        * score_scale
    )
    stacked_layers = jnp.stack(
        [
            query_grad.astype(jnp.bfloat16).reshape(row_count, model_width),
            key_grad.astype(jnp.bfloat16).reshape(row_count, model_width),
            value_grad.reshape(row_count, model_width),
        ]
    )
    projection_gradient = jnp.einsum(
        "cg,yca->yga", token_row_block, stacked_layers, preferred_element_type=jnp.float32
    )
    token_grad = first_grad + jnp.einsum(
        "skl,scl->kc", stacked_layers, attention_matrices[:3], preferred_element_type=jnp.float32
    )
    column_sums = jnp.sum(stacked_layers.astype(jnp.float32), axis=1)
    attn_grads = jnp.concatenate([projection_gradient, out_mat_grad[None], rel_grad[None]], axis=0)
    small_rows = jnp.stack(
        [
            gain_one,
            shift_one,
            gain_two,
            shift_two,
            column_sums[0],
            column_sums[2],
            jnp.sum(attn_grad.astype(jnp.float32), axis=0),
            jnp.sum(ffn_grad.astype(jnp.float32), axis=0),
        ]
    )
    up_bias_rows = jnp.sum(pre_grad.astype(jnp.float32), axis=0).reshape(-1, model_width)
    vector_grad = jnp.concatenate([small_rows, up_bias_rows], axis=0)
    return (token_grad, (attn_grads, up_grad, down_grad, vector_grad))


def adam_update(weight, first, second, grad, rate, decay_weight):
    first_new = DECAY * first + (1.0 - DECAY) * grad
    second_new = DECAY * second + (1.0 - DECAY) * grad * grad
    correction = 1.0 - DECAY**STEP
    direction = first_new / correction / (jnp.sqrt(second_new / correction) + EPS_ADAM)
    return (weight - rate * (direction + decay_weight * weight), first_new, second_new)


AXES = ("fsdp", "rep")
ORDERS = ((8, 4, 2, 1), (8, 4, 1, 2))
LOW = jnp.bfloat16
WIDE = jnp.float32
CHUNK = 256
SLAB = 128
VMEM_BYTES = 58 * 1024 * 1024
ATTN_VMEM_BYTES = 28 * 1024 * 1024
CORE_AT, LENGTH_AT = 64, 65


def mask_table(order):
    masks = [0]
    for bit in order:
        masks = masks + [bit ^ mask for mask in masks]
    return masks


CORE_PAIRS = [(chip * 2 + core, chip * 2 + 1 - core) for chip in range(16) for core in range(2)]


def place_of(mask, order):
    place = 0
    for bit_at, bit in enumerate(order):
        place = place + jnp.where((mask & bit) != 0, 1 << bit_at, 0)
    return place


def block_scalars(chip, core, length):
    rows, lane = [], jnp.arange(16, dtype=jnp.int32)
    blocks = [jnp.array(mask_table(order), jnp.int32) ^ chip for order in ORDERS]
    places = [place_of(lane ^ chip, order) for order in ORDERS]
    for pair in (blocks, places):
        rows.append(jnp.where(core == 0, pair[0], pair[1]))
        rows.append(jnp.where(core == 0, pair[1], pair[0]))
    last = jnp.where(lane == 0, core, jnp.where(lane == 1, length, 0))
    return jnp.stack(rows + [last]).astype(jnp.int32).reshape(-1)


def after(value, *others):
    return lax.optimization_barrier((value, *others))[0]


def swap_cores(block):
    return lax.ppermute(block, AXES, CORE_PAIRS)


def hop(held, step, orders=ORDERS):
    pairs = [
        (chip * 2 + core, (chip ^ orders[core][step]) * 2 + core)
        for chip in range(16)
        for core in range(2)
    ]
    return lax.ppermute(held, AXES, pairs)


def join(held, arrived):
    return jnp.concatenate([held, arrived], axis=0)


def add_up(terms):
    total_sum = terms[0].astype(WIDE)
    for term in terms[1:]:
        total_sum = total_sum + term.astype(WIDE)
    return total_sum.astype(terms[0].dtype)


def halve(terms):
    half = terms[0].shape[0] // 2
    return [term[:half] for term in terms], add_up([term[half:] for term in terms])


def by_half(core, sums):
    mine, other = sums
    first = jnp.where(core == 0, mine, other)
    second = jnp.where(core == 0, other, mine)
    return first.astype(WIDE), second.astype(WIDE)


def dot(left_op, right_op, left_dim, right_dim):
    return lax.dot_general(
        left_op,
        right_op,
        (((left_dim,), (right_dim,)), ((), ())),
        preferred_element_type=WIDE,
    )


def each(count, size, body, flat=False):
    def step(index, carry):
        body(pl.ds(pl.multiple_of(index * size, size), size))
        return carry

    if flat:
        for index in range(count // size):
            body(pl.ds(index * size, size))
    else:
        lax.fori_loop(0, count // size, step, 0)


def block_at(index):
    return pl.ds(pl.multiple_of(index * 48, 16), 48)


def turned(block):
    return (block & 3) | ((block & 4) << 1) | ((block & 8) >> 1)


def start_copies(make, count):
    def start(place, carry):
        for copy in make(place):
            copy.start()
        return carry

    lax.fori_loop(0, count, start, 0)


def wait_for(buffer, sem):
    pltpu.make_async_copy(buffer, buffer, sem).wait()


def sources(scal, pieces):
    core = scal[CORE_AT]
    bases = (0, 8, 16, 24)
    halves = (core, core, 1 - core, 1 - core)
    return [(piece, base, half) for piece, base, half in zip(pieces, bases, halves, strict=True)]


def attn_copies(scal, pieces, lanes, mats, spot, sem, place):
    copies = []
    for source, base, half in sources(scal, pieces):
        block = scal[base + place]
        for part in range(2):
            row = block if part == 0 else jnp.where(half == 1, turned(block), block)
            copies.append(
                pltpu.make_async_copy(
                    source.at[place, pl.ds(48 * part, 48), lanes],
                    mats.at[2 * half + part, block_at(row), spot],
                    sem,
                )
            )
    return copies


def group_lanes(group):
    return 0 if group == 0 else group - 1


def head_masks(dtype):
    lane = lax.broadcasted_iota(jnp.int32, (1, 128), 1)
    first = jnp.where(lane < 64, 1.0, 0.0)
    return (first.astype(dtype), (1.0 - first).astype(dtype))


def attend_kernel(
    group,
    scal,
    tokens,
    vec,
    sines,
    cosines,
    encoded,
    *refs,
):
    pieces = refs[:4]
    (
    q_out,
    k_out,
    v_out,
    ctx_out,
    prob_out,
    mats,
    right,
    sem,
    ) = refs[4:]
    pair = pl.program_id(0)
    width = tokens.shape[1]
    rows = tokens.shape[0]

    @pl.when(pair == 0)
    def _():
        cols = mats.shape[2]
        lane_at = pl.ds(group_lanes(group) * cols, cols)
        start_copies(partial(attn_copies, scal, pieces, lane_at, mats, pl.ds(0, cols), sem), 8)
        wait_for(mats, sem)
        right[:, :width] = encoded[...]

        def project(at):
            x = tokens[at, :]
            q_out[at, :] = (dot(x, mats[0], 1, 0) + vec[4:5, :]).astype(LOW)
            k_out[at, :] = dot(x, mats[1], 1, 0).astype(LOW)
            v_out[at, :] = (dot(x, mats[2], 1, 0) + vec[5:6, :]).astype(LOW)

        each(rows, CHUNK, project)

    lanes = pl.ds(pl.multiple_of(pair * 128, 128), 128)
    right[:, width:] = k_out[:, lanes]
    rel = mats[3, :, lanes]
    live = lax.broadcasted_iota(jnp.int32, (1, rows), 1) < scal[LENGTH_AT]
    half = width // 2

    def score(at):
        q_pair = q_out[at, :] if q_out.shape[1] == 128 else q_out[at, lanes]
        sin, cos = sines[at, :], cosines[at, :]
        mixed = []
        for head, mask in enumerate(head_masks(LOW)):
            q_head = q_pair * mask
            table = dot(q_head, rel, 1, 1)
            us, uc = table[:, :half], table[:, half:]
            left = jnp.concatenate(
                [(uc * sin - us * cos).astype(LOW), (us * sin + uc * cos).astype(LOW), q_head], axis=1
            )
            s = dot(left, right[...], 1, 1) * HEAD_DIM ** (-0.5)
            s = jnp.where(live, s, MASK_FILL)
            top = jnp.max(s, axis=-1, keepdims=True)
            e = jnp.exp(s - top)
            prob = (e * (1.0 / jnp.sum(e, axis=-1, keepdims=True))).astype(LOW)
            prob_out[head, at, :] = prob
            mixed.append(dot(prob, v_out[:, lanes], 1, 0))
        masks = head_masks(WIDE)
        ctx_out[at, :] = (mixed[0] * masks[0] + mixed[1] * masks[1]).astype(LOW)

    each(rows, rows, score, True)


def any_space():
    return pl.BlockSpec(memory_space=pl.ANY)


def whole(shape):
    return pl.BlockSpec(shape, lambda *_: (0,) * len(shape))


def attend(group, scal, tokens, vec, sines, cosines, encoded, pieces):
    rows, width = tokens.shape
    cols = width // GROUPS
    pairs = cols // 128
    low = jax.ShapeDtypeStruct((rows, cols), LOW)
    return pl.pallas_call(
        partial(attend_kernel, group),
        out_shape=(low, low, low, low, jax.ShapeDtypeStruct((2 * pairs, rows, rows), LOW)),
        grid_spec=pltpu.PrefetchScalarGridSpec(
            num_scalar_prefetch=1,
            grid=(pairs,),
            in_specs=[
                whole((rows, width)),
                pl.BlockSpec((vec.shape[0], cols), lambda *_: (0, group)),
                whole((rows, width // 2)),
                whole((rows, width // 2)),
                whole((rows, width)),
            ]
            + [any_space()] * 4,
            out_specs=[whole((rows, cols))] * 3
            + [
                pl.BlockSpec((rows, 128), lambda p, _: (0, p)),
                pl.BlockSpec((2, rows, rows), lambda p, _: (p, 0, 0)),
            ],
            scratch_shapes=[
                pltpu.VMEM((4, width, cols), LOW),
                pltpu.VMEM((rows, width + 128), LOW),
                pltpu.SemaphoreType.DMA,
            ],
        ),
        compiler_params=pltpu.CompilerParams(
            dimension_semantics=("arbitrary",), vmem_limit_bytes=ATTN_VMEM_BYTES
        ),
        cost_estimate=pl.CostEstimate(
            flops=pairs * 2 * rows * width * 3072, transcendentals=0, bytes_accessed=24 * 1024 * 1024
        ),
        name="attend",
    )(scal, tokens, vec, sines, cosines, encoded, *pieces)


CDF_POLY = (
    -0.020695917308330536,
    0.09534552693367004,
    -0.15029412508010864,
    0.07120334357023239,
    -0.011180647648870945,
    0.05997580662369728,
    0.08762594312429428,
    0.11413583159446716,
    0.12694157660007477,
    0.12694266438484192,
)
CDF_SLOPE = 0.45 / math.sqrt(2.0)


def gelu_pair(x):
    size = jnp.abs(x)
    t = 1.0 / (1.0 + CDF_SLOPE * size)
    bell = jnp.exp(-0.5 * x * x)
    poly = CDF_POLY[0]
    for value in CDF_POLY[1:]:
        poly = poly * t + value
    tail = poly * t * bell
    cdf = jnp.where(x < 0.0, tail, 1.0 - tail)
    return x * cdf, cdf + x * bell * (1.0 / math.sqrt(2.0 * math.pi))


def moments(z):
    center = z - jnp.mean(z, axis=-1, keepdims=True)
    r = lax.rsqrt(jnp.mean(center * center, axis=-1, keepdims=True) + EPS_NORM)
    return center * r, r


def norm_back(grad, xh, r, gain):
    dxh = grad * gain
    return r * (
        dxh - jnp.mean(dxh, axis=-1, keepdims=True) - xh * jnp.mean(dxh * xh, axis=-1, keepdims=True)
    )


def total(values):
    return jnp.sum(values, axis=0, keepdims=True)


def out_copies(scal, pieces, out_mat, sem, place):
    return [
        pltpu.make_async_copy(
            source.at[place, :, pl.ds(0, 384)],
            out_mat.at[block_at(scal[base + place]), pl.ds(pl.multiple_of(half * 384, 128), 384)],
            sem,
        )
        for source, base, half in sources(scal, pieces)
    ]


def up_copies(scal, pieces, up_mat, sem, place):
    return [
        pltpu.make_async_copy(
            source.at[place, :, pl.ds(384 + 768 * part, 768)],
            up_mat.at[2 * half + part, block_at(scal[base + place])],
            sem,
        )
        for source, base, half in sources(scal, pieces)
        for part in range(2)
    ]


def per_core(scal, body):
    for core in range(2):

        @pl.when(scal[CORE_AT] == core)
        def _(core=core):
            body(core)


def place_at(scal, side, block):
    return scal[32 + 16 * side + block]


def feed_kernel(groups, *refs):
    scal, tokens, cot, vec = refs[:4]
    ctx_parts = refs[4 : 4 + groups]
    two_pieces, down_ref = refs[4 + groups : 8 + groups], refs[8 + groups]
    (
        page_out,
        dh1_out,
        dctx_out,
        vec_out,
        *outs,
    ) = refs[9 + groups : 17 + groups]
    two_outs, three_outs = outs[:2], outs[2:]
    (
        out_mat,
        up_mat,
        down_mat,
        ctx,
        norm_low,
        xh1,
        r1,
        act,
        slope,
        held,
        df,
        dpre,
        dattn,
        g_out,
        g_up,
        g_down,
        sem_in,
        sem_up,
        sem_down,
        sem_out,
    ) = refs[17 + groups :]
    step = pl.program_id(0)
    rows, width = tokens.shape
    length = scal[LENGTH_AT]

    @pl.when(step == 0)
    def _():
        start_copies(partial(out_copies, scal, two_pieces, out_mat, sem_in.at[0]), 8)
        start_copies(partial(up_copies, scal, two_pieces, up_mat, sem_in.at[1]), 8)
        pltpu.make_async_copy(down_ref, down_mat, sem_in.at[2]).start()
        wait_for(out_mat, sem_in.at[0])
        vec_out[...] = jnp.zeros_like(vec_out)
        cols = width // groups
        for g in range(groups):
            ctx[:, cols * g : cols * (g + 1)] = ctx_parts[g][...]

        def first(at):
            attn = dot(ctx[at, :], out_mat[...], 1, 0) + vec[6:7, :]
            hat, r = moments(tokens[at, :].astype(WIDE) + attn)
            normed = hat * vec[0:1, :] + vec[1:2, :]
            xh1[at, :] = hat
            r1[at, :] = jnp.broadcast_to(r, (r.shape[0], 128))
            norm_low[at, :] = normed.astype(LOW)
            held[at, :] = normed + vec[7:8, :]

        each(rows, CHUNK, first)
        wait_for(up_mat, sem_in.at[1])
        wait_for(down_mat, sem_in.at[2])

    @pl.when(step < 4)
    def _():
        bias = vec[pl.ds(8 + step, 1), :]
        down_at = pl.ds(pl.multiple_of(step * width, width), width)
        spots = [pl.ds(CHUNK * index, CHUNK) for index in range(rows // CHUNK)]

        def front(at):
            return dot(norm_low[at, :], up_mat[step], 1, 0) + bias

        pre = front(spots[0])
        for index, at in enumerate(spots):
            ahead = front(spots[index + 1]) if index + 1 < len(spots) else None
            value, grad = gelu_pair(pre)
            low = value.astype(LOW)
            act[step, at, :] = low
            slope[step, at, :] = grad
            held[at, :] += dot(low, down_mat[down_at, :], 1, 0)
            pre = ahead

    @pl.when(step == 3)
    def _():
        def second(at):
            hat, r = moments(held[at, :])
            place = lax.broadcasted_iota(jnp.int32, (SLAB, 1), 0) + at.start
            live = jnp.where(place < length, 1.0, 0.0)
            page_out[at, :] = ((hat * vec[2:3, :] + vec[3:4, :]) * live).astype(LOW)
            dy = cot[at, :].astype(WIDE) * live
            vec_out[2:3, :] += total(dy * hat)
            vec_out[3:4, :] += total(dy)
            dh2 = norm_back(dy, hat, r, vec[2:3, :])
            low = dh2.astype(LOW)
            df[at, :] = low
            vec_out[7:8, :] += total(low.astype(WIDE))
            held[at, :] = dh2

        each(rows, SLAB, second)

    def send_up(slot, unit):
        at = pl.ds(pl.multiple_of(384 + 768 * lax.rem(unit, 2), 128), 768)
        for side in range(2):

            @pl.when((unit // 2 == scal[CORE_AT]) == (side == 0))
            def _(side=side):
                def body(block, carry):
                    pltpu.make_async_copy(
                        g_up.at[slot, block_at(block)],
                        two_outs[side].at[place_at(scal, side, block), :, at],
                        sem_up.at[slot],
                    ).start()
                    return carry

                lax.fori_loop(0, 16, body, 0)

    def send_down(slot, unit):
        def body(core):
            for part in range(8):
                side = (part % 2) ^ core
                pltpu.make_async_copy(
                    g_down.at[slot, pl.ds(96 * part, 96)],
                    three_outs[side].at[place_at(scal, side, 4 * unit + part // 2)],
                    sem_down.at[slot],
                ).start()

        per_core(scal, body)

    def send_out():
        def on(core):
            def body(block, carry):
                for half in range(2):
                    side = half ^ core
                    pltpu.make_async_copy(
                        g_out.at[block_at(block), pl.ds(384 * half, 384)],
                        two_outs[side].at[place_at(scal, side, block), :, pl.ds(0, 384)],
                        sem_out,
                    ).start()
                return carry

            lax.fori_loop(0, 16, body, 0)

        per_core(scal, on)

    @pl.when(step >= 4)
    def _():
        unit = step - 4
        slot = lax.rem(unit, 2)
        down_at = pl.ds(pl.multiple_of(unit * width, width), width)

        @pl.when(unit >= 2)
        def _():
            wait_for(g_up.at[slot], sem_up.at[slot])
            wait_for(g_down.at[slot], sem_down.at[slot])

        def backward(at):
            grad = dot(df[at, :], down_mat[down_at, :], 1, 1) * slope[unit, at, :]
            low = grad.astype(LOW)
            dpre[at, :] = low
            vec_out[pl.ds(8 + unit, 1), :] += total(low.astype(WIDE))
            held[at, :] += dot(low, up_mat[unit], 1, 1)

        each(rows, rows, backward, True)

        def weights(at):
            g_down[slot, at, :] = dot(act[unit, :, at], df[...], 0, 0).astype(LOW)
            g_up[slot, at, :] = dot(norm_low[:, at], dpre[...], 0, 0).astype(LOW)

        each(width, width, weights, True)
        send_down(slot, unit)
        send_up(slot, unit)

    @pl.when(step == 7)
    def _():
        def last(at):
            grad, hat = held[at, :], xh1[at, :]
            vec_out[0:1, :] += total(grad * hat)
            vec_out[1:2, :] += total(grad)
            dh1 = norm_back(grad, hat, r1[at, :1], vec[0:1, :])
            dh1_out[at, :] = dh1
            low = dh1.astype(LOW)
            dattn[at, :] = low
            vec_out[6:7, :] += total(low.astype(WIDE))

        each(rows, SLAB, last)

        def context(at):
            dctx_out[at, :] = dot(dattn[at, :], out_mat[...], 1, 1).astype(LOW)

        each(rows, CHUNK, context)

        def weights(at):
            g_out[at, :] = dot(ctx[:, at], dattn[...], 0, 0).astype(LOW)

        each(width, CHUNK, weights)
        send_out()
        for slot in range(2):
            wait_for(g_up.at[slot], sem_up.at[slot])
            wait_for(g_down.at[slot], sem_down.at[slot])
        wait_for(g_out, sem_out)


def feed(scal, tokens, cot, vec, ctx_parts, two, down):
    rows, width = tokens.shape
    groups = len(ctx_parts)
    return pl.pallas_call(
        partial(feed_kernel, groups),
        out_shape=(
            jax.ShapeDtypeStruct((rows, width), LOW),
            jax.ShapeDtypeStruct((rows, width), WIDE),
            jax.ShapeDtypeStruct((rows, width), LOW),
            jax.ShapeDtypeStruct((16, width), WIDE),
        )
        + (jax.ShapeDtypeStruct((16, 48, 384 + 2 * width), LOW),) * 2
        + (jax.ShapeDtypeStruct((16, 96, width), LOW),) * 2,
        grid_spec=pltpu.PrefetchScalarGridSpec(
            num_scalar_prefetch=1,
            grid=(8,),
            in_specs=[whole((rows, width)), whole((rows, width)), whole((16, width))]
            + [whole((rows, width // groups))] * groups
            + [any_space()] * 5,
            out_specs=[whole((rows, width))] * 3 + [whole((16, width))] + [any_space()] * 4,
            scratch_shapes=[
                pltpu.VMEM((width, width), LOW),
                pltpu.VMEM((4, width, width), LOW),
                pltpu.VMEM((4 * width, width), LOW),
                pltpu.VMEM((rows, width), LOW),
                pltpu.VMEM((rows, width), LOW),
                pltpu.VMEM((rows, width), WIDE),
                pltpu.VMEM((rows, 128), WIDE),
                pltpu.VMEM((4, rows, width), LOW),
                pltpu.VMEM((4, rows, width), WIDE),
                pltpu.VMEM((rows, width), WIDE),
                pltpu.VMEM((rows, width), LOW),
                pltpu.VMEM((rows, width), LOW),
                pltpu.VMEM((rows, width), LOW),
                pltpu.VMEM((width, width), LOW),
                pltpu.VMEM((2, width, width), LOW),
                pltpu.VMEM((2, width, width), LOW),
                pltpu.SemaphoreType.DMA((3,)),
                pltpu.SemaphoreType.DMA((2,)),
                pltpu.SemaphoreType.DMA((2,)),
                pltpu.SemaphoreType.DMA,
            ],
        ),
        compiler_params=pltpu.CompilerParams(
            dimension_semantics=("arbitrary",), vmem_limit_bytes=VMEM_BYTES
        ),
        cost_estimate=pl.CostEstimate(
            flops=2 * rows * width * width * 27, transcendentals=0, bytes_accessed=32 * 1024 * 1024
        ),
        name="feed",
    )(scal, tokens, cot, vec, *ctx_parts, *two, down)


def unattend_kernel(
    group,
    scal,
    tokens,
    sines,
    cosines,
    encoded,
    q_in,
    k_in,
    v_in,
    dctx_in,
    prob,
    *refs,
):
    pieces = refs[:4]
    refs = refs[4:] if group != 1 else refs[6:]
    dq_out, dk_out, dv_out, vec_out = refs[:4]
    outs = refs[4:6]
    (
    mats,
    right,
    ds_low,
    du_low,
    q_heads,
    d_heads,
    grads,
    sem,
    sem_out,
    ) = refs[6:]
    pair = pl.program_id(0)
    rows, width = tokens.shape
    half = width // 2
    scale = HEAD_DIM ** (-0.5)

    @pl.when(pair == 0)
    def _():
        cols = mats.shape[2]
        lane_at = pl.ds(group_lanes(group) * cols, cols)
        start_copies(partial(attn_copies, scal, pieces, lane_at, mats, pl.ds(0, cols), sem), 8)
        wait_for(mats, sem)
        right[:, :width] = encoded[...]

    lanes = pl.ds(pl.multiple_of(pair * 128, 128), 128)
    right[:, width:] = k_in[...]
    rel = mats[3, :, lanes]
    low_masks, wide_masks = head_masks(LOW), head_masks(WIDE)

    def score(at):
        sin, cos = sines[at, :], cosines[at, :]
        dq = None
        for head in range(2):
            spot = pl.ds(pl.multiple_of(head * rows + at.start, at.size), at.size)
            dctx = dctx_in[at, :] * low_masks[head]
            d_heads[spot, :] = dctx
            q_heads[spot, :] = q_in[at, :] * low_masks[head]
            p = prob[head, at, :].astype(WIDE)
            dp = dot(dctx, v_in[...], 1, 1)
            ds = (p * (dp - jnp.sum(p * dp, axis=-1, keepdims=True))).astype(LOW)
            ds_low[spot, :] = ds
            dl = dot(ds, right[...], 1, 0) * scale
            ls, lc = dl[:, :half], dl[:, half:width]
            du = jnp.concatenate(
                [(lc * sin - ls * cos).astype(LOW), (ls * sin + lc * cos).astype(LOW)], axis=1
            )
            du_low[spot, :] = du
            part = (dl[:, width:] + dot(du, rel, 1, 0)) * wide_masks[head]
            dq = part if dq is None else dq + part
        dq_out[at, lanes] = dq.astype(LOW)

    each(rows, rows, score, True)
    dv_out[:, lanes] = dot(prob[...].reshape(2 * rows, rows), d_heads[...], 0, 0).astype(LOW)
    dk_out[:, lanes] = (dot(ds_low[...], q_heads[...], 0, 0) * scale).astype(LOW)
    grads[3, :, lanes] = dot(du_low[...], q_heads[...], 0, 0).astype(LOW)

    @pl.when(pair == pl.num_programs(0) - 1)
    def _():
        def weights(at):
            x = tokens[:, at]
            grads[0, at, :] = dot(x, dq_out[...], 0, 0).astype(LOW)
            grads[1, at, :] = dot(x, dk_out[...], 0, 0).astype(LOW)
            grads[2, at, :] = dot(x, dv_out[...], 0, 0).astype(LOW)

        each(width, CHUNK, weights)

        spot = pl.ds(mats.shape[2] if group == 1 else 0, mats.shape[2])

        def on(core):
            def body(block, carry):
                for slot in range(4):
                    row = turned(block) if slot == 3 else block
                    side = (slot // 2) ^ core
                    pltpu.make_async_copy(
                        grads.at[slot, block_at(row)],
                        outs[side].at[place_at(scal, side, block), pl.ds(48 * (slot % 2), 48), spot],
                        sem_out,
                    ).start()
                return carry

            lax.fori_loop(0, 16, body, 0)

        per_core(scal, on)
        vec_out[...] = jnp.zeros_like(vec_out)
        vec_out[0:1, :] = total(dq_out[...].astype(WIDE))
        vec_out[1:2, :] = total(dv_out[...].astype(WIDE))
        wait_for(grads, sem_out)


def unattend(group, scal, tokens, sines, cosines, encoded, q, k, v, dctx, prob, pieces, blocks):
    rows, width = tokens.shape
    cols = width // GROUPS
    pairs = cols // 128
    low = jax.ShapeDtypeStruct((rows, cols), LOW)
    lane_block = pl.BlockSpec((rows, 128), lambda p, _: (0, p))
    return pl.pallas_call(
        partial(unattend_kernel, group),
        out_shape=(low, low, low, jax.ShapeDtypeStruct((8, cols), WIDE))
        + (jax.ShapeDtypeStruct((16, 96, cols if group == 2 else 2 * cols), LOW),) * 2,
        grid_spec=pltpu.PrefetchScalarGridSpec(
            num_scalar_prefetch=1,
            grid=(pairs,),
            in_specs=[
                whole((rows, width)),
                whole((rows, half_of(width))),
                whole((rows, half_of(width))),
                whole((rows, width)),
                lane_block,
                lane_block,
                lane_block,
                pl.BlockSpec((rows, 128), lambda p, _: (0, group * pairs + p)),
                pl.BlockSpec((2, rows, rows), lambda p, _: (p, 0, 0)),
            ]
            + [any_space()] * (4 + len(blocks)),
            out_specs=[whole((rows, cols))] * 3 + [whole((8, cols))] + [any_space()] * 2,
            scratch_shapes=[
                pltpu.VMEM((4, width, cols), LOW),
                pltpu.VMEM((rows, width + 128), LOW),
                pltpu.VMEM((2 * rows, rows), LOW),
                pltpu.VMEM((2 * rows, width), LOW),
                pltpu.VMEM((2 * rows, 128), LOW),
                pltpu.VMEM((2 * rows, 128), LOW),
                pltpu.VMEM((4, width, cols), LOW),
                pltpu.SemaphoreType.DMA,
                pltpu.SemaphoreType.DMA,
            ],
        ),
        compiler_params=pltpu.CompilerParams(
            dimension_semantics=("arbitrary",), vmem_limit_bytes=ATTN_VMEM_BYTES
        ),
        cost_estimate=pl.CostEstimate(
            flops=pairs * 2 * rows * width * 5000, transcendentals=0, bytes_accessed=24 * 1024 * 1024
        ),
        input_output_aliases={14 + at: 4 + at for at in range(len(blocks))},
        name="unattend",
    )(scal, tokens, sines, cosines, encoded, q, k, v, dctx, prob, *pieces, *blocks)


def half_of(width):
    return width // 2


def input_grad_kernel(scal, dh1, *refs):
    parts, near = refs[: 3 * GROUPS], refs[3 * GROUPS : 3 * GROUPS + 4]
    rest = refs[3 * GROUPS + 4 : 3 * GROUPS + 8]
    out, mats, sem = refs[3 * GROUPS + 8 :]
    rows, width = dh1.shape
    cols = width // GROUPS
    for pieces, start, size in ((near, 0, cols), (rest, cols, width - cols)):
        at = pl.ds(start, size)
        start_copies(partial(attn_copies, scal, pieces, pl.ds(0, size), mats, at, sem), 8)
    wait_for(mats, sem)

    def rows_of(at):
        grad = dh1[at, :]
        for slot in range(3):
            left = jnp.concatenate([parts[3 * g + slot][at, :] for g in range(GROUPS)], axis=1)
            grad = grad + dot(left, mats[slot], 1, 1)
        out[at, :] = grad

    each(rows, CHUNK, rows_of)


def input_grad(scal, dh1, parts, pieces):
    rows, width = dh1.shape
    cols = width // GROUPS
    return pl.pallas_call(
        input_grad_kernel,
        out_shape=jax.ShapeDtypeStruct((rows, width), WIDE),
        grid_spec=pltpu.PrefetchScalarGridSpec(
            num_scalar_prefetch=1,
            grid=(1,),
            in_specs=[whole((rows, width))]
            + [whole((rows, cols))] * (3 * GROUPS)
            + [any_space()] * 8,
            out_specs=whole((rows, width)),
            scratch_shapes=[pltpu.VMEM((4, width, width), LOW), pltpu.SemaphoreType.DMA],
        ),
        compiler_params=pltpu.CompilerParams(
            dimension_semantics=("arbitrary",), vmem_limit_bytes=VMEM_BYTES
        ),
        cost_estimate=pl.CostEstimate(
            flops=2 * rows * width * width * 3, transcendentals=0, bytes_accessed=10 * 1024 * 1024
        ),
        name="input_grad",
    )(scal, dh1, *parts, *pieces)


GROUPS = 3


def local(
    tokens,
    boxes,
    lengths,
    cotangent,
    attn_weight,
    up_weight,
    down_weight,
    vectors,
    attn_first,
    up_first,
    down_first,
    vector_first,
    attn_second,
    up_second,
    down_second,
    vector_second,
):
    chip, core = lax.axis_index("fsdp"), lax.axis_index("rep")
    width = tokens.shape[2]
    cols = width // GROUPS
    first = core == 0
    page = tokens[0]
    same = (ORDERS[0], ORDERS[0])

    def attn_own(start, stop):
        own = jnp.where(first, attn_weight[:2, :, start:stop], attn_weight[2:5:2, :, start:stop])
        return own.astype(LOW).reshape(1, 96, stop - start)

    near = attn_own(0, cols)
    near_far = hop(near, 0)
    tick = after(lengths, near)
    down_own = after(jnp.where(first, down_weight[:96], down_weight[96:]).astype(LOW), tick)
    rest = after(attn_own(cols, width), tick)
    vec = after(vectors.astype(LOW), tick)
    vec = lax.dynamic_update_slice(
        jnp.zeros((vectors.shape[0], width), LOW), vec, (jnp.int32(0), chip * vectors.shape[1])
    )
    scal = block_scalars(chip, core, lengths[0])
    near = join(near, near_far)
    tick = after(tick, near, rest, down_own, vec, scal)

    near_far = hop(after(near, tick), 1)
    rest_far = hop(after(rest, tick), 0)
    vec_far = hop(after(vec, tick), 0, same)
    down_full = lax.all_gather(after(down_own, tick), AXES, axis=0, tiled=True)
    two = after(
        jnp.concatenate(
            [
                jnp.where(first, attn_weight[3, :, :384], attn_weight[3, :, 384:]),
                jnp.where(first, up_weight[:, :1536], up_weight[:, 1536:]),
            ],
            axis=1,
        ).astype(LOW)[None],
        tick,
    )
    near, vec, rest = join(near, near_far), vec + vec_far, join(rest, rest_far)
    tick = after(tick, near, vec, two, rest)

    near_far = hop(after(near, tick), 2)
    vec_far = hop(after(vec, tick), 1, same)
    rest_far = hop(after(rest, tick), 1)
    two_far = hop(after(two, tick), 0)
    quarter = width // 4
    frequency = jnp.exp(jnp.arange(quarter).astype(WIDE) * (-math.log(10000.0) / quarter))
    place = after(boxes[0], tick).astype(WIDE)
    angles = jnp.concatenate([place[0][:, None] * frequency, place[1][:, None] * frequency], axis=1)
    sines, cosines = jnp.sin(angles), jnp.cos(angles)
    encoded = jnp.concatenate([sines, cosines], axis=1).astype(LOW)
    near, vec = join(near, near_far), vec + vec_far
    tick = after(tick, near, vec, sines, cosines, encoded)

    vec_far = hop(after(vec, tick), 2, same)
    near_far = hop(after(near, tick), 3)
    near_swap = swap_cores(after(near, tick))
    vec = vec + vec_far
    tick = after(tick, near_far, vec)

    near_far_swap = swap_cores(after(near_far, tick))
    vec_far = hop(after(vec, tick), 3, same)
    rest, two = join(rest, rest_far), join(two, two_far)
    rest_far = hop(after(rest, tick), 2)
    two_far = hop(after(two, tick), 1)
    vec = jnp.pad((vec + vec_far).astype(WIDE), ((0, 16 - vec.shape[0]), (0, 0)))
    near_pieces = (near, near_far, near_swap, near_far_swap)

    def go(group, tick):
        pieces = near_pieces if group == 0 else rest_pieces
        return attend(group, after(scal, tick), page, vec, sines, cosines, encoded, pieces)

    kept = [go(0, tick)]
    rest, two = join(rest, rest_far), join(two, two_far)
    tick = after(tick, rest, two, kept[0][3])

    rest_far = hop(after(rest, tick), 3)
    two_far = hop(after(two, tick), 2)
    rest_swap = swap_cores(after(rest, tick))
    tick = after(tick, rest_far)
    rest_pieces = (rest, rest_far, rest_swap, swap_cores(after(rest_far, tick)))
    two = join(two, two_far)
    tick = after(tick, rest_pieces[3], two)
    two_far = hop(after(two, tick), 3)
    two_swap = swap_cores(after(two, tick))
    kept.append(go(1, tick))
    tick = after(tick, kept[1][3])
    kept.append(go(2, tick))
    two_far = after(two_far, kept[2][3])
    two_pieces = (two, two_far, two_swap, swap_cores(two_far))

    page_out, dh1, dctx, vec_one, *sent = feed(
        scal, page, cotangent[0], vec, [k[3] for k in kept], two_pieces, down_full
    )

    tick = after(tick, dctx)
    three_terms, three_high = halve([sent[2], swap_cores(sent[3])])
    two_swap = swap_cores(sent[1])
    tick = after(tick, three_high)

    def undo(group, tick, blocks):
        return unattend(
            group,
            after(scal, tick),
            page,
            sines,
            cosines,
            encoded,
            *kept[group][:3],
            dctx,
            kept[group][4],
            near_pieces if group == 0 else rest_pieces,
            blocks,
        )

    three_far = hop(after(three_high, tick), 3)
    two_terms, two_high = halve([sent[0], two_swap])
    back = [undo(0, tick, [])]
    tick = after(tick, three_far, two_high, back[0][0])

    two_far = hop(after(two_high, tick), 3)
    three_terms, three_high = halve(three_terms + [three_far])
    back.append(undo(1, tick, back[0][4:]))
    tick = after(tick, two_far, three_high, back[1][0])

    three_far = hop(after(three_high, tick), 2)
    two_terms, two_high = halve(two_terms + [two_far])
    two_far = hop(after(two_high, tick), 2)
    one_swap = swap_cores(after(back[1][5], tick))
    back.append(undo(2, tick, []))
    one_terms, one_high = halve([back[1][4], one_swap])
    three_terms, three_high = halve(three_terms + [three_far])
    two_terms, two_high = halve(two_terms + [two_far])
    tick = after(tick, three_high, two_high, one_high, back[2][0])

    end_swap = swap_cores(after(back[2][5], tick))
    one_far = hop(after(one_high, tick), 3)
    three_far = hop(after(three_high, tick), 1)
    two_far = hop(after(two_high, tick), 1)
    end_terms, end_high = halve([back[2][4], end_swap])
    tick = after(tick, end_high)
    end_far = hop(after(end_high, tick), 3)
    vec_two = jnp.concatenate([b[3][:2] for b in back], axis=1)
    vec_grad = jnp.concatenate([vec_one[:4], vec_two, vec_one[6:12]], axis=0)
    vec_grad = vec_grad + swap_cores(after(vec_grad, tick))
    token_grad = input_grad(
        after(scal, tick), dh1, [part for b in back for part in b[:3]], near_pieces + rest_pieces
    )
    one_terms, one_high = halve(one_terms + [one_far])
    three_terms, three_high = halve(three_terms + [three_far])
    two_terms, two_high = halve(two_terms + [two_far])
    end_terms, end_high = halve(end_terms + [end_far])
    tick = after(tick, end_high, one_high, three_high, two_high, vec_grad, token_grad)

    end_far = hop(after(end_high, tick), 2)
    one_far = hop(after(one_high, tick), 2)
    three_far = hop(after(three_high, tick), 0)
    two_far = hop(after(two_high, tick), 0)
    vec_grad = vec_grad + hop(after(vec_grad, tick), 2, same)
    end_terms, end_high = halve(end_terms + [end_far])
    one_terms, one_high = halve(one_terms + [one_far])
    tick = after(tick, end_high, one_high, vec_grad)

    end_far = hop(after(end_high, tick), 1)
    one_far = hop(after(one_high, tick), 1)
    vec_grad = vec_grad + hop(after(vec_grad, tick), 3, same)
    three_mine = add_up(three_terms + [three_far])[0]
    two_mine = add_up(two_terms + [two_far])[0]
    three_sum = by_half(core, (three_mine, swap_cores(after(three_mine, tick))))
    two_sum = by_half(core, (two_mine, swap_cores(after(two_mine, tick))))
    end_terms, end_high = halve(end_terms + [end_far])
    one_terms, one_high = halve(one_terms + [one_far])
    tick = after(tick, end_high, one_high, vec_grad)

    end_far = hop(after(end_high, tick), 0)
    one_far = hop(after(one_high, tick), 0)
    vec_grad = vec_grad + hop(after(vec_grad, tick), 0, same)
    vec_grad = vec_grad + hop(vec_grad, 1, same)
    one_mine = jnp.concatenate(
        [add_up(one_terms + [one_far])[0], add_up(end_terms + [end_far])[0]], axis=1
    )
    one_sum = by_half(core, (one_mine, swap_cores(one_mine)))
    vec_sum = lax.dynamic_slice(
        vec_grad, (jnp.int32(0), chip * vectors.shape[1]), vectors.shape
    )

    reduced = (
        jnp.stack(
            [
                one_sum[0][:48],
                one_sum[0][48:],
                one_sum[1][:48],
                jnp.concatenate([two_sum[0][:, :384], two_sum[1][:, :384]], axis=1),
                one_sum[1][48:],
            ]
        ),
        jnp.concatenate([two_sum[0][:, 384:], two_sum[1][:, 384:]], axis=1),
        jnp.concatenate(three_sum, axis=0),
        vec_sum,
    )
    layer_out, token_grad = page_out[None], token_grad[None]
    attn_rates = jnp.array(ATTN_RATES, jnp.float32)[:, None, None]
    attn_new, attn_first_new, attn_second_new = adam_update(
        attn_weight, attn_first, attn_second, reduced[0], attn_rates, WEIGHT_DECAY
    )
    up_new, up_first_new, up_second_new = adam_update(
        up_weight, up_first, up_second, reduced[1], UP_RATE, WEIGHT_DECAY
    )
    down_new, down_first_new, down_second_new = adam_update(
        down_weight, down_first, down_second, reduced[2], DOWN_RATE, WEIGHT_DECAY
    )
    vectors_new, vector_first_new, vector_second_new = adam_update(
        vectors, vector_first, vector_second, reduced[3], VECTOR_RATE, 0.0
    )
    return (
        layer_out,
        token_grad,
        attn_new,
        up_new,
        down_new,
        vectors_new,
        attn_first_new,
        up_first_new,
        down_first_new,
        vector_first_new,
        attn_second_new,
        up_second_new,
        down_second_new,
        vector_second_new,
        attn_new.astype(jnp.bfloat16),
        up_new.astype(jnp.bfloat16),
        down_new.astype(jnp.bfloat16),
        vectors_new.astype(jnp.bfloat16),
    )


def local_general(
    tokens,
    boxes,
    lengths,
    cotangent,
    attn_weight,
    up_weight,
    down_weight,
    vectors,
    attn_first,
    up_first,
    down_first,
    vector_first,
    attn_second,
    up_second,
    down_second,
    vector_second,
):
    lowered = (
        attn_weight.astype(jnp.bfloat16),
        up_weight.astype(jnp.bfloat16),
        down_weight.astype(jnp.bfloat16),
        vectors.astype(jnp.bfloat16),
    )
    gathered = (
        lax.all_gather(lowered[0], "fsdp", axis=1, tiled=True),
        lax.all_gather(lowered[1], "fsdp", axis=0, tiled=True),
        lax.all_gather(lowered[2], "fsdp", axis=0, tiled=True),
        lax.all_gather(lowered[3], "fsdp", axis=1, tiled=True),
    )

    def forward_step(carry, page):
        token_row_block, box_rows, page_length = page
        return (carry, forward_page(gathered, token_row_block, box_rows, page_length))

    _, (layer_out, saved_all) = lax.scan(forward_step, None, (tokens, boxes, lengths))
    backward_weights = (
        lax.all_gather(lowered[0], "fsdp", axis=1, tiled=True),
        lax.all_gather(lowered[1], "fsdp", axis=0, tiled=True),
        lax.all_gather(lowered[2], "fsdp", axis=0, tiled=True),
        lax.all_gather(lowered[3], "fsdp", axis=1, tiled=True),
    )
    model_width = gathered[0].shape[2]
    ffn_width = gathered[1].shape[1]
    zero_grads = (
        jnp.zeros((5, model_width, model_width), jnp.float32),
        jnp.zeros((model_width, ffn_width), jnp.float32),
        jnp.zeros((ffn_width, model_width), jnp.float32),
        jnp.zeros(gathered[3].shape, jnp.float32),
    )

    def backward_step(totals, page):
        token_row_block, box_rows, page_length, upstream, saved_state = page
        token_grad, grads = backward_page(
            backward_weights, token_row_block, box_rows, page_length, upstream, saved_state
        )
        return (jax.tree.map(jnp.add, totals, grads), token_grad)

    totals, token_grad = lax.scan(
        backward_step, zero_grads, (tokens, boxes, lengths, cotangent, saved_all)
    )
    shards = (
        lax.psum_scatter(totals[0], "fsdp", scatter_dimension=1, tiled=True),
        lax.psum_scatter(totals[1], "fsdp", scatter_dimension=0, tiled=True),
        lax.psum_scatter(totals[2], "fsdp", scatter_dimension=0, tiled=True),
        lax.psum_scatter(totals[3], "fsdp", scatter_dimension=1, tiled=True),
    )
    reduced = (
        lax.psum(shards[0].astype(jnp.bfloat16), "rep").astype(jnp.float32),
        lax.psum(shards[1].astype(jnp.bfloat16), "rep").astype(jnp.float32),
        lax.psum(shards[2].astype(jnp.bfloat16), "rep").astype(jnp.float32),
        lax.psum(shards[3].astype(jnp.bfloat16), "rep").astype(jnp.float32),
    )
    attn_rates = jnp.array(ATTN_RATES, jnp.float32)[:, None, None]
    attn_new, attn_first_new, attn_second_new = adam_update(
        attn_weight, attn_first, attn_second, reduced[0], attn_rates, WEIGHT_DECAY
    )
    up_new, up_first_new, up_second_new = adam_update(
        up_weight, up_first, up_second, reduced[1], UP_RATE, WEIGHT_DECAY
    )
    down_new, down_first_new, down_second_new = adam_update(
        down_weight, down_first, down_second, reduced[2], DOWN_RATE, WEIGHT_DECAY
    )
    vectors_new, vector_first_new, vector_second_new = adam_update(
        vectors, vector_first, vector_second, reduced[3], VECTOR_RATE, 0.0
    )
    return (
        layer_out,
        token_grad,
        attn_new,
        up_new,
        down_new,
        vectors_new,
        attn_first_new,
        up_first_new,
        down_first_new,
        vector_first_new,
        attn_second_new,
        up_second_new,
        down_second_new,
        vector_second_new,
        attn_new.astype(jnp.bfloat16),
        up_new.astype(jnp.bfloat16),
        down_new.astype(jnp.bfloat16),
        vectors_new.astype(jnp.bfloat16),
    )


def solution(mesh):
    blocked = mesh.shape["fsdp"] == 16 and mesh.shape["rep"] == 2
    return jax.shard_map(
        local if blocked else local_general,
        mesh=mesh,
        in_specs=(
            P(("fsdp", "rep"), None, None),
            P(("fsdp", "rep"), None, None),
            P(("fsdp", "rep")),
            P(("fsdp", "rep"), None, None),
            P(None, "fsdp", None),
            P("fsdp", None),
            P("fsdp", None),
            P(None, "fsdp"),
            P(None, "fsdp", None),
            P("fsdp", None),
            P("fsdp", None),
            P(None, "fsdp"),
            P(None, "fsdp", None),
            P("fsdp", None),
            P("fsdp", None),
            P(None, "fsdp"),
        ),
        out_specs=(
            P(("fsdp", "rep"), None, None),
            P(("fsdp", "rep"), None, None),
            P(None, "fsdp", None),
            P("fsdp", None),
            P("fsdp", None),
            P(None, "fsdp"),
            P(None, "fsdp", None),
            P("fsdp", None),
            P("fsdp", None),
            P(None, "fsdp"),
            P(None, "fsdp", None),
            P("fsdp", None),
            P("fsdp", None),
            P(None, "fsdp"),
            P(None, "fsdp", None),
            P("fsdp", None),
            P("fsdp", None),
            P(None, "fsdp"),
        ),
        check_vma=False,
    )
```

```python
from functools import partial
import math

import jax
import jax.numpy as jnp
from jax import lax
from jax.experimental import pallas as pl
from jax.experimental.pallas import tpu as pltpu
from jax.sharding import PartitionSpec as P

HEADS = 12
HEAD_DIM = 64
STEP = 7


EPS_NORM = 1e-12
EPS_ADAM = 1e-08
DECAY = 0.5
MASK_FILL = -1e30
WEIGHT_DECAY = 0.01
ATTN_RATES = (0.04, 0.04, 0.04, 0.2, 0.04)
UP_RATE = 0.04
DOWN_RATE = 0.02
VECTOR_RATE = 0.3


def contract(left_op, right_op, left_dim, right_dim):
    return lax.dot_general(
        left_op,
        right_op,
        (((left_dim,), (right_dim,)), ((), ())),
        preferred_element_type=jnp.float32,
    )


def layer_norm(hidden, gain_row, shift_row):
    center = hidden - jnp.mean(hidden, axis=-1, keepdims=True)
    spread = jnp.mean(center * center, axis=-1, keepdims=True)
    return center * lax.rsqrt(spread + EPS_NORM) * gain_row + shift_row


def box_tables(box_rows, model_width):
    quarter = model_width // 4
    frequency = jnp.exp(jnp.arange(quarter).astype(jnp.float32) * (-math.log(10000.0) / quarter))
    angles = box_rows.astype(jnp.float32)[:, :, None] * frequency
    return (jnp.sin(angles), jnp.cos(angles))


def encode(sine_rows, cosine_rows):
    return jnp.concatenate([sine_rows[0], cosine_rows[0], sine_rows[1], cosine_rows[1]], axis=-1)


def rotate(pos_table, sine_rows, cosine_rows):
    quarter = sine_rows.shape[-1]
    pieces = []
    for coord in range(2):
        sine_part = pos_table[..., 2 * coord * quarter : (2 * coord + 1) * quarter]
        cosine_part = pos_table[..., (2 * coord + 1) * quarter : (2 * coord + 2) * quarter]
        pieces.append(cosine_part * sine_rows[coord] - sine_part * cosine_rows[coord])
        pieces.append(sine_part * sine_rows[coord] + cosine_part * cosine_rows[coord])
    return jnp.concatenate(pieces, axis=-1)


def scores(query_rows, key_rows, left_rows, encoded, page_live):
    text_part = jnp.einsum("ihd,jhd->hij", query_rows, key_rows, preferred_element_type=jnp.float32)
    place_part = jnp.einsum("hie,je->hij", left_rows, encoded, preferred_element_type=jnp.float32)
    score_rows = (text_part + place_part) * HEAD_DIM ** (-0.5)
    return jnp.where(page_live[None, None, :], score_rows, MASK_FILL)


def forward_page(weights, token_row_block, box_rows, page_length):
    attention_matrices, up_mat, down_mat, vector_rows = weights
    row_count, model_width = token_row_block.shape
    vector_f32 = vector_rows.astype(jnp.float32)
    page_live = jnp.arange(row_count) < page_length
    projected_rows = jnp.einsum(
        "tb,mby->mty", token_row_block, attention_matrices[:3], preferred_element_type=jnp.float32
    )
    query_rows = (
        (projected_rows[0] + vector_f32[4]).astype(jnp.bfloat16).reshape(row_count, HEADS, HEAD_DIM)
    )
    key_rows = projected_rows[1].astype(jnp.bfloat16).reshape(row_count, HEADS, HEAD_DIM)
    value_rows = (
        (projected_rows[2] + vector_f32[5]).astype(jnp.bfloat16).reshape(row_count, HEADS, HEAD_DIM)
    )
    sine_rows, cosine_rows = box_tables(box_rows, model_width)
    encoded = encode(sine_rows, cosine_rows).astype(jnp.bfloat16)
    rel_heads = attention_matrices[4].reshape(model_width, HEADS, HEAD_DIM)
    pos_table = jnp.einsum(
        "ihd,ehd->hie", query_rows, rel_heads, preferred_element_type=jnp.float32
    )
    left_rows = rotate(pos_table, sine_rows, cosine_rows).astype(jnp.bfloat16)
    score_rows = scores(query_rows, key_rows, left_rows, encoded, page_live)
    row_top = jnp.max(score_rows, axis=-1, keepdims=True)
    exponent = jnp.exp(score_rows - row_top)
    row_total = jnp.sum(exponent, axis=-1, keepdims=True)
    prob_low = (exponent / row_total).astype(jnp.bfloat16)
    logsum = row_top + jnp.log(row_total)
    mixed_rows = jnp.einsum(
        "hij,jhd->ihd", prob_low, value_rows, preferred_element_type=jnp.float32
    )
    context = mixed_rows.reshape(row_count, model_width).astype(jnp.bfloat16)
    attn_out = (
        jnp.dot(context, attention_matrices[3], preferred_element_type=jnp.float32) + vector_f32[6]
    )
    first_sum = token_row_block.astype(jnp.float32) + attn_out
    normed = layer_norm(first_sum, vector_f32[0], vector_f32[1])
    pre_act = jnp.dot(
        normed.astype(jnp.bfloat16), up_mat, preferred_element_type=jnp.float32
    ) + vector_f32[8:].reshape(-1)
    act_low = jax.nn.gelu(pre_act, approximate=False).astype(jnp.bfloat16)
    second_sum = normed + (
        jnp.dot(act_low, down_mat, preferred_element_type=jnp.float32) + vector_f32[7]
    )
    page_out = (layer_norm(second_sum, vector_f32[2], vector_f32[3]) * page_live[:, None]).astype(
        jnp.bfloat16
    )
    saved_state = (
        query_rows,
        key_rows,
        value_rows,
        left_rows,
        logsum,
        context,
        first_sum,
        pre_act,
        act_low,
        second_sum,
    )
    return (page_out, saved_state)


def backward_page(weights, token_row_block, box_rows, page_length, upstream, saved_state):
    attention_matrices, up_mat, down_mat, vector_rows = weights
    (
        query_rows,
        key_rows,
        value_rows,
        left_rows,
        logsum,
        context,
        first_sum,
        pre_act,
        act_low,
        second_sum,
    ) = saved_state
    row_count, model_width = token_row_block.shape
    vector_f32 = vector_rows.astype(jnp.float32)
    page_live = jnp.arange(row_count) < page_length
    sine_rows, cosine_rows = box_tables(box_rows, model_width)
    encoded = encode(sine_rows, cosine_rows).astype(jnp.bfloat16)
    out_grad = upstream.astype(jnp.float32) * page_live[:, None]
    _, pull_second = jax.vjp(layer_norm, second_sum, vector_f32[2], vector_f32[3])
    second_grad, gain_two, shift_two = pull_second(out_grad)
    ffn_grad = second_grad.astype(jnp.bfloat16)
    down_grad = contract(act_low, ffn_grad, 0, 0)
    act_grad = contract(ffn_grad, down_mat, 1, 1)
    _, pull_gelu = jax.vjp(partial(jax.nn.gelu, approximate=False), pre_act)
    pre_grad = pull_gelu(act_grad)[0].astype(jnp.bfloat16)
    normed, pull_first = jax.vjp(layer_norm, first_sum, vector_f32[0], vector_f32[1])
    up_grad = contract(normed.astype(jnp.bfloat16), pre_grad, 0, 0)
    normed_grad = contract(pre_grad, up_mat, 1, 1) + second_grad
    first_grad, gain_one, shift_one = pull_first(normed_grad)
    attn_grad = first_grad.astype(jnp.bfloat16)
    out_mat_grad = contract(context, attn_grad, 0, 0)
    context_grad = (
        contract(attn_grad, attention_matrices[3], 1, 1)
        .astype(jnp.bfloat16)
        .reshape(row_count, HEADS, HEAD_DIM)
    )
    score_rows = scores(query_rows, key_rows, left_rows, encoded, page_live)
    prob_rows = jnp.exp(score_rows - logsum)
    value_grad = jnp.einsum(
        "hij,ihd->jhd",
        prob_rows.astype(jnp.bfloat16),
        context_grad,
        preferred_element_type=jnp.float32,
    ).astype(jnp.bfloat16)
    prob_grad = jnp.einsum(
        "ihd,jhd->hij", context_grad, value_rows, preferred_element_type=jnp.float32
    )
    score_grad = (
        prob_rows * (prob_grad - jnp.sum(prob_rows * prob_grad, axis=-1, keepdims=True))
    ).astype(jnp.bfloat16)
    score_scale = HEAD_DIM ** (-0.5)
    left_grad = (
        jnp.einsum("hij,je->hie", score_grad, encoded, preferred_element_type=jnp.float32)
        * score_scale
    )
    table_grad = rotate(left_grad, sine_rows, cosine_rows).astype(jnp.bfloat16)
    rel_heads = attention_matrices[4].reshape(model_width, HEADS, HEAD_DIM)
    rel_grad = jnp.einsum(
        "hie,ihd->ehd", table_grad, query_rows, preferred_element_type=jnp.float32
    ).reshape(model_width, model_width)
    query_grad = (
        jnp.einsum("hij,jhd->ihd", score_grad, key_rows, preferred_element_type=jnp.float32)
        * score_scale
    )
    query_grad = query_grad + jnp.einsum(
        "hie,ehd->ihd", table_grad, rel_heads, preferred_element_type=jnp.float32
    )
    key_grad = (
        jnp.einsum("hij,ihd->jhd", score_grad, query_rows, preferred_element_type=jnp.float32)
        * score_scale
    )
    stacked_layers = jnp.stack(
        [
            query_grad.astype(jnp.bfloat16).reshape(row_count, model_width),
            key_grad.astype(jnp.bfloat16).reshape(row_count, model_width),
            value_grad.reshape(row_count, model_width),
        ]
    )
    projection_gradient = jnp.einsum(
        "cg,yca->yga", token_row_block, stacked_layers, preferred_element_type=jnp.float32
    )
    token_grad = first_grad + jnp.einsum(
        "skl,scl->kc", stacked_layers, attention_matrices[:3], preferred_element_type=jnp.float32
    )
    column_sums = jnp.sum(stacked_layers.astype(jnp.float32), axis=1)
    attn_grads = jnp.concatenate([projection_gradient, out_mat_grad[None], rel_grad[None]], axis=0)
    small_rows = jnp.stack(
        [
            gain_one,
            shift_one,
            gain_two,
            shift_two,
            column_sums[0],
            column_sums[2],
            jnp.sum(attn_grad.astype(jnp.float32), axis=0),
            jnp.sum(ffn_grad.astype(jnp.float32), axis=0),
        ]
    )
    up_bias_rows = jnp.sum(pre_grad.astype(jnp.float32), axis=0).reshape(-1, model_width)
    vector_grad = jnp.concatenate([small_rows, up_bias_rows], axis=0)
    return (token_grad, (attn_grads, up_grad, down_grad, vector_grad))


def adam_update(weight, first, second, grad, rate, decay_weight):
    first_new = DECAY * first + (1.0 - DECAY) * grad
    second_new = DECAY * second + (1.0 - DECAY) * grad * grad
    correction = 1.0 - DECAY**STEP
    direction = first_new / correction / (jnp.sqrt(second_new / correction) + EPS_ADAM)
    return (weight - rate * (direction + decay_weight * weight), first_new, second_new)


AXES = ("fsdp", "rep")
ORDERS = ((8, 4, 2, 1), (8, 4, 1, 2))
PLANE_FIRST = ((1, 8, 4, 2), (2, 8, 4, 1))
DEPTH_FIRST = ((8, 2, 1, 4), (8, 1, 2, 4))
PLAIN_AT, DEPTH_AT, PLANE_AT = 32, 96, 64
LOW = jnp.bfloat16
WIDE = jnp.float32
CHUNK = 256
SLAB = 128
FEED_VMEM_BYTES = 58 * 1024 * 1024
ATTN_VMEM_BYTES = 28 * 1024 * 1024
CORE_AT, LENGTH_AT = 128, 129


def mask_table(order):
    masks = [0]
    for bit in order:
        masks = masks + [bit ^ mask for mask in masks]
    return masks


CORE_PAIRS = [(chip * 2 + core, chip * 2 + 1 - core) for chip in range(16) for core in range(2)]


def place_of(mask, order):
    place = 0
    for bit_at, bit in enumerate(order):
        place = place + jnp.where((mask & bit) != 0, 1 << bit_at, 0)
    return place


def block_scalars(chip, core, length):
    rows, lane = [], jnp.arange(16, dtype=jnp.int32)
    blocks = [jnp.array(mask_table(order), jnp.int32) ^ chip for order in ORDERS]
    places = [place_of(lane ^ chip, order) for order in ORDERS]
    plane_blocks = [jnp.array(mask_table(order), jnp.int32) ^ chip for order in PLANE_FIRST]
    depth_places = [place_of(lane ^ chip, order) for order in DEPTH_FIRST]
    for pair in (blocks, places, plane_blocks, depth_places):
        rows.append(jnp.where(core == 0, pair[0], pair[1]))
        rows.append(jnp.where(core == 0, pair[1], pair[0]))
    last = jnp.where(lane == 0, core, jnp.where(lane == 1, length, 0))
    return jnp.stack(rows + [last]).astype(jnp.int32).reshape(-1)


def after(value, *others):
    return lax.optimization_barrier((value, *others))[0]


def sync(*values):
    return lax.optimization_barrier(values)


def swap_cores(block):
    return lax.ppermute(block, AXES, CORE_PAIRS)


def hop(held, step, orders=ORDERS):
    pairs = [
        (chip * 2 + core, (chip ^ orders[core][step]) * 2 + core)
        for chip in range(16)
        for core in range(2)
    ]
    return lax.ppermute(held, AXES, pairs)


def join(held, arrived):
    return jnp.concatenate([held, arrived], axis=0)


def add_up(terms):
    total_sum = terms[0].astype(WIDE)
    for term in terms[1:]:
        total_sum = total_sum + term.astype(WIDE)
    return total_sum.astype(terms[0].dtype)


def halve(terms):
    half = terms[0].shape[0] // 2
    return [term[:half] for term in terms], add_up([term[half:] for term in terms])


def by_half(core, sums):
    mine, other = sums
    first = jnp.where(core == 0, mine, other)
    second = jnp.where(core == 0, other, mine)
    return first.astype(WIDE), second.astype(WIDE)


def dot(left_op, right_op, left_dim, right_dim):
    return lax.dot_general(
        left_op,
        right_op,
        (((left_dim,), (right_dim,)), ((), ())),
        preferred_element_type=WIDE,
    )


def each(count, size, body, flat=False):
    def step(index, carry):
        body(pl.ds(pl.multiple_of(index * size, size), size))
        return carry

    if flat:
        for index in range(count // size):
            body(pl.ds(index * size, size))
    else:
        lax.fori_loop(0, count // size, step, 0)


def block_at(index):
    return pl.ds(pl.multiple_of(index * 48, 16), 48)


def turned(block):
    return (block & 3) | ((block & 4) << 1) | ((block & 8) >> 1)


def start_copies(make, count):
    def start(place, carry):
        for copy in make(place):
            copy.start()
        return carry

    lax.fori_loop(0, count, start, 0)


def wait_for(buffer, sem):
    pltpu.make_async_copy(buffer, buffer, sem).wait()


def sources(scal, pieces):
    core = scal[CORE_AT]
    bases = (0, 8, 16, 24)
    halves = (core, core, 1 - core, 1 - core)
    return [(piece, base, half) for piece, base, half in zip(pieces, bases, halves, strict=True)]


def attn_copies(scal, pieces, lanes, mats, spot, sem, place):
    copies = []
    for source, base, half in sources(scal, pieces):
        block = scal[base + place]
        for part in range(2):
            row = block if part == 0 else jnp.where(half == 1, turned(block), block)
            copies.append(
                pltpu.make_async_copy(
                    source.at[place, pl.ds(48 * part, 48), lanes],
                    mats.at[2 * half + part, block_at(row), spot],
                    sem,
                )
            )
    return copies


def head_masks(dtype):
    lane = lax.broadcasted_iota(jnp.int32, (1, 128), 1)
    first = jnp.where(lane < 64, 1.0, 0.0)
    return (first.astype(dtype), (1.0 - first).astype(dtype))


def attend_kernel(
    group,
    scal,
    tokens,
    vec,
    sines,
    cosines,
    encoded,
    *refs,
):
    pieces = refs[:4]
    refs = refs[4:] if group == 0 else refs[9:]
    (
    q_out,
    k_out,
    v_out,
    ctx_out,
    prob_out,
    mats,
    right,
    sem,
    ) = refs
    pair = pl.program_id(0)
    width = tokens.shape[1]
    rows = tokens.shape[0]

    @pl.when(pair == 0)
    def _():
        cols = mats.shape[2]
        lane_at = pl.ds(group * cols, cols)
        start_copies(partial(attn_copies, scal, pieces, lane_at, mats, pl.ds(0, cols), sem), 8)
        wait_for(mats, sem)
        right[:, :width] = encoded[...]

        def project(at):
            x = tokens[at, :]
            q_out[at, :] = (dot(x, mats[0], 1, 0) + vec[4:5, :]).astype(LOW)
            k_out[at, :] = dot(x, mats[1], 1, 0).astype(LOW)
            v_out[at, :] = (dot(x, mats[2], 1, 0) + vec[5:6, :]).astype(LOW)

        each(rows, CHUNK, project)

    lanes = pl.ds(pl.multiple_of(pair * 128, 128), 128)
    right[:, width:] = k_out[:, lanes]
    rel = mats[3, :, lanes]
    live = lax.broadcasted_iota(jnp.int32, (1, rows), 1) < scal[LENGTH_AT]
    half = width // 2

    def score(at):
        q_pair = q_out[at, :] if q_out.shape[1] == 128 else q_out[at, lanes]
        sin, cos = sines[at, :], cosines[at, :]
        mixed = []
        for head, mask in enumerate(head_masks(LOW)):
            q_head = q_pair * mask
            table = dot(q_head, rel, 1, 1)
            us, uc = table[:, :half], table[:, half:]
            left = jnp.concatenate(
                [(uc * sin - us * cos).astype(LOW), (us * sin + uc * cos).astype(LOW), q_head], axis=1
            )
            s = dot(left, right[...], 1, 1) * HEAD_DIM ** (-0.5)
            s = jnp.where(live, s, MASK_FILL)
            top = jnp.max(s, axis=-1, keepdims=True)
            e = jnp.exp(s - top)
            prob = (e * (1.0 / jnp.sum(e, axis=-1, keepdims=True))).astype(LOW)
            prob_out[head, at, :] = prob
            mixed.append(dot(prob, v_out[:, lanes], 1, 0))
        masks = head_masks(WIDE)
        ctx_out[at, :] = (mixed[0] * masks[0] + mixed[1] * masks[1]).astype(LOW)

    each(rows, rows, score, True)


def any_space():
    return pl.BlockSpec(memory_space=pl.ANY)


def whole(shape):
    return pl.BlockSpec(shape, lambda *_: (0,) * len(shape))


def attend(group, scal, tokens, vec, sines, cosines, encoded, pieces, before):
    rows, width = tokens.shape
    pairs, cols = PAIRS, 128 * PAIRS
    low = jax.ShapeDtypeStruct((rows, width), LOW)
    return pl.pallas_call(
        partial(attend_kernel, group),
        out_shape=(low, low, low, low, jax.ShapeDtypeStruct((width // 64, rows, rows), LOW)),
        grid_spec=pltpu.PrefetchScalarGridSpec(
            num_scalar_prefetch=1,
            grid=(pairs,),
            in_specs=[
                whole((rows, width)),
                pl.BlockSpec((vec.shape[0], cols), lambda *_: (0, group)),
                whole((rows, width // 2)),
                whole((rows, width // 2)),
                whole((rows, width)),
            ]
            + [any_space()] * (4 + len(before)),
            out_specs=[pl.BlockSpec((rows, cols), lambda *_: (0, group))] * 3
            + [
                pl.BlockSpec((rows, 128), lambda p, _: (0, group * pairs + p)),
                pl.BlockSpec((2, rows, rows), lambda p, _: (group * pairs + p, 0, 0)),
            ],
            scratch_shapes=[
                pltpu.VMEM((4, width, cols), LOW),
                pltpu.VMEM((rows, width + 128), LOW),
                pltpu.SemaphoreType.DMA,
            ],
        ),
        compiler_params=pltpu.CompilerParams(
            dimension_semantics=("arbitrary",), vmem_limit_bytes=ATTN_VMEM_BYTES
        ),
        cost_estimate=pl.CostEstimate(
            flops=pairs * 2 * rows * width * 3072, transcendentals=0, bytes_accessed=24 * 1024 * 1024
        ),
        input_output_aliases={10 + at: at for at in range(len(before))},
        name="attend",
    )(scal, tokens, vec, sines, cosines, encoded, *pieces, *before)


CDF_POLY = (
    -0.020695917308330536,
    0.09534552693367004,
    -0.15029412508010864,
    0.07120334357023239,
    -0.011180647648870945,
    0.05997580662369728,
    0.08762594312429428,
    0.11413583159446716,
    0.12694157660007477,
    0.12694266438484192,
)
CDF_SLOPE = 0.45 / math.sqrt(2.0)


def gelu_pair(x):
    size = jnp.abs(x)
    t = 1.0 / (1.0 + CDF_SLOPE * size)
    bell = jnp.exp2(x * x * (-0.5 / math.log(2.0)))
    poly = CDF_POLY[0]
    for value in CDF_POLY[1:]:
        poly = poly * t + value
    tail = poly * t * bell
    cdf = jnp.where(x < 0.0, tail, 1.0 - tail)
    return x * cdf, cdf + x * bell * (1.0 / math.sqrt(2.0 * math.pi))


def moments(z):
    center = z - jnp.mean(z, axis=-1, keepdims=True)
    r = lax.rsqrt(jnp.mean(center * center, axis=-1, keepdims=True) + EPS_NORM)
    return center * r, r


def norm_back(grad, xh, r, gain):
    dxh = grad * gain
    return r * (
        dxh - jnp.mean(dxh, axis=-1, keepdims=True) - xh * jnp.mean(dxh * xh, axis=-1, keepdims=True)
    )


def total(values):
    return jnp.sum(values, axis=0, keepdims=True)


def out_copies(scal, pieces, out_mat, sem, place):
    return [
        pltpu.make_async_copy(
            source.at[place, :, pl.ds(0, 384)],
            out_mat.at[block_at(scal[base + place]), pl.ds(pl.multiple_of(half * 384, 128), 384)],
            sem,
        )
        for source, base, half in sources(scal, pieces)
    ]


def down_copies(scal, pieces, down_mat, sem, place):
    return [
        pltpu.make_async_copy(
            source.at[place],
            down_mat.at[pl.ds(pl.multiple_of(scal[PLANE_AT + base + place] * 192 + half * 96, 32), 96)],
            sem,
        )
        for source, base, half in sources(scal, pieces)
    ]


def per_core(scal, body):
    for core in range(2):

        @pl.when(scal[CORE_AT] == core)
        def _(core=core):
            body(core)


def send_block(scal, source, outs, side, block, cut, sem, table=PLAIN_AT):
    place = scal[table + 16 * side + block]
    if side == 0:
        pltpu.make_async_copy(source, cut(outs[0], place), sem).start()
        return
    for part in range(2):

        @pl.when(place // 8 == part)
        def _(part=part):
            pltpu.make_async_copy(source, cut(outs[1 + part], lax.rem(place, 8)), sem).start()


def block_shapes(rows, cols):
    return tuple(jax.ShapeDtypeStruct((count, rows, cols), LOW) for count in (16, 8, 8))


def feed_kernel(*refs):
    scal, tokens, cot, vec = refs[:4]
    ctx = refs[4]
    two_pieces, three_pieces = refs[5:9], refs[9:13]
    page_out, dh1_out, dctx_out, *outs = refs[13:22]
    two_outs, three_outs = outs[:3], outs[3:]
    (
        out_mat,
        up_mat,
        down_mat,
        norm_low,
        xh1,
        r1,
        act,
        slope,
        held,
        df,
        dpre,
        dattn,
        g_out,
        g_up,
        g_down,
        vec_out,
        vec_low,
        sem_in,
        sem_up,
        sem_down,
        sem_out,
        sem_page,
        sem_rows,
    ) = refs[22:]
    step = pl.program_id(0)
    rows, width = tokens.shape
    length = scal[LENGTH_AT]

    @pl.when(step == 0)
    def _():
        start_copies(partial(out_copies, scal, two_pieces, out_mat, sem_in.at[0]), 8)

        def fetch(core):
            for unit in range(4):
                near = 0 if unit // 2 == core else 2

                def start(place, carry, unit=unit, near=near):
                    for index in (near, near + 1):
                        pltpu.make_async_copy(
                            two_pieces[index].at[place, :, pl.ds(384 + 768 * (unit % 2), 768)],
                            up_mat.at[unit, block_at(scal[8 * index + place])],
                            sem_in.at[1 + unit],
                        ).start()
                    return carry

                lax.fori_loop(0, 8, start, 0)

        per_core(scal, fetch)
        start_copies(partial(down_copies, scal, three_pieces, down_mat, sem_in.at[5]), 8)
        wait_for(out_mat, sem_in.at[0])
        vec_out[...] = jnp.zeros_like(vec_out)
        def first(at):
            attn = dot(ctx[at, :], out_mat[...], 1, 0) + vec[6:7, :]
            hat, r = moments(tokens[at, :].astype(WIDE) + attn)
            normed = hat * vec[0:1, :] + vec[1:2, :]
            xh1[at, :] = hat
            r1[at, :] = jnp.broadcast_to(r, (r.shape[0], 128))
            norm_low[at, :] = normed.astype(LOW)
            held[at, :] = normed + vec[7:8, :]

        each(rows, CHUNK, first)

    @pl.when(step < 4)
    def _():
        bias = vec[pl.ds(8 + step, 1), :]
        down_at = pl.ds(pl.multiple_of(step * width, width), width)
        spots = [pl.ds(CHUNK * index, CHUNK) for index in range(rows // CHUNK)]

        wait_for(up_mat.at[step], sem_in.at[1 + step])

        def front(at):
            return dot(norm_low[at, :], up_mat[step], 1, 0) + bias

        pre = front(spots[0])

        @pl.when(step == 0)
        def _():
            wait_for(down_mat, sem_in.at[5])

        for index, at in enumerate(spots):
            ahead = front(spots[index + 1]) if index + 1 < len(spots) else None
            value, grad = gelu_pair(pre)
            low = value.astype(LOW)
            act[step, at, :] = low
            slope[step, at, :] = grad
            held[at, :] += dot(low, down_mat[down_at, :], 1, 0)
            pre = ahead

    @pl.when(step == 3)
    def _():
        def second(at):
            hat, r = moments(held[at, :])
            place = lax.broadcasted_iota(jnp.int32, (SLAB, 1), 0) + at.start
            live = jnp.where(place < length, 1.0, 0.0)
            dattn[at, :] = ((hat * vec[2:3, :] + vec[3:4, :]) * live).astype(LOW)
            dy = cot[at, :].astype(WIDE) * live
            vec_out[2:3, :] += total(dy * hat)
            vec_out[3:4, :] += total(dy)
            dh2 = norm_back(dy, hat, r, vec[2:3, :])
            low = dh2.astype(LOW)
            df[at, :] = low
            vec_out[7:8, :] += total(low.astype(WIDE))
            held[at, :] = dh2

        each(rows, SLAB, second)
        pltpu.make_async_copy(dattn, page_out, sem_page).start()

    def send_up(slot, unit):
        at = pl.ds(pl.multiple_of(384 + 768 * lax.rem(unit, 2), 128), 768)
        for side in range(2):

            @pl.when((unit // 2 == scal[CORE_AT]) == (side == 0))
            def _(side=side):
                def body(block, carry):
                    send_block(
                        scal,
                        g_up.at[slot, block_at(block)],
                        two_outs,
                        side,
                        block,
                        lambda ref, place: ref.at[place, :, at],
                        sem_up.at[slot],
                    )
                    return carry

                lax.fori_loop(0, 16, body, 0)

    def send_down(slot, unit):
        def body(core):
            for part in range(8):
                send_block(
                    scal,
                    g_down.at[slot, pl.ds(96 * part, 96)],
                    three_outs,
                    (part % 2) ^ core,
                    4 * unit + part // 2,
                    lambda ref, place: ref.at[place, pl.ds(0, 96)],
                    sem_down.at[slot],
                    DEPTH_AT,
                )

        per_core(scal, body)

    def send_out():
        def on(core):
            def body(block, carry):
                for half in range(2):
                    send_block(
                        scal,
                        g_out.at[block_at(block), pl.ds(384 * half, 384)],
                        two_outs,
                        half ^ core,
                        block,
                        lambda ref, place: ref.at[place, :, pl.ds(0, 384)],
                        sem_out,
                    )
                return carry

            lax.fori_loop(0, 16, body, 0)

        per_core(scal, on)

    @pl.when(step >= 4)
    def _():
        unit = step - 4
        slot = lax.rem(unit, 2)
        down_at = pl.ds(pl.multiple_of(unit * width, width), width)

        @pl.when(unit >= 2)
        def _():
            wait_for(g_up.at[slot], sem_up.at[slot])
            wait_for(g_down.at[slot], sem_down.at[slot])

        def backward(at):
            grad = dot(df[at, :], down_mat[down_at, :], 1, 1) * slope[unit, at, :]
            low = grad.astype(LOW)
            dpre[at, :] = low
            vec_out[pl.ds(8 + unit, 1), :] += total(low.astype(WIDE))
            held[at, :] += dot(low, up_mat[unit], 1, 1)

        each(rows, rows, backward, True)

        def weights(at):
            g_down[slot, at, :] = dot(act[unit, :, at], df[...], 0, 0).astype(LOW)
            g_up[slot, at, :] = dot(norm_low[:, at], dpre[...], 0, 0).astype(LOW)

        each(width, width, weights, True)
        send_down(slot, unit)
        send_up(slot, unit)

    @pl.when(step == 7)
    def _():
        wait_for(dattn, sem_page)

        def last(at):
            grad, hat = held[at, :], xh1[at, :]
            vec_out[0:1, :] += total(grad * hat)
            vec_out[1:2, :] += total(grad)
            dh1 = norm_back(grad, hat, r1[at, :1], vec[0:1, :])
            held[at, :] = dh1
            pltpu.make_async_copy(held.at[at], dh1_out.at[at], sem_rows.at[0]).start()
            low = dh1.astype(LOW)
            dattn[at, :] = low
            vec_out[6:7, :] += total(low.astype(WIDE))

        each(rows, SLAB, last)
        vec_low[...] = jnp.zeros_like(vec_low)
        vec_low[0, 0:4, :] = vec_out[0:4, :].astype(LOW)
        vec_low[0, 4:5, :] = vec_out[6:7, :].astype(LOW)
        vec_low[1, 0:5, :] = vec_out[7:12, :].astype(LOW)

        def send_vectors(core):
            def body(block, carry):
                for half in range(2):
                    send_block(
                        scal,
                        vec_low.at[half],
                        three_outs,
                        half ^ core,
                        block,
                        lambda ref, place: ref.at[place, pl.ds(96, 8)],
                        sem_page,
                        DEPTH_AT,
                    )
                return carry

            lax.fori_loop(0, 16, body, 0)

        per_core(scal, send_vectors)

        def weights(at):
            g_out[at, :] = dot(ctx[:, at], dattn[...], 0, 0).astype(LOW)

        each(width, CHUNK, weights)
        send_out()

        def context(at):
            df[at, :] = dot(dattn[at, :], out_mat[...], 1, 1).astype(LOW)
            pltpu.make_async_copy(df.at[at], dctx_out.at[at], sem_rows.at[1]).start()

        each(rows, CHUNK, context)
        for slot in range(2):
            wait_for(g_up.at[slot], sem_up.at[slot])
            wait_for(g_down.at[slot], sem_down.at[slot])
        wait_for(g_out, sem_out)
        wait_for(held, sem_rows.at[0])
        wait_for(df, sem_rows.at[1])
        lax.fori_loop(0, 16, lambda _, carry: (wait_for(vec_low, sem_page), carry)[1], 0)


def feed(scal, tokens, cot, vec, ctx, two, three):
    rows, width = tokens.shape
    return pl.pallas_call(
        feed_kernel,
        out_shape=(
            jax.ShapeDtypeStruct((rows, width), LOW),
            jax.ShapeDtypeStruct((rows, width), WIDE),
            jax.ShapeDtypeStruct((rows, width), LOW),
        )
        + block_shapes(48, 384 + 2 * width)
        + block_shapes(104, width),
        grid_spec=pltpu.PrefetchScalarGridSpec(
            num_scalar_prefetch=1,
            grid=(8,),
            in_specs=[whole((rows, width)), whole((rows, width)), whole((16, width))]
            + [whole((rows, width))]
            + [any_space()] * 8,
            out_specs=[any_space()] * 9,
            scratch_shapes=[
                pltpu.VMEM((width, width), LOW),
                pltpu.VMEM((4, width, width), LOW),
                pltpu.VMEM((4 * width, width), LOW),
                pltpu.VMEM((rows, width), LOW),
                pltpu.VMEM((rows, width), WIDE),
                pltpu.VMEM((rows, 128), WIDE),
                pltpu.VMEM((4, rows, width), LOW),
                pltpu.VMEM((4, rows, width), WIDE),
                pltpu.VMEM((rows, width), WIDE),
                pltpu.VMEM((rows, width), LOW),
                pltpu.VMEM((rows, width), LOW),
                pltpu.VMEM((rows, width), LOW),
                pltpu.VMEM((width, width), LOW),
                pltpu.VMEM((2, width, width), LOW),
                pltpu.VMEM((2, width, width), LOW),
                pltpu.VMEM((16, width), WIDE),
                pltpu.VMEM((2, 8, width), LOW),
                pltpu.SemaphoreType.DMA((6,)),
                pltpu.SemaphoreType.DMA((2,)),
                pltpu.SemaphoreType.DMA((2,)),
                pltpu.SemaphoreType.DMA,
                pltpu.SemaphoreType.DMA,
                pltpu.SemaphoreType.DMA((2,)),
            ],
        ),
        compiler_params=pltpu.CompilerParams(
            dimension_semantics=("arbitrary",), vmem_limit_bytes=FEED_VMEM_BYTES
        ),
        cost_estimate=pl.CostEstimate(
            flops=2 * rows * width * width * 27, transcendentals=0, bytes_accessed=32 * 1024 * 1024
        ),
        name="feed",
    )(scal, tokens, cot, vec, ctx, *two, *three)


def split_kernel(scal, attn, up, down, two_out, three_out):
    for core in range(2):

        @pl.when(scal[0] == core)
        def _(core=core):
            two_out[0, :, :384] = attn[3, :, 384 * core : 384 * (core + 1)].astype(LOW)
            two_out[0, :, 384:] = up[:, 1536 * core : 1536 * (core + 1)].astype(LOW)
            three_out[0] = down[96 * core : 96 * (core + 1), :].astype(LOW)


def split_weights(core, attn, up, down):
    width = attn.shape[2]
    shapes = ((1, 48, 384 + 2 * width), (1, 96, width))
    return pl.pallas_call(
        split_kernel,
        out_shape=tuple(jax.ShapeDtypeStruct(shape, LOW) for shape in shapes),
        grid_spec=pltpu.PrefetchScalarGridSpec(
            num_scalar_prefetch=1,
            grid=(1,),
            in_specs=[whole(attn.shape), whole(up.shape), whole(down.shape)],
            out_specs=[whole(shape) for shape in shapes],
        ),
        cost_estimate=pl.CostEstimate(flops=0, transcendentals=0, bytes_accessed=3 * 1024 * 1024),
        name="split_weights",
    )(core, attn, up, down)


def unattend_kernel(
    group,
    scal,
    tokens,
    sines,
    cosines,
    encoded,
    q_in,
    k_in,
    v_in,
    dctx_in,
    prob,
    *refs,
):
    pieces = refs[:4]
    refs = refs[4:] if group != 1 else refs[7:]
    dq_out, dk_out, dv_out = refs[:3]
    outs = refs[3:6]
    (
    mats,
    right,
    ds_low,
    du_low,
    q_heads,
    d_heads,
    grads,
    sums,
    sem,
    sem_out,
    sem_sums,
    ) = refs[6:]
    pair = pl.program_id(0)
    rows, width = tokens.shape
    half = width // 2
    scale = HEAD_DIM ** (-0.5)

    @pl.when(pair == 0)
    def _():
        cols = mats.shape[2]
        lane_at = pl.ds(group * cols, cols)
        start_copies(partial(attn_copies, scal, pieces, lane_at, mats, pl.ds(0, cols), sem), 8)
        wait_for(mats, sem)
        right[:, :width] = encoded[...]

    lanes = pl.ds(pl.multiple_of(pair * 128, 128), 128)
    right[:, width:] = k_in[...]
    rel = mats[3, :, lanes]
    low_masks, wide_masks = head_masks(LOW), head_masks(WIDE)

    def score(at):
        sin, cos = sines[at, :], cosines[at, :]
        dq = None
        for head in range(2):
            spot = pl.ds(pl.multiple_of(head * rows + at.start, at.size), at.size)
            dctx = dctx_in[at, :] * low_masks[head]
            d_heads[spot, :] = dctx
            q_heads[spot, :] = q_in[at, :] * low_masks[head]
            p = prob[head, at, :].astype(WIDE)
            dp = dot(dctx, v_in[...], 1, 1)
            ds = (p * (dp - jnp.sum(p * dp, axis=-1, keepdims=True))).astype(LOW)
            ds_low[spot, :] = ds
            dl = dot(ds, right[...], 1, 0) * scale
            ls, lc = dl[:, :half], dl[:, half:width]
            du = jnp.concatenate(
                [(lc * sin - ls * cos).astype(LOW), (ls * sin + lc * cos).astype(LOW)], axis=1
            )
            du_low[spot, :] = du
            part = (dl[:, width:] + dot(du, rel, 1, 0)) * wide_masks[head]
            dq = part if dq is None else dq + part
        dq_out[at, lanes] = dq.astype(LOW)

    each(rows, rows, score, True)
    dv_out[:, lanes] = dot(prob[...].reshape(2 * rows, rows), d_heads[...], 0, 0).astype(LOW)
    dk_out[:, lanes] = (dot(ds_low[...], q_heads[...], 0, 0) * scale).astype(LOW)
    grads[3, :, lanes] = dot(du_low[...], q_heads[...], 0, 0).astype(LOW)

    @pl.when(pair == pl.num_programs(0) - 1)
    def _():
        def weights(at):
            x = tokens[:, at]
            grads[0, at, :] = dot(x, dq_out[...], 0, 0).astype(LOW)
            grads[1, at, :] = dot(x, dk_out[...], 0, 0).astype(LOW)
            grads[2, at, :] = dot(x, dv_out[...], 0, 0).astype(LOW)

        each(width, CHUNK, weights)

        spot = pl.ds(mats.shape[2] if group == 1 else 0, mats.shape[2])
        sums[...] = jnp.zeros_like(sums)
        sums[0, 0:1, :] = total(dq_out[...].astype(WIDE)).astype(LOW)
        sums[1, 0:1, :] = total(dv_out[...].astype(WIDE)).astype(LOW)

        def on(core):
            def body(block, carry):
                for slot in range(4):
                    row = turned(block) if slot == 3 else block
                    at = pl.ds(48 * (slot % 2), 48)
                    send_block(
                        scal,
                        grads.at[slot, block_at(row)],
                        outs,
                        (slot // 2) ^ core,
                        block,
                        lambda ref, place, at=at: ref.at[place, at, spot],
                        sem_out,
                    )
                for half in range(2):
                    send_block(
                        scal,
                        sums.at[half],
                        outs,
                        half ^ core,
                        block,
                        lambda ref, place: ref.at[place, pl.ds(96, 8), spot],
                        sem_sums,
                    )
                return carry

            lax.fori_loop(0, 16, body, 0)

        per_core(scal, on)
        wait_for(grads, sem_out)
        lax.fori_loop(0, 16, lambda _, carry: (wait_for(sums, sem_sums), carry)[1], 0)


def unattend(group, scal, tokens, sines, cosines, encoded, q, k, v, dctx, prob, pieces, blocks):
    rows, width = tokens.shape
    pairs, cols = BACK_PAIRS, 128 * BACK_PAIRS
    low = jax.ShapeDtypeStruct((rows, cols), LOW)
    lane_block = pl.BlockSpec((rows, 128), lambda p, _: (0, group * pairs + p))
    return pl.pallas_call(
        partial(unattend_kernel, group),
        out_shape=(low, low, low) + block_shapes(104, 2 * cols if group < 2 else cols),
        grid_spec=pltpu.PrefetchScalarGridSpec(
            num_scalar_prefetch=1,
            grid=(pairs,),
            in_specs=[
                whole((rows, width)),
                whole((rows, half_of(width))),
                whole((rows, half_of(width))),
                whole((rows, width)),
                lane_block,
                lane_block,
                lane_block,
                lane_block,
                pl.BlockSpec((2, rows, rows), lambda p, _: (group * pairs + p, 0, 0)),
            ]
            + [any_space()] * (4 + len(blocks)),
            out_specs=[whole((rows, cols))] * 3 + [any_space()] * 3,
            scratch_shapes=[
                pltpu.VMEM((4, width, cols), LOW),
                pltpu.VMEM((rows, width + 128), LOW),
                pltpu.VMEM((2 * rows, rows), LOW),
                pltpu.VMEM((2 * rows, width), LOW),
                pltpu.VMEM((2 * rows, 128), LOW),
                pltpu.VMEM((2 * rows, 128), LOW),
                pltpu.VMEM((4, width, cols), LOW),
                pltpu.VMEM((2, 8, cols), LOW),
                pltpu.SemaphoreType.DMA,
                pltpu.SemaphoreType.DMA,
                pltpu.SemaphoreType.DMA,
            ],
        ),
        compiler_params=pltpu.CompilerParams(
            dimension_semantics=("arbitrary",), vmem_limit_bytes=ATTN_VMEM_BYTES
        ),
        cost_estimate=pl.CostEstimate(
            flops=pairs * 2 * rows * width * 5000, transcendentals=0, bytes_accessed=24 * 1024 * 1024
        ),
        input_output_aliases={14 + at: 3 + at for at in range(len(blocks))},
        name="unattend",
    )(scal, tokens, sines, cosines, encoded, q, k, v, dctx, prob, *pieces, *blocks)


def half_of(width):
    return width // 2


def input_grad_kernel(scal, dh1, *refs):
    parts, pieces = refs[: 3 * BACK_GROUPS], refs[3 * BACK_GROUPS : 3 * BACK_GROUPS + 4]
    out, mats, sem = refs[3 * BACK_GROUPS + 4 :]
    rows, width = dh1.shape
    at = pl.ds(0, width)
    start_copies(partial(attn_copies, scal, pieces, at, mats, at, sem), 8)
    wait_for(mats, sem)

    def rows_of(at):
        grad = dh1[at, :]
        for slot in range(3):
            left = jnp.concatenate([parts[3 * g + slot][at, :] for g in range(BACK_GROUPS)], axis=1)
            grad = grad + dot(left, mats[slot], 1, 1)
        out[at, :] = grad

    each(rows, CHUNK, rows_of)


def input_grad(scal, dh1, parts, pieces):
    rows, width = dh1.shape
    cols = width // BACK_GROUPS
    return pl.pallas_call(
        input_grad_kernel,
        out_shape=jax.ShapeDtypeStruct((rows, width), WIDE),
        grid_spec=pltpu.PrefetchScalarGridSpec(
            num_scalar_prefetch=1,
            grid=(1,),
            in_specs=[whole((rows, width))]
            + [whole((rows, cols))] * (3 * BACK_GROUPS)
            + [any_space()] * 4,
            out_specs=whole((rows, width)),
            scratch_shapes=[pltpu.VMEM((4, width, width), LOW), pltpu.SemaphoreType.DMA],
        ),
        compiler_params=pltpu.CompilerParams(
            dimension_semantics=("arbitrary",), vmem_limit_bytes=ATTN_VMEM_BYTES
        ),
        cost_estimate=pl.CostEstimate(
            flops=2 * rows * width * width * 3, transcendentals=0, bytes_accessed=10 * 1024 * 1024
        ),
        name="input_grad",
    )(scal, dh1, *parts, *pieces)


PAIRS = 3
BACK_PAIRS = 2
BACK_GROUPS = 3


def local(
    tokens,
    boxes,
    lengths,
    cotangent,
    attn_weight,
    up_weight,
    down_weight,
    vectors,
    attn_first,
    up_first,
    down_first,
    vector_first,
    attn_second,
    up_second,
    down_second,
    vector_second,
):
    chip, core = lax.axis_index("fsdp"), lax.axis_index("rep")
    width = tokens.shape[2]
    cols = width - width // BACK_GROUPS
    first = core == 0
    page = tokens[0]
    same = (ORDERS[0], ORDERS[0])

    near = jnp.where(first, attn_weight[:2], attn_weight[2:5:2]).astype(LOW).reshape(1, 96, width)
    near_far = hop(near, 0)
    core_at = after(core.astype(jnp.int32)[None], near)
    two, three = split_weights(core_at, attn_weight, up_weight, down_weight)
    three_far = hop(three, 0, PLANE_FIRST)
    vec = lax.dynamic_update_slice(
        jnp.zeros((vectors.shape[0], width), LOW),
        after(vectors.astype(LOW), near),
        (jnp.int32(0), chip * vectors.shape[1]),
    )
    scal = block_scalars(chip, core, lengths[0])
    near, near_far, two, vec, scal, place = sync(near, near_far, two, vec, scal, boxes[0])

    near = join(near, near_far)
    near_far = hop(near, 1)
    vec_far = hop(vec, 0, same)
    quarter = width // 4
    frequency = jnp.exp(jnp.arange(quarter).astype(WIDE) * (-math.log(10000.0) / quarter))
    place = place.astype(WIDE)
    angles = jnp.concatenate([place[0][:, None] * frequency, place[1][:, None] * frequency], axis=1)
    sines, cosines = jnp.sin(angles), jnp.cos(angles)
    encoded = jnp.concatenate([sines, cosines], axis=1).astype(LOW)
    near, near_far, vec, vec_far, two, three, three_far, sines, cosines, encoded = sync(
        near, near_far, vec, vec_far, two, three, three_far, sines, cosines, encoded
    )

    near = join(near, near_far)
    near_far = hop(near, 2)
    two_far = hop(two, 0)
    vec = vec + vec_far
    vec_far = hop(vec, 1, same)
    near, near_far, vec, vec_far, two, two_far = sync(near, near_far, vec, vec_far, two, two_far)

    near = join(near, near_far)
    near_far = hop(near, 3)
    near_swap = swap_cores(near)
    vec = vec + vec_far
    vec_far = hop(vec, 2, same)
    two = join(two, two_far)
    two_far = hop(two, 1)
    three = join(three, three_far)
    near_far, near_swap, vec, vec_far, two, two_far, three = sync(
        near_far, near_swap, vec, vec_far, two, two_far, three
    )

    near_far_swap = swap_cores(near_far)
    vec = vec + vec_far
    vec_far = hop(vec, 3, same)
    two = join(two, two_far)
    two_far = hop(two, 2)
    three_far = hop(three, 1, PLANE_FIRST)
    vec, near_far_swap, two, three = sync(vec + vec_far, near_far_swap, two, three)
    vec = jnp.pad(vec.astype(WIDE), ((0, 16 - vec.shape[0]), (0, 0)))
    pieces = (near, near_far, near_swap, near_far_swap)

    def go(group, tick, before):
        return attend(group, after(scal, tick), page, vec, sines, cosines, encoded, pieces, before)

    kept = go(0, two, [])
    two, two_far, three, three_far, *kept = sync(two, two_far, three, three_far, *kept)

    two = join(two, two_far)
    two_far = hop(two, 3)
    three = join(three, three_far)
    three_far = hop(three, 2, PLANE_FIRST)
    two_swap = swap_cores(two)
    kept = go(1, three, kept)
    two_far, two_swap, three, three_far, *kept = sync(two_far, two_swap, three, three_far, *kept)

    two_far_swap = swap_cores(two_far)
    three = join(three, three_far)
    three_far = hop(three, 3, PLANE_FIRST)
    three_swap = swap_cores(three)
    two_pieces = (two, two_far, two_swap, two_far_swap)
    three_pieces = (three, three_far, three_swap, swap_cores(three_far))
    page_out, dh1, dctx, *sent = feed(
        scal, page, cotangent[0], vec, kept[3], two_pieces, three_pieces
    )
    two_sent, three_sent = sent[:3], sent[3:]

    three_swap, two_swap, three_low, two_low, mark = sync(
        swap_cores(three_sent[2]), swap_cores(two_sent[2]), three_sent[1], two_sent[1], scal
    )
    three_high = add_up([three_sent[0][8:], three_swap])
    three_far = hop(three_high, 3, DEPTH_FIRST)
    two_high = add_up([two_sent[0][8:], two_swap])
    two_far = hop(two_high, 3)
    three_low = swap_cores(three_low)
    two_low = swap_cores(two_low)

    def undo(group, tick, blocks):
        return unattend(
            group,
            after(scal, tick),
            page,
            sines,
            cosines,
            encoded,
            *kept[:3],
            dctx,
            kept[4],
            pieces,
            blocks,
        )

    back = [undo(0, mark, [])]
    two_far, three_low, two_low, mark, *one_sent = sync(
        two_far, three_low, two_low, back[0][0], *back[0][3:]
    )

    two_terms, two_high = halve([two_sent[0][:8], two_low, two_far])
    two_far = hop(two_high, 2)
    back.append(undo(1, mark, one_sent))
    two_far, three_far, mark, *one_sent = sync(
        two_far, three_far, back[1][0], *back[1][3:]
    )

    one_swap = swap_cores(one_sent[2])
    three_terms, three_high = halve([three_sent[0][:8], three_low, three_far])
    three_far = hop(three_high, 2, DEPTH_FIRST)
    two_terms, two_high = halve(two_terms + [two_far])
    two_far = hop(two_high, 1)
    one_swap, one_low, mark, three_high, two_high = sync(
        one_swap, one_sent[1], mark, three_high, two_high
    )
    one_high = add_up([one_sent[0][8:], one_swap])
    one_far = hop(one_high, 3)
    one_low = swap_cores(one_low)
    back.append(undo(2, mark, []))
    two_far, three_far, one_far, one_low, *end_sent = sync(
        two_far, three_far, one_far, one_low, *back[2][3:]
    )

    end_swap = swap_cores(end_sent[2])
    one_terms, one_high = halve([one_sent[0][:8], one_low, one_far])
    one_far = hop(one_high, 2)
    three_terms, three_high = halve(three_terms + [three_far])
    three_far = hop(three_high, 1, DEPTH_FIRST)
    two_terms, two_high = halve(two_terms + [two_far])
    two_far = hop(two_high, 0)
    end_swap, end_low, mark, one_high, two_high, three_high = sync(
        end_swap, end_sent[1], scal, one_high, two_high, three_high
    )
    end_high = add_up([end_sent[0][8:], end_swap])
    end_far = hop(end_high, 3)
    end_low = swap_cores(end_low)
    token_grad = input_grad(
        after(mark, end_high), dh1, [part for b in back for part in b[:3]], pieces
    )
    end_far, end_low, one_far, three_far, two_far, token_grad = sync(
        end_far, end_low, one_far, three_far, two_far, token_grad
    )

    end_terms, end_high = halve([end_sent[0][:8], end_low, end_far])
    end_far = hop(end_high, 2)
    one_terms, one_high = halve(one_terms + [one_far])
    one_far = hop(one_high, 1)
    three_terms, three_high = halve(three_terms + [three_far])
    three_far = hop(three_high, 0, DEPTH_FIRST)
    two_mine = add_up(two_terms + [two_far])[0]
    two_other = swap_cores(two_mine)
    end_far, one_far, three_far, two_other = sync(end_far, one_far, three_far, two_other)

    end_terms, end_high = halve(end_terms + [end_far])
    end_far = hop(end_high, 1)
    one_terms, one_high = halve(one_terms + [one_far])
    one_far = hop(one_high, 0)
    three_mine = add_up(three_terms + [three_far])[0]
    three_other = swap_cores(three_mine)
    two_sum = by_half(core, (two_mine, two_other))
    up_sum = jnp.concatenate([two_sum[0][:, 384:], two_sum[1][:, 384:]], axis=1)
    up_next = adam_update(up_weight, up_first, up_second, up_sum, UP_RATE, WEIGHT_DECAY)
    end_far, one_far, three_other, up_new, up_first_new, up_second_new = sync(
        end_far, one_far, three_other, *up_next
    )

    end_terms, end_high = halve(end_terms + [end_far])
    end_far = hop(end_high, 0)
    three_sum = by_half(core, (three_mine, three_other))
    down_next = adam_update(
        down_weight,
        down_first,
        down_second,
        jnp.concatenate([part[:96] for part in three_sum]),
        DOWN_RATE,
        WEIGHT_DECAY,
    )
    one_mine = add_up(one_terms + [one_far])[0]
    end_far, one_mine, down_new, down_first_new, down_second_new = sync(
        end_far, one_mine, *down_next
    )

    one_mine = jnp.concatenate([one_mine, add_up(end_terms + [end_far])[0]], axis=1)
    one_sum = by_half(core, (one_mine, swap_cores(one_mine)))
    vec_grad = jnp.concatenate(
        [
            three_sum[0][96:100],
            one_sum[0][96:97],
            one_sum[1][96:97],
            three_sum[0][100:101],
            three_sum[1][96:101],
        ]
    )
    vec_sum = lax.dynamic_slice(
        vec_grad, (jnp.int32(0), chip * vectors.shape[1]), vectors.shape
    )
    attn_sum = jnp.stack(
        [
            one_sum[0][:48],
            one_sum[0][48:96],
            one_sum[1][:48],
            jnp.concatenate([two_sum[0][:, :384], two_sum[1][:, :384]], axis=1),
            one_sum[1][48:96],
        ]
    )
    layer_out, token_grad = page_out[None], token_grad[None]
    attn_rates = jnp.array(ATTN_RATES, jnp.float32)[:, None, None]
    attn_new, attn_first_new, attn_second_new = adam_update(
        attn_weight, attn_first, attn_second, attn_sum, attn_rates, WEIGHT_DECAY
    )
    vectors_new, vector_first_new, vector_second_new = adam_update(
        vectors, vector_first, vector_second, vec_sum, VECTOR_RATE, 0.0
    )
    return (
        layer_out,
        token_grad,
        attn_new,
        up_new,
        down_new,
        vectors_new,
        attn_first_new,
        up_first_new,
        down_first_new,
        vector_first_new,
        attn_second_new,
        up_second_new,
        down_second_new,
        vector_second_new,
        attn_new.astype(jnp.bfloat16),
        up_new.astype(jnp.bfloat16),
        down_new.astype(jnp.bfloat16),
        vectors_new.astype(jnp.bfloat16),
    )


def local_general(
    tokens,
    boxes,
    lengths,
    cotangent,
    attn_weight,
    up_weight,
    down_weight,
    vectors,
    attn_first,
    up_first,
    down_first,
    vector_first,
    attn_second,
    up_second,
    down_second,
    vector_second,
):
    lowered = (
        attn_weight.astype(jnp.bfloat16),
        up_weight.astype(jnp.bfloat16),
        down_weight.astype(jnp.bfloat16),
        vectors.astype(jnp.bfloat16),
    )
    gathered = (
        lax.all_gather(lowered[0], "fsdp", axis=1, tiled=True),
        lax.all_gather(lowered[1], "fsdp", axis=0, tiled=True),
        lax.all_gather(lowered[2], "fsdp", axis=0, tiled=True),
        lax.all_gather(lowered[3], "fsdp", axis=1, tiled=True),
    )

    def forward_step(carry, page):
        token_row_block, box_rows, page_length = page
        return (carry, forward_page(gathered, token_row_block, box_rows, page_length))

    _, (layer_out, saved_all) = lax.scan(forward_step, None, (tokens, boxes, lengths))
    backward_weights = (
        lax.all_gather(lowered[0], "fsdp", axis=1, tiled=True),
        lax.all_gather(lowered[1], "fsdp", axis=0, tiled=True),
        lax.all_gather(lowered[2], "fsdp", axis=0, tiled=True),
        lax.all_gather(lowered[3], "fsdp", axis=1, tiled=True),
    )
    model_width = gathered[0].shape[2]
    ffn_width = gathered[1].shape[1]
    zero_grads = (
        jnp.zeros((5, model_width, model_width), jnp.float32),
        jnp.zeros((model_width, ffn_width), jnp.float32),
        jnp.zeros((ffn_width, model_width), jnp.float32),
        jnp.zeros(gathered[3].shape, jnp.float32),
    )

    def backward_step(totals, page):
        token_row_block, box_rows, page_length, upstream, saved_state = page
        token_grad, grads = backward_page(
            backward_weights, token_row_block, box_rows, page_length, upstream, saved_state
        )
        return (jax.tree.map(jnp.add, totals, grads), token_grad)

    totals, token_grad = lax.scan(
        backward_step, zero_grads, (tokens, boxes, lengths, cotangent, saved_all)
    )
    shards = (
        lax.psum_scatter(totals[0], "fsdp", scatter_dimension=1, tiled=True),
        lax.psum_scatter(totals[1], "fsdp", scatter_dimension=0, tiled=True),
        lax.psum_scatter(totals[2], "fsdp", scatter_dimension=0, tiled=True),
        lax.psum_scatter(totals[3], "fsdp", scatter_dimension=1, tiled=True),
    )
    reduced = (
        lax.psum(shards[0].astype(jnp.bfloat16), "rep").astype(jnp.float32),
        lax.psum(shards[1].astype(jnp.bfloat16), "rep").astype(jnp.float32),
        lax.psum(shards[2].astype(jnp.bfloat16), "rep").astype(jnp.float32),
        lax.psum(shards[3].astype(jnp.bfloat16), "rep").astype(jnp.float32),
    )
    attn_rates = jnp.array(ATTN_RATES, jnp.float32)[:, None, None]
    attn_new, attn_first_new, attn_second_new = adam_update(
        attn_weight, attn_first, attn_second, reduced[0], attn_rates, WEIGHT_DECAY
    )
    up_new, up_first_new, up_second_new = adam_update(
        up_weight, up_first, up_second, reduced[1], UP_RATE, WEIGHT_DECAY
    )
    down_new, down_first_new, down_second_new = adam_update(
        down_weight, down_first, down_second, reduced[2], DOWN_RATE, WEIGHT_DECAY
    )
    vectors_new, vector_first_new, vector_second_new = adam_update(
        vectors, vector_first, vector_second, reduced[3], VECTOR_RATE, 0.0
    )
    return (
        layer_out,
        token_grad,
        attn_new,
        up_new,
        down_new,
        vectors_new,
        attn_first_new,
        up_first_new,
        down_first_new,
        vector_first_new,
        attn_second_new,
        up_second_new,
        down_second_new,
        vector_second_new,
        attn_new.astype(jnp.bfloat16),
        up_new.astype(jnp.bfloat16),
        down_new.astype(jnp.bfloat16),
        vectors_new.astype(jnp.bfloat16),
    )


def solution(mesh):
    blocked = mesh.shape["fsdp"] == 16 and mesh.shape["rep"] == 2
    return jax.shard_map(
        local if blocked else local_general,
        mesh=mesh,
        in_specs=(
            P(("fsdp", "rep"), None, None),
            P(("fsdp", "rep"), None, None),
            P(("fsdp", "rep")),
            P(("fsdp", "rep"), None, None),
            P(None, "fsdp", None),
            P("fsdp", None),
            P("fsdp", None),
            P(None, "fsdp"),
            P(None, "fsdp", None),
            P("fsdp", None),
            P("fsdp", None),
            P(None, "fsdp"),
            P(None, "fsdp", None),
            P("fsdp", None),
            P("fsdp", None),
            P(None, "fsdp"),
        ),
        out_specs=(
            P(("fsdp", "rep"), None, None),
            P(("fsdp", "rep"), None, None),
            P(None, "fsdp", None),
            P("fsdp", None),
            P("fsdp", None),
            P(None, "fsdp"),
            P(None, "fsdp", None),
            P("fsdp", None),
            P("fsdp", None),
            P(None, "fsdp"),
            P(None, "fsdp", None),
            P("fsdp", None),
            P("fsdp", None),
            P(None, "fsdp"),
            P(None, "fsdp", None),
            P("fsdp", None),
            P("fsdp", None),
            P(None, "fsdp"),
        ),
        check_vma=False,
    )
```

```python
from functools import partial
import math

import jax
import jax.numpy as jnp
from jax import lax
from jax.experimental import pallas as pl
from jax.experimental.pallas import tpu as pltpu
from jax.sharding import PartitionSpec as P

HEADS = 12
HEAD_DIM = 64
STEP = 7


EPS_NORM = 1e-12
EPS_ADAM = 1e-08
DECAY = 0.5
MASK_FILL = -1e30
WEIGHT_DECAY = 0.01
ATTN_RATES = (0.04, 0.04, 0.04, 0.2, 0.04)
UP_RATE = 0.04
DOWN_RATE = 0.02
VECTOR_RATE = 0.3


def contract(left_op, right_op, left_dim, right_dim):
    return lax.dot_general(
        left_op,
        right_op,
        (((left_dim,), (right_dim,)), ((), ())),
        preferred_element_type=jnp.float32,
    )


def layer_norm(hidden, gain_row, shift_row):
    center = hidden - jnp.mean(hidden, axis=-1, keepdims=True)
    spread = jnp.mean(center * center, axis=-1, keepdims=True)
    return center * lax.rsqrt(spread + EPS_NORM) * gain_row + shift_row


def box_tables(box_rows, model_width):
    quarter = model_width // 4
    frequency = jnp.exp(jnp.arange(quarter).astype(jnp.float32) * (-math.log(10000.0) / quarter))
    angles = box_rows.astype(jnp.float32)[:, :, None] * frequency
    return (jnp.sin(angles), jnp.cos(angles))


def encode(sine_rows, cosine_rows):
    return jnp.concatenate([sine_rows[0], cosine_rows[0], sine_rows[1], cosine_rows[1]], axis=-1)


def rotate(pos_table, sine_rows, cosine_rows):
    quarter = sine_rows.shape[-1]
    pieces = []
    for coord in range(2):
        sine_part = pos_table[..., 2 * coord * quarter : (2 * coord + 1) * quarter]
        cosine_part = pos_table[..., (2 * coord + 1) * quarter : (2 * coord + 2) * quarter]
        pieces.append(cosine_part * sine_rows[coord] - sine_part * cosine_rows[coord])
        pieces.append(sine_part * sine_rows[coord] + cosine_part * cosine_rows[coord])
    return jnp.concatenate(pieces, axis=-1)


def scores(query_rows, key_rows, left_rows, encoded, page_live):
    text_part = jnp.einsum("ihd,jhd->hij", query_rows, key_rows, preferred_element_type=jnp.float32)
    place_part = jnp.einsum("hie,je->hij", left_rows, encoded, preferred_element_type=jnp.float32)
    score_rows = (text_part + place_part) * HEAD_DIM ** (-0.5)
    return jnp.where(page_live[None, None, :], score_rows, MASK_FILL)


def forward_page(weights, token_row_block, box_rows, page_length):
    attention_matrices, up_mat, down_mat, vector_rows = weights
    row_count, model_width = token_row_block.shape
    vector_f32 = vector_rows.astype(jnp.float32)
    page_live = jnp.arange(row_count) < page_length
    projected_rows = jnp.einsum(
        "tb,mby->mty", token_row_block, attention_matrices[:3], preferred_element_type=jnp.float32
    )
    query_rows = (
        (projected_rows[0] + vector_f32[4]).astype(jnp.bfloat16).reshape(row_count, HEADS, HEAD_DIM)
    )
    key_rows = projected_rows[1].astype(jnp.bfloat16).reshape(row_count, HEADS, HEAD_DIM)
    value_rows = (
        (projected_rows[2] + vector_f32[5]).astype(jnp.bfloat16).reshape(row_count, HEADS, HEAD_DIM)
    )
    sine_rows, cosine_rows = box_tables(box_rows, model_width)
    encoded = encode(sine_rows, cosine_rows).astype(jnp.bfloat16)
    rel_heads = attention_matrices[4].reshape(model_width, HEADS, HEAD_DIM)
    pos_table = jnp.einsum(
        "ihd,ehd->hie", query_rows, rel_heads, preferred_element_type=jnp.float32
    )
    left_rows = rotate(pos_table, sine_rows, cosine_rows).astype(jnp.bfloat16)
    score_rows = scores(query_rows, key_rows, left_rows, encoded, page_live)
    row_top = jnp.max(score_rows, axis=-1, keepdims=True)
    exponent = jnp.exp(score_rows - row_top)
    row_total = jnp.sum(exponent, axis=-1, keepdims=True)
    prob_low = (exponent / row_total).astype(jnp.bfloat16)
    logsum = row_top + jnp.log(row_total)
    mixed_rows = jnp.einsum(
        "hij,jhd->ihd", prob_low, value_rows, preferred_element_type=jnp.float32
    )
    context = mixed_rows.reshape(row_count, model_width).astype(jnp.bfloat16)
    attn_out = (
        jnp.dot(context, attention_matrices[3], preferred_element_type=jnp.float32) + vector_f32[6]
    )
    first_sum = token_row_block.astype(jnp.float32) + attn_out
    normed = layer_norm(first_sum, vector_f32[0], vector_f32[1])
    pre_act = jnp.dot(
        normed.astype(jnp.bfloat16), up_mat, preferred_element_type=jnp.float32
    ) + vector_f32[8:].reshape(-1)
    act_low = jax.nn.gelu(pre_act, approximate=False).astype(jnp.bfloat16)
    second_sum = normed + (
        jnp.dot(act_low, down_mat, preferred_element_type=jnp.float32) + vector_f32[7]
    )
    page_out = (layer_norm(second_sum, vector_f32[2], vector_f32[3]) * page_live[:, None]).astype(
        jnp.bfloat16
    )
    saved_state = (
        query_rows,
        key_rows,
        value_rows,
        left_rows,
        logsum,
        context,
        first_sum,
        pre_act,
        act_low,
        second_sum,
    )
    return (page_out, saved_state)


def backward_page(weights, token_row_block, box_rows, page_length, upstream, saved_state):
    attention_matrices, up_mat, down_mat, vector_rows = weights
    (
        query_rows,
        key_rows,
        value_rows,
        left_rows,
        logsum,
        context,
        first_sum,
        pre_act,
        act_low,
        second_sum,
    ) = saved_state
    row_count, model_width = token_row_block.shape
    vector_f32 = vector_rows.astype(jnp.float32)
    page_live = jnp.arange(row_count) < page_length
    sine_rows, cosine_rows = box_tables(box_rows, model_width)
    encoded = encode(sine_rows, cosine_rows).astype(jnp.bfloat16)
    out_grad = upstream.astype(jnp.float32) * page_live[:, None]
    _, pull_second = jax.vjp(layer_norm, second_sum, vector_f32[2], vector_f32[3])
    second_grad, gain_two, shift_two = pull_second(out_grad)
    ffn_grad = second_grad.astype(jnp.bfloat16)
    down_grad = contract(act_low, ffn_grad, 0, 0)
    act_grad = contract(ffn_grad, down_mat, 1, 1)
    _, pull_gelu = jax.vjp(partial(jax.nn.gelu, approximate=False), pre_act)
    pre_grad = pull_gelu(act_grad)[0].astype(jnp.bfloat16)
    normed, pull_first = jax.vjp(layer_norm, first_sum, vector_f32[0], vector_f32[1])
    up_grad = contract(normed.astype(jnp.bfloat16), pre_grad, 0, 0)
    normed_grad = contract(pre_grad, up_mat, 1, 1) + second_grad
    first_grad, gain_one, shift_one = pull_first(normed_grad)
    attn_grad = first_grad.astype(jnp.bfloat16)
    out_mat_grad = contract(context, attn_grad, 0, 0)
    context_grad = (
        contract(attn_grad, attention_matrices[3], 1, 1)
        .astype(jnp.bfloat16)
        .reshape(row_count, HEADS, HEAD_DIM)
    )
    score_rows = scores(query_rows, key_rows, left_rows, encoded, page_live)
    prob_rows = jnp.exp(score_rows - logsum)
    value_grad = jnp.einsum(
        "hij,ihd->jhd",
        prob_rows.astype(jnp.bfloat16),
        context_grad,
        preferred_element_type=jnp.float32,
    ).astype(jnp.bfloat16)
    prob_grad = jnp.einsum(
        "ihd,jhd->hij", context_grad, value_rows, preferred_element_type=jnp.float32
    )
    score_grad = (
        prob_rows * (prob_grad - jnp.sum(prob_rows * prob_grad, axis=-1, keepdims=True))
    ).astype(jnp.bfloat16)
    score_scale = HEAD_DIM ** (-0.5)
    left_grad = (
        jnp.einsum("hij,je->hie", score_grad, encoded, preferred_element_type=jnp.float32)
        * score_scale
    )
    table_grad = rotate(left_grad, sine_rows, cosine_rows).astype(jnp.bfloat16)
    rel_heads = attention_matrices[4].reshape(model_width, HEADS, HEAD_DIM)
    rel_grad = jnp.einsum(
        "hie,ihd->ehd", table_grad, query_rows, preferred_element_type=jnp.float32
    ).reshape(model_width, model_width)
    query_grad = (
        jnp.einsum("hij,jhd->ihd", score_grad, key_rows, preferred_element_type=jnp.float32)
        * score_scale
    )
    query_grad = query_grad + jnp.einsum(
        "hie,ehd->ihd", table_grad, rel_heads, preferred_element_type=jnp.float32
    )
    key_grad = (
        jnp.einsum("hij,ihd->jhd", score_grad, query_rows, preferred_element_type=jnp.float32)
        * score_scale
    )
    stacked_layers = jnp.stack(
        [
            query_grad.astype(jnp.bfloat16).reshape(row_count, model_width),
            key_grad.astype(jnp.bfloat16).reshape(row_count, model_width),
            value_grad.reshape(row_count, model_width),
        ]
    )
    projection_gradient = jnp.einsum(
        "cg,yca->yga", token_row_block, stacked_layers, preferred_element_type=jnp.float32
    )
    token_grad = first_grad + jnp.einsum(
        "skl,scl->kc", stacked_layers, attention_matrices[:3], preferred_element_type=jnp.float32
    )
    column_sums = jnp.sum(stacked_layers.astype(jnp.float32), axis=1)
    attn_grads = jnp.concatenate([projection_gradient, out_mat_grad[None], rel_grad[None]], axis=0)
    small_rows = jnp.stack(
        [
            gain_one,
            shift_one,
            gain_two,
            shift_two,
            column_sums[0],
            column_sums[2],
            jnp.sum(attn_grad.astype(jnp.float32), axis=0),
            jnp.sum(ffn_grad.astype(jnp.float32), axis=0),
        ]
    )
    up_bias_rows = jnp.sum(pre_grad.astype(jnp.float32), axis=0).reshape(-1, model_width)
    vector_grad = jnp.concatenate([small_rows, up_bias_rows], axis=0)
    return (token_grad, (attn_grads, up_grad, down_grad, vector_grad))


def adam_update(weight, first, second, grad, rate, decay_weight):
    first_new = DECAY * first + (1.0 - DECAY) * grad
    second_new = DECAY * second + (1.0 - DECAY) * grad * grad
    correction = 1.0 - DECAY**STEP
    direction = first_new / correction / (jnp.sqrt(second_new / correction) + EPS_ADAM)
    return (weight - rate * (direction + decay_weight * weight), first_new, second_new)


AXES = ("fsdp", "rep")
ORDERS = ((8, 4, 2, 1), (8, 4, 1, 2))
PLANE_FIRST = ((1, 8, 4, 2), (2, 8, 4, 1))
DEPTH_FIRST = ((8, 2, 1, 4), (8, 1, 2, 4))
PLAIN_AT, DEPTH_AT, PLANE_AT = 32, 96, 64
LOW = jnp.bfloat16
WIDE = jnp.float32
CHUNK = 256
SLAB = 128
FEED_VMEM_BYTES = 58 * 1024 * 1024
OPEN_VMEM_BYTES = 28 * 1024 * 1024
ATTN_VMEM_BYTES = 28 * 1024 * 1024
CORE_AT, LENGTH_AT = 128, 129


def mask_table(order):
    masks = [0]
    for bit in order:
        masks = masks + [bit ^ mask for mask in masks]
    return masks


CORE_PAIRS = [(chip * 2 + core, chip * 2 + 1 - core) for chip in range(16) for core in range(2)]


def place_of(mask, order):
    place = 0
    for bit_at, bit in enumerate(order):
        place = place + jnp.where((mask & bit) != 0, 1 << bit_at, 0)
    return place


def block_scalars(chip, core, length):
    rows, lane = [], jnp.arange(16, dtype=jnp.int32)
    blocks = [jnp.array(mask_table(order), jnp.int32) ^ chip for order in ORDERS]
    places = [place_of(lane ^ chip, order) for order in ORDERS]
    plane_blocks = [jnp.array(mask_table(order), jnp.int32) ^ chip for order in PLANE_FIRST]
    depth_places = [place_of(lane ^ chip, order) for order in DEPTH_FIRST]
    for pair in (blocks, places, plane_blocks, depth_places):
        rows.append(jnp.where(core == 0, pair[0], pair[1]))
        rows.append(jnp.where(core == 0, pair[1], pair[0]))
    last = jnp.where(lane == 0, core, jnp.where(lane == 1, length, 0))
    return jnp.stack(rows + [last]).astype(jnp.int32).reshape(-1)


def after(value, *others):
    return lax.optimization_barrier((value, *others))[0]


def sync(*values):
    return lax.optimization_barrier(values)


def swap_cores(block):
    return lax.ppermute(block, AXES, CORE_PAIRS)


def hop(held, step, orders=ORDERS):
    pairs = [
        (chip * 2 + core, (chip ^ orders[core][step]) * 2 + core)
        for chip in range(16)
        for core in range(2)
    ]
    return lax.ppermute(held, AXES, pairs)


def join(held, arrived):
    return jnp.concatenate([held, arrived], axis=0)


def add_up(terms):
    total_sum = terms[0].astype(WIDE)
    for term in terms[1:]:
        total_sum = total_sum + term.astype(WIDE)
    return total_sum.astype(terms[0].dtype)


def halve(terms):
    half = terms[0].shape[0] // 2
    return [term[:half] for term in terms], add_up([term[half:] for term in terms])


def by_half(core, sums):
    mine, other = sums
    first = jnp.where(core == 0, mine, other)
    second = jnp.where(core == 0, other, mine)
    return first.astype(WIDE), second.astype(WIDE)


def dot(left_op, right_op, left_dim, right_dim):
    return lax.dot_general(
        left_op,
        right_op,
        (((left_dim,), (right_dim,)), ((), ())),
        preferred_element_type=WIDE,
    )


def each(count, size, body, flat=False):
    def step(index, carry):
        body(pl.ds(pl.multiple_of(index * size, size), size))
        return carry

    if flat:
        for index in range(count // size):
            body(pl.ds(index * size, size))
    else:
        lax.fori_loop(0, count // size, step, 0)


def block_at(index):
    return pl.ds(pl.multiple_of(index * 48, 16), 48)


def turned(block):
    return (block & 3) | ((block & 4) << 1) | ((block & 8) >> 1)


def start_copies(make, count):
    def start(place, carry):
        for copy in make(place):
            copy.start()
        return carry

    lax.fori_loop(0, count, start, 0)


def wait_for(buffer, sem):
    pltpu.make_async_copy(buffer, buffer, sem).wait()


def sources(scal, pieces):
    core = scal[CORE_AT]
    bases = (0, 8, 16, 24)
    halves = (core, core, 1 - core, 1 - core)
    return [(piece, base, half) for piece, base, half in zip(pieces, bases, halves, strict=True)]


def attn_copies(scal, pieces, lanes, mats, spot, sem, place):
    copies = []
    for source, base, half in sources(scal, pieces):
        block = scal[base + place]
        for part in range(2):
            row = block if part == 0 else jnp.where(half == 1, turned(block), block)
            copies.append(
                pltpu.make_async_copy(
                    source.at[place, pl.ds(48 * part, 48), lanes],
                    mats.at[2 * half + part, block_at(row), spot],
                    sem,
                )
            )
    return copies


def head_masks(dtype):
    lane = lax.broadcasted_iota(jnp.int32, (1, 128), 1)
    first = jnp.where(lane < 64, 1.0, 0.0)
    return (first.astype(dtype), (1.0 - first).astype(dtype))


def attend_kernel(
    group,
    scal,
    tokens,
    vec,
    sines,
    cosines,
    encoded,
    *refs,
):
    pieces, refs = refs[:4], refs[4:] if group == 0 else refs[10:]
    q_out, k_out, v_out, ctx_out, prob_out, mats_out = refs[:6]
    mats, right, sem, sem_out = refs[6:]
    pair = pl.program_id(0)
    width = tokens.shape[1]
    rows = tokens.shape[0]

    @pl.when(pair == 0)
    def _():
        cols = mats.shape[2]
        lane_at = pl.ds(group * cols, cols)
        start_copies(partial(attn_copies, scal, pieces, lane_at, mats, pl.ds(0, cols), sem), 8)
        wait_for(mats, sem)
        pltpu.make_async_copy(mats, mats_out.at[:, :, lane_at], sem_out).start()
        right[:, :width] = encoded[...]

        def project(at):
            x = tokens[at, :]
            q_out[at, :] = (dot(x, mats[0], 1, 0) + vec[4:5, :]).astype(LOW)
            k_out[at, :] = dot(x, mats[1], 1, 0).astype(LOW)
            v_out[at, :] = (dot(x, mats[2], 1, 0) + vec[5:6, :]).astype(LOW)

        each(rows, CHUNK, project)

    lanes = pl.ds(pl.multiple_of(pair * 128, 128), 128)
    right[:, width:] = k_out[:, lanes]
    rel = mats[3, :, lanes]
    live = lax.broadcasted_iota(jnp.int32, (1, rows), 1) < scal[LENGTH_AT]
    half = width // 2

    def score(at):
        q_pair = q_out[at, :] if q_out.shape[1] == 128 else q_out[at, lanes]
        sin, cos = sines[at, :], cosines[at, :]
        mixed = []
        for head, mask in enumerate(head_masks(LOW)):
            q_head = q_pair * mask
            table = dot(q_head, rel, 1, 1)
            us, uc = table[:, :half], table[:, half:]
            left = jnp.concatenate(
                [(uc * sin - us * cos).astype(LOW), (us * sin + uc * cos).astype(LOW), q_head], axis=1
            )
            s = dot(left, right[...], 1, 1) * HEAD_DIM ** (-0.5)
            s = jnp.where(live, s, MASK_FILL)
            top = jnp.max(s, axis=-1, keepdims=True)
            e = jnp.exp(s - top)
            prob = (e * (1.0 / jnp.sum(e, axis=-1, keepdims=True))).astype(LOW)
            prob_out[head, at, :] = prob
            mixed.append(dot(prob, v_out[:, lanes], 1, 0))
        masks = head_masks(WIDE)
        ctx_out[at, :] = (mixed[0] * masks[0] + mixed[1] * masks[1]).astype(LOW)

    each(rows, rows, score, True)

    @pl.when(pair == pl.num_programs(0) - 1)
    def _():
        wait_for(mats, sem_out)


def any_space():
    return pl.BlockSpec(memory_space=pl.ANY)


def whole(shape):
    return pl.BlockSpec(shape, lambda *_: (0,) * len(shape))


def attend(group, scal, tokens, vec, sines, cosines, encoded, pieces, before):
    rows, width = tokens.shape
    pairs, cols = PAIRS, 128 * PAIRS
    low = jax.ShapeDtypeStruct((rows, width), LOW)
    prob = pltpu.HBM((width // HEAD_DIM, rows, rows), LOW)
    mats = jax.ShapeDtypeStruct((4, width, width), LOW)
    return pl.pallas_call(
        partial(attend_kernel, group),
        out_shape=(low, low, low, low, prob, mats),
        grid_spec=pltpu.PrefetchScalarGridSpec(
            num_scalar_prefetch=1,
            grid=(pairs,),
            in_specs=[
                whole((rows, width)),
                pl.BlockSpec((vec.shape[0], cols), lambda p, _: (0, group)),
                whole((rows, width // 2)),
                whole((rows, width // 2)),
                whole((rows, width)),
            ]
            + [any_space()] * (4 + len(before)),
            out_specs=[pl.BlockSpec((rows, cols), lambda p, _: (0, group))] * 3
            + [
                pl.BlockSpec((rows, 128), lambda p, _: (0, group * pairs + p)),
                pl.BlockSpec((2, rows, rows), lambda p, _: (group * pairs + p, 0, 0)),
                any_space(),
            ],
            scratch_shapes=[
                pltpu.VMEM((4, width, cols), LOW),
                pltpu.VMEM((rows, width + 128), LOW),
                pltpu.SemaphoreType.DMA,
                pltpu.SemaphoreType.DMA,
            ],
        ),
        compiler_params=pltpu.CompilerParams(
            dimension_semantics=("arbitrary",), vmem_limit_bytes=ATTN_VMEM_BYTES
        ),
        cost_estimate=pl.CostEstimate(
            flops=pairs * 2 * rows * width * 3072, transcendentals=0, bytes_accessed=24 * 1024 * 1024
        ),
        input_output_aliases={10 + at: at for at in range(len(before))},
        name="attend",
    )(scal, tokens, vec, sines, cosines, encoded, *pieces, *before)


CDF_POLY = (
    -0.020695917308330536,
    0.09534552693367004,
    -0.15029412508010864,
    0.07120334357023239,
    -0.011180647648870945,
    0.05997580662369728,
    0.08762594312429428,
    0.11413583159446716,
    0.12694157660007477,
    0.12694266438484192,
)
CDF_SLOPE = 0.45 / math.sqrt(2.0)


def gelu_pair(x):
    size = jnp.abs(x)
    t = 1.0 / (1.0 + CDF_SLOPE * size)
    bell = jnp.exp2(x * x * (-0.5 / math.log(2.0)))
    poly = CDF_POLY[0]
    for value in CDF_POLY[1:]:
        poly = poly * t + value
    tail = poly * t * bell
    cdf = jnp.where(x < 0.0, tail, 1.0 - tail)
    return x * cdf, cdf + x * bell * (1.0 / math.sqrt(2.0 * math.pi))


def moments(z):
    center = z - jnp.mean(z, axis=-1, keepdims=True)
    r = lax.rsqrt(jnp.mean(center * center, axis=-1, keepdims=True) + EPS_NORM)
    return center * r, r


def norm_back(grad, xh, r, gain):
    dxh = grad * gain
    return r * (
        dxh - jnp.mean(dxh, axis=-1, keepdims=True) - xh * jnp.mean(dxh * xh, axis=-1, keepdims=True)
    )


def total(values):
    return jnp.sum(values, axis=0, keepdims=True)


def out_copies(scal, pieces, out_mat, sem, place):
    return [
        pltpu.make_async_copy(
            source.at[place, :, pl.ds(0, 384)],
            out_mat.at[block_at(scal[base + place]), pl.ds(pl.multiple_of(half * 384, 128), 384)],
            sem,
        )
        for source, base, half in sources(scal, pieces)
    ]


def down_copies(scal, pieces, down_mat, sem, place):
    return [
        pltpu.make_async_copy(
            source.at[place],
            down_mat.at[pl.ds(pl.multiple_of(scal[PLANE_AT + base + place] * 192 + half * 96, 32), 96)],
            sem,
        )
        for source, base, half in sources(scal, pieces)
    ]


def per_core(scal, body):
    for core in range(2):

        @pl.when(scal[CORE_AT] == core)
        def _(core=core):
            body(core)


def send_block(scal, source, outs, side, block, cut, sem, table=PLAIN_AT):
    place = scal[table + 16 * side + block]
    if side == 0:
        pltpu.make_async_copy(source, cut(outs[0], place), sem).start()
        return
    for part in range(2):

        @pl.when(place // 8 == part)
        def _(part=part):
            pltpu.make_async_copy(source, cut(outs[1 + part], lax.rem(place, 8)), sem).start()


def block_shapes(rows, cols):
    return tuple(jax.ShapeDtypeStruct((count, rows, cols), LOW) for count in (16, 8, 8))


def up_fetch(scal, pieces, up_mat, sems, first):
    def fetch(core):
        for unit in range(4):
            near = 0 if unit // 2 == core else 2

            def start(place, carry, unit=unit, near=near):
                for index in (near, near + 1):
                    pltpu.make_async_copy(
                        pieces[index].at[place, :, pl.ds(384 + 768 * (unit % 2), 768)],
                        up_mat.at[unit, block_at(scal[8 * index + place])],
                        sems.at[first + unit],
                    ).start()
                return carry

            lax.fori_loop(0, 8, start, 0)

    per_core(scal, fetch)


def open_kernel(
    scal, tokens, vec, *refs
):
    ctx, pieces = refs[0], refs[1:5]
    norm_low, xh1, r1, act, slope, out_mat, up_mat, sem_in = refs[5:]
    step = pl.program_id(0)
    rows, width = tokens.shape

    @pl.when(step == 0)
    def _():
        start_copies(partial(out_copies, scal, pieces, out_mat, sem_in.at[0]), 8)
        up_fetch(scal, pieces, up_mat, sem_in, 1)
        wait_for(out_mat, sem_in.at[0])

        def first(at):
            attn = dot(ctx[at, :], out_mat[...], 1, 0) + vec[6:7, :]
            hat, r = moments(tokens[at, :].astype(WIDE) + attn)
            xh1[at, :] = hat
            r1[at, :] = jnp.broadcast_to(r, (r.shape[0], 128))
            norm_low[at, :] = (hat * vec[0:1, :] + vec[1:2, :]).astype(LOW)

        each(rows, CHUNK, first)

    wait_for(up_mat.at[step], sem_in.at[1 + step])

    bias = vec[pl.ds(8 + step, 1), :]
    spots = [pl.ds(CHUNK * index, CHUNK) for index in range(rows // CHUNK)]

    def front(at):
        return dot(norm_low[at, :], up_mat[step], 1, 0) + bias

    pre = front(spots[0])
    for index, at in enumerate(spots):
        ahead = front(spots[index + 1]) if index + 1 < len(spots) else None
        value, grad = gelu_pair(pre)
        act[0, at, :] = value.astype(LOW)
        slope[0, at, :] = grad
        pre = ahead


def open_ffn(scal, tokens, vec, ctx, two):
    rows, width = tokens.shape
    unit = pl.BlockSpec((1, rows, width), lambda j, _: (j, 0, 0))
    return pl.pallas_call(
        open_kernel,
        out_shape=(
            pltpu.HBM((rows, width), LOW),
            pltpu.HBM((rows, width), WIDE),
            pltpu.HBM((rows, 128), WIDE),
            pltpu.HBM((4, rows, width), LOW),
            pltpu.HBM((4, rows, width), WIDE),
        ),
        grid_spec=pltpu.PrefetchScalarGridSpec(
            num_scalar_prefetch=1,
            grid=(4,),
            in_specs=[whole((rows, width)), whole((16, width))]
            + [whole((rows, width))]
            + [any_space()] * 4,
            out_specs=[whole((rows, width))] * 2 + [whole((rows, 128)), unit, unit],
            scratch_shapes=[
                pltpu.VMEM((width, width), LOW),
                pltpu.VMEM((4, width, width), LOW),
                pltpu.SemaphoreType.DMA((5,)),
            ],
        ),
        compiler_params=pltpu.CompilerParams(
            dimension_semantics=("arbitrary",), vmem_limit_bytes=OPEN_VMEM_BYTES
        ),
        cost_estimate=pl.CostEstimate(
            flops=2 * rows * width * width * 9, transcendentals=0, bytes_accessed=18 * 1024 * 1024
        ),
        name="open_ffn",
    )(scal, tokens, vec, ctx, *two)


def feed_kernel(*refs):
    scal, cot, vec, ctx, act_in, slope_in, norm_in, xh_in, r_in = refs[:9]
    two_pieces, three_pieces = refs[9:13], refs[13:17]
    page_out, dh1_out, dctx_out, *outs = refs[17:26]
    two_outs, three_outs = outs[:3], outs[3:]
    (
        out_mat,
        up_mat,
        down_mat,
        norm_low,
        xh1,
        r1,
        act,
        slope,
        held,
        df,
        dpre,
        dattn,
        g_out,
        g_up,
        g_down,
        vec_out,
        vec_low,
        sem_in,
        sem_up,
        sem_down,
        sem_out,
        sem_page,
        sem_rows,
    ) = refs[26:]
    step = pl.program_id(0)
    rows, width = cot.shape
    length = scal[LENGTH_AT]

    @pl.when(step == 0)
    def _():
        start_copies(partial(down_copies, scal, three_pieces, down_mat, sem_in.at[0]), 8)
        for source, target, at in (
            (xh_in, xh1, 1),
            (act_in, act, 2),
            (norm_in, norm_low, 3),
            (r_in, r1, 4),
            (slope_in, slope, 5),
        ):
            pltpu.make_async_copy(source, target, sem_in.at[at]).start()
        up_fetch(scal, two_pieces, up_mat, sem_in, 6)
        start_copies(partial(out_copies, scal, two_pieces, out_mat, sem_in.at[10]), 8)
        vec_out[...] = jnp.zeros_like(vec_out)
        wait_for(xh1, sem_in.at[1])

        def prime(at):
            held[at, :] = xh1[at, :] * vec[0:1, :] + (vec[1:2, :] + vec[7:8, :])

        each(rows, SLAB, prime)
        wait_for(act, sem_in.at[2])
        wait_for(down_mat, sem_in.at[0])

    @pl.when(step < 4)
    def _():
        down_at = pl.ds(pl.multiple_of(step * width, width), width)
        held[...] += dot(act[step], down_mat[down_at, :], 1, 0)

    @pl.when(step == 3)
    def _():
        def second(at):
            hat, r = moments(held[at, :])
            place = lax.broadcasted_iota(jnp.int32, (SLAB, 1), 0) + at.start
            live = jnp.where(place < length, 1.0, 0.0)
            dattn[at, :] = ((hat * vec[2:3, :] + vec[3:4, :]) * live).astype(LOW)
            dy = cot[at, :].astype(WIDE) * live
            vec_out[2:3, :] += total(dy * hat)
            vec_out[3:4, :] += total(dy)
            dh2 = norm_back(dy, hat, r, vec[2:3, :])
            low = dh2.astype(LOW)
            df[at, :] = low
            vec_out[7:8, :] += total(low.astype(WIDE))
            held[at, :] = dh2

        each(rows, SLAB, second)
        pltpu.make_async_copy(dattn, page_out, sem_page).start()
        wait_for(slope, sem_in.at[5])
        wait_for(norm_low, sem_in.at[3])
        wait_for(r1, sem_in.at[4])
        wait_for(out_mat, sem_in.at[10])
        for unit in range(4):
            wait_for(up_mat.at[unit], sem_in.at[6 + unit])

    def send_up(slot, unit):
        at = pl.ds(pl.multiple_of(384 + 768 * lax.rem(unit, 2), 128), 768)
        for side in range(2):

            @pl.when((unit // 2 == scal[CORE_AT]) == (side == 0))
            def _(side=side):
                def body(block, carry):
                    send_block(
                        scal,
                        g_up.at[slot, block_at(block)],
                        two_outs,
                        side,
                        block,
                        lambda ref, place: ref.at[place, :, at],
                        sem_up.at[slot],
                    )
                    return carry

                lax.fori_loop(0, 16, body, 0)

    def send_down(slot, unit):
        def body(core):
            for part in range(8):
                send_block(
                    scal,
                    g_down.at[slot, pl.ds(96 * part, 96)],
                    three_outs,
                    (part % 2) ^ core,
                    4 * unit + part // 2,
                    lambda ref, place: ref.at[place, pl.ds(0, 96)],
                    sem_down.at[slot],
                    DEPTH_AT,
                )

        per_core(scal, body)

    def send_out():
        def on(core):
            def body(block, carry):
                for half in range(2):
                    send_block(
                        scal,
                        g_out.at[block_at(block), pl.ds(384 * half, 384)],
                        two_outs,
                        half ^ core,
                        block,
                        lambda ref, place: ref.at[place, :, pl.ds(0, 384)],
                        sem_out,
                    )
                return carry

            lax.fori_loop(0, 16, body, 0)

        per_core(scal, on)

    @pl.when(step >= 4)
    def _():
        unit = step - 4
        slot = lax.rem(unit, 2)
        down_at = pl.ds(pl.multiple_of(unit * width, width), width)

        @pl.when(unit >= 2)
        def _():
            wait_for(g_up.at[slot], sem_up.at[slot])
            wait_for(g_down.at[slot], sem_down.at[slot])

        def backward(at):
            grad = dot(df[at, :], down_mat[down_at, :], 1, 1) * slope[unit, at, :]
            low = grad.astype(LOW)
            dpre[at, :] = low
            vec_out[pl.ds(8 + unit, 1), :] += total(low.astype(WIDE))
            held[at, :] += dot(low, up_mat[unit], 1, 1)

        each(rows, rows, backward, True)

        def weights(at):
            g_down[slot, at, :] = dot(act[unit, :, at], df[...], 0, 0).astype(LOW)
            g_up[slot, at, :] = dot(norm_low[:, at], dpre[...], 0, 0).astype(LOW)

        each(width, width, weights, True)
        send_down(slot, unit)
        send_up(slot, unit)

    @pl.when(step == 7)
    def _():
        wait_for(dattn, sem_page)

        def last(at):
            grad, hat = held[at, :], xh1[at, :]
            vec_out[0:1, :] += total(grad * hat)
            vec_out[1:2, :] += total(grad)
            dh1 = norm_back(grad, hat, r1[at, :1], vec[0:1, :])
            held[at, :] = dh1
            pltpu.make_async_copy(held.at[at], dh1_out.at[at], sem_rows.at[0]).start()
            low = dh1.astype(LOW)
            dattn[at, :] = low
            vec_out[6:7, :] += total(low.astype(WIDE))

        each(rows, SLAB, last)
        vec_low[...] = jnp.zeros_like(vec_low)
        vec_low[0, 0:4, :] = vec_out[0:4, :].astype(LOW)
        vec_low[0, 4:5, :] = vec_out[6:7, :].astype(LOW)
        vec_low[1, 0:5, :] = vec_out[7:12, :].astype(LOW)

        def send_vectors(core):
            def body(block, carry):
                for half in range(2):
                    send_block(
                        scal,
                        vec_low.at[half],
                        three_outs,
                        half ^ core,
                        block,
                        lambda ref, place: ref.at[place, pl.ds(96, 8)],
                        sem_page,
                        DEPTH_AT,
                    )
                return carry

            lax.fori_loop(0, 16, body, 0)

        per_core(scal, send_vectors)

        def weights(at):
            g_out[at, :] = dot(ctx[:, at], dattn[...], 0, 0).astype(LOW)

        each(width, CHUNK, weights)
        send_out()

        def context(at):
            df[at, :] = dot(dattn[at, :], out_mat[...], 1, 1).astype(LOW)
            pltpu.make_async_copy(df.at[at], dctx_out.at[at], sem_rows.at[1]).start()

        each(rows, CHUNK, context)
        for slot in range(2):
            wait_for(g_up.at[slot], sem_up.at[slot])
            wait_for(g_down.at[slot], sem_down.at[slot])
        wait_for(g_out, sem_out)
        wait_for(held, sem_rows.at[0])
        wait_for(df, sem_rows.at[1])
        lax.fori_loop(0, 16, lambda _, carry: (wait_for(vec_low, sem_page), carry)[1], 0)


def feed(scal, cot, vec, ctx, opened, two, three):
    rows, width = cot.shape
    return pl.pallas_call(
        feed_kernel,
        out_shape=(
            jax.ShapeDtypeStruct((rows, width), LOW),
            jax.ShapeDtypeStruct((rows, width), WIDE),
            jax.ShapeDtypeStruct((rows, width), LOW),
        )
        + block_shapes(48, 384 + 2 * width)
        + block_shapes(104, width),
        grid_spec=pltpu.PrefetchScalarGridSpec(
            num_scalar_prefetch=1,
            grid=(8,),
            in_specs=[whole((rows, width)), whole((16, width)), whole((rows, width))]
            + [any_space()] * 13,
            out_specs=[any_space()] * 9,
            scratch_shapes=[
                pltpu.VMEM((width, width), LOW),
                pltpu.VMEM((4, width, width), LOW),
                pltpu.VMEM((4 * width, width), LOW),
                pltpu.VMEM((rows, width), LOW),
                pltpu.VMEM((rows, width), WIDE),
                pltpu.VMEM((rows, 128), WIDE),
                pltpu.VMEM((4, rows, width), LOW),
                pltpu.VMEM((4, rows, width), WIDE),
                pltpu.VMEM((rows, width), WIDE),
                pltpu.VMEM((rows, width), LOW),
                pltpu.VMEM((rows, width), LOW),
                pltpu.VMEM((rows, width), LOW),
                pltpu.VMEM((width, width), LOW),
                pltpu.VMEM((2, width, width), LOW),
                pltpu.VMEM((2, width, width), LOW),
                pltpu.VMEM((16, width), WIDE),
                pltpu.VMEM((2, 8, width), LOW),
                pltpu.SemaphoreType.DMA((11,)),
                pltpu.SemaphoreType.DMA((2,)),
                pltpu.SemaphoreType.DMA((2,)),
                pltpu.SemaphoreType.DMA,
                pltpu.SemaphoreType.DMA,
                pltpu.SemaphoreType.DMA((2,)),
            ],
        ),
        compiler_params=pltpu.CompilerParams(
            dimension_semantics=("arbitrary",), vmem_limit_bytes=FEED_VMEM_BYTES
        ),
        cost_estimate=pl.CostEstimate(
            flops=2 * rows * width * width * 27, transcendentals=0, bytes_accessed=32 * 1024 * 1024
        ),
        name="feed",
    )(scal, cot, vec, ctx, *opened, *two, *three)


def split_kernel(scal, attn, up, down, two_out, three_out):
    for core in range(2):

        @pl.when(scal[0] == core)
        def _(core=core):
            two_out[0, :, :384] = attn[3, :, 384 * core : 384 * (core + 1)].astype(LOW)
            two_out[0, :, 384:] = up[:, 1536 * core : 1536 * (core + 1)].astype(LOW)
            three_out[0] = down[96 * core : 96 * (core + 1), :].astype(LOW)


def split_weights(core, attn, up, down):
    width = attn.shape[2]
    shapes = ((1, 48, 384 + 2 * width), (1, 96, width))
    return pl.pallas_call(
        split_kernel,
        out_shape=tuple(jax.ShapeDtypeStruct(shape, LOW) for shape in shapes),
        grid_spec=pltpu.PrefetchScalarGridSpec(
            num_scalar_prefetch=1,
            grid=(1,),
            in_specs=[whole(attn.shape), whole(up.shape), whole(down.shape)],
            out_specs=[whole(shape) for shape in shapes],
        ),
        cost_estimate=pl.CostEstimate(flops=0, transcendentals=0, bytes_accessed=3 * 1024 * 1024),
        name="split_weights",
    )(core, attn, up, down)


def unattend_kernel(
    group,
    scal,
    tokens,
    sines,
    cosines,
    encoded,
    q_in,
    k_in,
    v_in,
    dctx_in,
    prob,
    *refs,
):
    mats_in, dq_out, dk_out, dv_out = refs[:4]
    outs = refs[4:7]
    (
    mats,
    right,
    ds_low,
    du_low,
    q_heads,
    d_heads,
    grads,
    sums,
    sem,
    sem_out,
    sem_sums,
    ) = refs[7:]
    pair = pl.program_id(0)
    rows, width = tokens.shape
    half = width // 2
    scale = HEAD_DIM ** (-0.5)

    @pl.when(pair == 0)
    def _():
        cols = mats.shape[1]
        lane_at = pl.ds(group * cols, cols)
        fetch = pltpu.make_async_copy(mats_in.at[3, :, lane_at], mats, sem)
        fetch.start()
        right[:, :width] = encoded[...]
        fetch.wait()

    lanes = pl.ds(pl.multiple_of(pair * 128, 128), 128)
    right[:, width:] = k_in[...]
    rel = mats[:, lanes]
    low_masks, wide_masks = head_masks(LOW), head_masks(WIDE)

    def score(at):
        sin, cos = sines[at, :], cosines[at, :]
        dq = None
        for head in range(2):
            spot = pl.ds(pl.multiple_of(head * rows + at.start, at.size), at.size)
            dctx = dctx_in[at, :] * low_masks[head]
            d_heads[spot, :] = dctx
            q_heads[spot, :] = q_in[at, :] * low_masks[head]
            p = prob[head, at, :].astype(WIDE)
            dp = dot(dctx, v_in[...], 1, 1)
            ds = (p * (dp - jnp.sum(p * dp, axis=-1, keepdims=True))).astype(LOW)
            ds_low[spot, :] = ds
            dl = dot(ds, right[...], 1, 0) * scale
            ls, lc = dl[:, :half], dl[:, half:width]
            du = jnp.concatenate(
                [(lc * sin - ls * cos).astype(LOW), (ls * sin + lc * cos).astype(LOW)], axis=1
            )
            du_low[spot, :] = du
            part = (dl[:, width:] + dot(du, rel, 1, 0)) * wide_masks[head]
            dq = part if dq is None else dq + part
        dq_out[at, lanes] = dq.astype(LOW)

    each(rows, rows, score, True)
    dv_out[:, lanes] = dot(prob[...].reshape(2 * rows, rows), d_heads[...], 0, 0).astype(LOW)
    dk_out[:, lanes] = (dot(ds_low[...], q_heads[...], 0, 0) * scale).astype(LOW)
    grads[3, :, lanes] = dot(du_low[...], q_heads[...], 0, 0).astype(LOW)

    @pl.when(pair == pl.num_programs(0) - 1)
    def _():
        def weights(at):
            x = tokens[:, at]
            grads[0, at, :] = dot(x, dq_out[...], 0, 0).astype(LOW)
            grads[1, at, :] = dot(x, dk_out[...], 0, 0).astype(LOW)
            grads[2, at, :] = dot(x, dv_out[...], 0, 0).astype(LOW)

        each(width, CHUNK, weights)

        sums[...] = jnp.zeros_like(sums)
        sums[0, 0:1, :] = total(dq_out[...].astype(WIDE)).astype(LOW)
        sums[1, 0:1, :] = total(dv_out[...].astype(WIDE)).astype(LOW)

        def on(core):
            def body(block, carry):
                for slot in range(4):
                    row = turned(block) if slot == 3 else block
                    at = pl.ds(48 * (slot % 2), 48)
                    send_block(
                        scal,
                        grads.at[slot, block_at(row)],
                        outs,
                        (slot // 2) ^ core,
                        block,
                        lambda ref, place, at=at: ref.at[place, at],
                        sem_out,
                    )
                for half in range(2):
                    send_block(
                        scal,
                        sums.at[half],
                        outs,
                        half ^ core,
                        block,
                        lambda ref, place: ref.at[place, pl.ds(96, 8)],
                        sem_sums,
                    )
                return carry

            lax.fori_loop(0, 16, body, 0)

        per_core(scal, on)
        wait_for(grads, sem_out)
        lax.fori_loop(0, 16, lambda _, carry: (wait_for(sums, sem_sums), carry)[1], 0)


def unattend(group, scal, tokens, sines, cosines, encoded, q, k, v, dctx, prob, mats):
    rows, width = tokens.shape
    pairs, cols = BACK_PAIRS, 128 * BACK_PAIRS
    low = jax.ShapeDtypeStruct((rows, cols), LOW)
    lane_block = pl.BlockSpec((rows, 128), lambda p, _: (0, group * pairs + p))
    return pl.pallas_call(
        partial(unattend_kernel, group),
        out_shape=(low, low, low) + block_shapes(104, cols),
        grid_spec=pltpu.PrefetchScalarGridSpec(
            num_scalar_prefetch=1,
            grid=(pairs,),
            in_specs=[
                whole((rows, width)),
                whole((rows, half_of(width))),
                whole((rows, half_of(width))),
                whole((rows, width)),
                lane_block,
                lane_block,
                lane_block,
                lane_block,
                pl.BlockSpec((2, rows, rows), lambda p, _: (group * pairs + p, 0, 0)),
            ]
            + [any_space()],
            out_specs=[whole((rows, cols))] * 3 + [any_space()] * 3,
            scratch_shapes=[
                pltpu.VMEM((width, cols), LOW),
                pltpu.VMEM((rows, width + 128), LOW),
                pltpu.VMEM((2 * rows, rows), LOW),
                pltpu.VMEM((2 * rows, width), LOW),
                pltpu.VMEM((2 * rows, 128), LOW),
                pltpu.VMEM((2 * rows, 128), LOW),
                pltpu.VMEM((4, width, cols), LOW),
                pltpu.VMEM((2, 8, cols), LOW),
                pltpu.SemaphoreType.DMA,
                pltpu.SemaphoreType.DMA,
                pltpu.SemaphoreType.DMA,
            ],
        ),
        compiler_params=pltpu.CompilerParams(
            dimension_semantics=("arbitrary",), vmem_limit_bytes=ATTN_VMEM_BYTES
        ),
        cost_estimate=pl.CostEstimate(
            flops=pairs * 2 * rows * width * 5000, transcendentals=0, bytes_accessed=24 * 1024 * 1024
        ),
        name="unattend",
    )(scal, tokens, sines, cosines, encoded, q, k, v, dctx, prob, mats)


def half_of(width):
    return width // 2


def input_grad_kernel(dh1, *refs):
    parts, (mats, out) = refs[: 3 * BACK_GROUPS], refs[3 * BACK_GROUPS :]
    slot = pl.program_id(0)

    @pl.when(slot == 0)
    def _():
        out[...] = dh1[...]

    for part in range(3):

        @pl.when(slot == part)
        def _(part=part):
            left = jnp.concatenate([parts[3 * g + part][...] for g in range(BACK_GROUPS)], axis=1)
            out[...] += dot(left, mats[0], 1, 1)


def input_grad(dh1, parts, mats):
    rows, width = dh1.shape
    slim = whole((rows, width // BACK_GROUPS))
    return pl.pallas_call(
        input_grad_kernel,
        out_shape=jax.ShapeDtypeStruct((rows, width), WIDE),
        grid=(3,),
        in_specs=[whole((rows, width))]
        + [slim] * (3 * BACK_GROUPS)
        + [pl.BlockSpec((1, width, width), lambda j: (j, 0, 0))],
        out_specs=whole((rows, width)),
        compiler_params=pltpu.CompilerParams(
            dimension_semantics=("arbitrary",), vmem_limit_bytes=ATTN_VMEM_BYTES
        ),
        cost_estimate=pl.CostEstimate(
            flops=2 * rows * width * width * 3, transcendentals=0, bytes_accessed=10 * 1024 * 1024
        ),
        name="input_grad",
    )(dh1, *parts, mats)


PAIRS = 3
BACK_PAIRS = 2
BACK_GROUPS = 3


def local(
    tokens,
    boxes,
    lengths,
    cotangent,
    attn_weight,
    up_weight,
    down_weight,
    vectors,
    attn_first,
    up_first,
    down_first,
    vector_first,
    attn_second,
    up_second,
    down_second,
    vector_second,
):
    chip, core = lax.axis_index("fsdp"), lax.axis_index("rep")
    width = tokens.shape[2]
    cols = width - width // BACK_GROUPS
    first = core == 0
    page = tokens[0]
    same = (ORDERS[0], ORDERS[0])

    near = jnp.where(first, attn_weight[:2], attn_weight[2:5:2]).astype(LOW).reshape(1, 96, width)
    near_far = hop(near, 0)
    core_at = after(core.astype(jnp.int32)[None], near)
    two, three = split_weights(core_at, attn_weight, up_weight, down_weight)
    three_far = hop(three, 0, PLANE_FIRST)
    vec = lax.dynamic_update_slice(
        jnp.zeros((vectors.shape[0], width), LOW),
        after(vectors.astype(LOW), near),
        (jnp.int32(0), chip * vectors.shape[1]),
    )
    scal = block_scalars(chip, core, lengths[0])
    near, near_far, two, vec, place, scal = sync(near, near_far, two, vec, boxes[0], scal)

    near = join(near, near_far)
    near_far = hop(near, 1)
    vec_far = hop(vec, 0, same)
    quarter = width // 4
    frequency = jnp.exp(jnp.arange(quarter).astype(WIDE) * (-math.log(10000.0) / quarter))
    place = place.astype(WIDE)
    angles = jnp.concatenate([place[0][:, None] * frequency, place[1][:, None] * frequency], axis=1)
    sines, cosines = jnp.sin(angles), jnp.cos(angles)
    encoded = jnp.concatenate([sines, cosines], axis=1).astype(LOW)
    near, near_far, vec, vec_far, two, three, three_far, sines, cosines, encoded = sync(
        near, near_far, vec, vec_far, two, three, three_far, sines, cosines, encoded
    )

    near = join(near, near_far)
    near_far = hop(near, 2)
    two_far = hop(two, 0)
    vec = vec + vec_far
    vec_far = hop(vec, 1, same)
    three = join(three, three_far)
    three_far = hop(after(three, vec), 1, PLANE_FIRST)
    near, near_far, vec, vec_far, two, two_far, three = sync(
        near, near_far, vec, vec_far, two, two_far, three
    )

    near = join(near, near_far)
    near_far = hop(near, 3)
    near_swap = swap_cores(near)
    vec = vec + vec_far
    vec_far = hop(vec, 2, same)
    two = join(two, two_far)
    two_far = hop(two, 1)
    near_far, near_swap, vec, vec_far, two, two_far, three, three_far = sync(
        near_far, near_swap, vec, vec_far, two, two_far, three, three_far
    )

    near_far_swap = swap_cores(near_far)
    vec = vec + vec_far
    vec_far = hop(vec, 3, same)
    two = join(two, two_far)
    two_far = hop(two, 2)
    three = join(three, three_far)
    three_far = hop(three, 2, PLANE_FIRST)
    vec, near_far_swap, two, three = sync(vec + vec_far, near_far_swap, two, three)
    vec = jnp.pad(vec.astype(WIDE), ((0, 16 - vec.shape[0]), (0, 0)))
    pieces = (near, near_far, near_swap, near_far_swap)

    def go(group, tick, before):
        return attend(
            group, after(scal, tick), page, vec, sines, cosines, encoded, pieces, before
        )

    kept = go(0, two, [])
    two, two_far, three, three_far, *kept = sync(two, two_far, three, three_far, *kept)

    two = join(two, two_far)
    two_far = hop(two, 3)
    three = join(three, three_far)
    two_swap = swap_cores(two)
    three_swap = swap_cores(three)
    kept = go(1, three, kept)
    two_far, two_swap, three_swap, *kept = sync(two_far, two_swap, three_swap, *kept)

    two_far_swap = swap_cores(two_far)
    three_far = hop(after(three, two_far), 3, PLANE_FIRST)
    two_pieces = (two, two_far, two_swap, two_far_swap)
    norm_low, xh1, r1, act, slope = open_ffn(scal, page, vec, kept[3], two_pieces)
    three_far, r1 = sync(three_far, r1)

    three_pieces = (three, three_far, three_swap, swap_cores(three_far))
    page_out, dh1, dctx, *sent = feed(
        scal,
        cotangent[0],
        vec,
        kept[3],
        (act, slope, norm_low, xh1, r1),
        two_pieces,
        three_pieces,
    )
    two_sent, three_sent = sent[:3], sent[3:]

    three_swap, two_swap, three_low, two_low, mark = sync(
        swap_cores(three_sent[2]), swap_cores(two_sent[2]), three_sent[1], two_sent[1], scal
    )
    three_high = add_up([three_sent[0][8:], three_swap])
    three_far = hop(three_high, 3, DEPTH_FIRST)
    two_high = add_up([two_sent[0][8:], two_swap])
    two_far = hop(two_high, 3)
    three_low = swap_cores(three_low)
    two_low = swap_cores(two_low)

    def undo(group, tick):
        return unattend(
            group,
            after(scal, tick),
            page,
            sines,
            cosines,
            encoded,
            *kept[:3],
            dctx,
            kept[4],
            kept[5],
        )

    def beside(left, right):
        return jnp.concatenate([left, right], axis=2)

    back = [undo(0, mark)]
    two_far, three_low, two_low, mark, *one_sent = sync(
        two_far, three_low, two_low, back[0][0], *back[0][3:]
    )

    two_terms, two_high = halve([two_sent[0][:8], two_low, two_far])
    two_far = hop(two_high, 2)
    one_swap = swap_cores(one_sent[2])
    one_low = swap_cores(one_sent[1])
    back.append(undo(1, mark))
    two_far, three_far, one_swap, one_low, mark, *next_sent = sync(
        two_far, three_far, one_swap, one_low, back[1][0], *back[1][3:]
    )

    next_swap = swap_cores(next_sent[2])
    three_terms, three_high = halve([three_sent[0][:8], three_low, three_far])
    three_far = hop(three_high, 2, DEPTH_FIRST)
    two_terms, two_high = halve(two_terms + [two_far])
    two_far = hop(two_high, 1)
    next_swap, next_low, mark, three_high, two_high = sync(
        next_swap, next_sent[1], mark, three_high, two_high
    )
    one_high = beside(
        add_up([one_sent[0][8:], one_swap]), add_up([next_sent[0][8:], next_swap])
    )
    one_far = hop(one_high, 3)
    next_low = swap_cores(next_low)
    back.append(undo(2, mark))
    two_far, three_far, one_far, next_low, *end_sent = sync(
        two_far, three_far, one_far, next_low, *back[2][3:]
    )

    end_high = add_up([end_sent[0][8:], swap_cores(end_sent[2])])
    end_far = hop(end_high, 3)
    end_low, one_far, three_far, two_far, mark = sync(
        end_sent[1], one_far, three_far, two_far, end_high
    )
    end_low = swap_cores(end_low)
    two_terms, two_high = halve(two_terms + [two_far])
    two_far = hop(two_high, 0)
    one_terms = [beside(one_sent[0][:8], next_sent[0][:8]), beside(one_low, next_low), one_far]
    one_terms, one_high = halve(one_terms)
    one_far = hop(one_high, 2)
    three_terms, three_high = halve(three_terms + [three_far])
    three_far = hop(three_high, 1, DEPTH_FIRST)
    end_far, end_low, one_far, three_far, two_far, mark = sync(
        end_far, end_low, one_far, three_far, two_far, mark
    )

    end_terms, end_high = halve([end_sent[0][:8], end_low, end_far])
    end_far = hop(end_high, 2)
    one_terms, one_high = halve(one_terms + [one_far])
    one_far = hop(one_high, 1)
    three_terms, three_high = halve(three_terms + [three_far])
    three_far = hop(three_high, 0, DEPTH_FIRST)
    two_mine = add_up(two_terms + [two_far])[0]
    two_other = swap_cores(two_mine)
    token_grad = input_grad(
        after(dh1, mark, two_mine), [part for b in back for part in b[:3]], kept[5]
    )
    end_far, one_far, three_far, two_other, token_grad = sync(
        end_far, one_far, three_far, two_other, token_grad
    )

    end_terms, end_high = halve(end_terms + [end_far])
    end_far = hop(end_high, 1)
    one_terms, one_high = halve(one_terms + [one_far])
    one_far = hop(one_high, 0)
    three_mine = add_up(three_terms + [three_far])[0]
    three_other = swap_cores(three_mine)
    two_sum = by_half(core, (two_mine, two_other))
    up_sum = jnp.concatenate([two_sum[0][:, 384:], two_sum[1][:, 384:]], axis=1)
    up_next = adam_update(up_weight, up_first, up_second, up_sum, UP_RATE, WEIGHT_DECAY)
    end_far, one_far, three_other, up_copy, up_new, up_first_new, up_second_new = sync(
        end_far, one_far, three_other, up_next[0].astype(LOW), *up_next
    )

    end_terms, end_high = halve(end_terms + [end_far])
    end_far = hop(end_high, 0)
    three_sum = by_half(core, (three_mine, three_other))
    down_next = adam_update(
        down_weight,
        down_first,
        down_second,
        jnp.concatenate([part[:96] for part in three_sum]),
        DOWN_RATE,
        WEIGHT_DECAY,
    )
    one_mine = add_up(one_terms + [one_far])[0]
    end_far, one_mine, down_copy, down_new, down_first_new, down_second_new = sync(
        end_far, one_mine, down_next[0].astype(LOW), *down_next
    )

    one_mine = jnp.concatenate([one_mine, add_up(end_terms + [end_far])[0]], axis=1)
    one_sum = by_half(core, (one_mine, swap_cores(one_mine)))
    vec_grad = jnp.concatenate(
        [
            three_sum[0][96:100],
            one_sum[0][96:97],
            one_sum[1][96:97],
            three_sum[0][100:101],
            three_sum[1][96:101],
        ]
    )
    vec_sum = lax.dynamic_slice(
        vec_grad, (jnp.int32(0), chip * vectors.shape[1]), vectors.shape
    )
    attn_sum = jnp.stack(
        [
            one_sum[0][:48],
            one_sum[0][48:96],
            one_sum[1][:48],
            jnp.concatenate([two_sum[0][:, :384], two_sum[1][:, :384]], axis=1),
            one_sum[1][48:96],
        ]
    )
    layer_out, token_grad = page_out[None], token_grad[None]
    attn_rates = jnp.array(ATTN_RATES, jnp.float32)[:, None, None]
    attn_new, attn_first_new, attn_second_new = adam_update(
        attn_weight, attn_first, attn_second, attn_sum, attn_rates, WEIGHT_DECAY
    )
    vectors_new, vector_first_new, vector_second_new = adam_update(
        vectors, vector_first, vector_second, vec_sum, VECTOR_RATE, 0.0
    )
    return (
        layer_out,
        token_grad,
        attn_new,
        up_new,
        down_new,
        vectors_new,
        attn_first_new,
        up_first_new,
        down_first_new,
        vector_first_new,
        attn_second_new,
        up_second_new,
        down_second_new,
        vector_second_new,
        attn_new.astype(jnp.bfloat16),
        up_copy,
        down_copy,
        vectors_new.astype(jnp.bfloat16),
    )


def local_general(
    tokens,
    boxes,
    lengths,
    cotangent,
    attn_weight,
    up_weight,
    down_weight,
    vectors,
    attn_first,
    up_first,
    down_first,
    vector_first,
    attn_second,
    up_second,
    down_second,
    vector_second,
):
    lowered = (
        attn_weight.astype(jnp.bfloat16),
        up_weight.astype(jnp.bfloat16),
        down_weight.astype(jnp.bfloat16),
        vectors.astype(jnp.bfloat16),
    )
    gathered = (
        lax.all_gather(lowered[0], "fsdp", axis=1, tiled=True),
        lax.all_gather(lowered[1], "fsdp", axis=0, tiled=True),
        lax.all_gather(lowered[2], "fsdp", axis=0, tiled=True),
        lax.all_gather(lowered[3], "fsdp", axis=1, tiled=True),
    )

    def forward_step(carry, page):
        token_row_block, box_rows, page_length = page
        return (carry, forward_page(gathered, token_row_block, box_rows, page_length))

    _, (layer_out, saved_all) = lax.scan(forward_step, None, (tokens, boxes, lengths))
    backward_weights = (
        lax.all_gather(lowered[0], "fsdp", axis=1, tiled=True),
        lax.all_gather(lowered[1], "fsdp", axis=0, tiled=True),
        lax.all_gather(lowered[2], "fsdp", axis=0, tiled=True),
        lax.all_gather(lowered[3], "fsdp", axis=1, tiled=True),
    )
    model_width = gathered[0].shape[2]
    ffn_width = gathered[1].shape[1]
    zero_grads = (
        jnp.zeros((5, model_width, model_width), jnp.float32),
        jnp.zeros((model_width, ffn_width), jnp.float32),
        jnp.zeros((ffn_width, model_width), jnp.float32),
        jnp.zeros(gathered[3].shape, jnp.float32),
    )

    def backward_step(totals, page):
        token_row_block, box_rows, page_length, upstream, saved_state = page
        token_grad, grads = backward_page(
            backward_weights, token_row_block, box_rows, page_length, upstream, saved_state
        )
        return (jax.tree.map(jnp.add, totals, grads), token_grad)

    totals, token_grad = lax.scan(
        backward_step, zero_grads, (tokens, boxes, lengths, cotangent, saved_all)
    )
    shards = (
        lax.psum_scatter(totals[0], "fsdp", scatter_dimension=1, tiled=True),
        lax.psum_scatter(totals[1], "fsdp", scatter_dimension=0, tiled=True),
        lax.psum_scatter(totals[2], "fsdp", scatter_dimension=0, tiled=True),
        lax.psum_scatter(totals[3], "fsdp", scatter_dimension=1, tiled=True),
    )
    reduced = (
        lax.psum(shards[0].astype(jnp.bfloat16), "rep").astype(jnp.float32),
        lax.psum(shards[1].astype(jnp.bfloat16), "rep").astype(jnp.float32),
        lax.psum(shards[2].astype(jnp.bfloat16), "rep").astype(jnp.float32),
        lax.psum(shards[3].astype(jnp.bfloat16), "rep").astype(jnp.float32),
    )
    attn_rates = jnp.array(ATTN_RATES, jnp.float32)[:, None, None]
    attn_new, attn_first_new, attn_second_new = adam_update(
        attn_weight, attn_first, attn_second, reduced[0], attn_rates, WEIGHT_DECAY
    )
    up_new, up_first_new, up_second_new = adam_update(
        up_weight, up_first, up_second, reduced[1], UP_RATE, WEIGHT_DECAY
    )
    down_new, down_first_new, down_second_new = adam_update(
        down_weight, down_first, down_second, reduced[2], DOWN_RATE, WEIGHT_DECAY
    )
    vectors_new, vector_first_new, vector_second_new = adam_update(
        vectors, vector_first, vector_second, reduced[3], VECTOR_RATE, 0.0
    )
    return (
        layer_out,
        token_grad,
        attn_new,
        up_new,
        down_new,
        vectors_new,
        attn_first_new,
        up_first_new,
        down_first_new,
        vector_first_new,
        attn_second_new,
        up_second_new,
        down_second_new,
        vector_second_new,
        attn_new.astype(jnp.bfloat16),
        up_new.astype(jnp.bfloat16),
        down_new.astype(jnp.bfloat16),
        vectors_new.astype(jnp.bfloat16),
    )


def solution(mesh):
    blocked = mesh.shape["fsdp"] == 16 and mesh.shape["rep"] == 2
    return jax.shard_map(
        local if blocked else local_general,
        mesh=mesh,
        in_specs=(
            P(("fsdp", "rep"), None, None),
            P(("fsdp", "rep"), None, None),
            P(("fsdp", "rep")),
            P(("fsdp", "rep"), None, None),
            P(None, "fsdp", None),
            P("fsdp", None),
            P("fsdp", None),
            P(None, "fsdp"),
            P(None, "fsdp", None),
            P("fsdp", None),
            P("fsdp", None),
            P(None, "fsdp"),
            P(None, "fsdp", None),
            P("fsdp", None),
            P("fsdp", None),
            P(None, "fsdp"),
        ),
        out_specs=(
            P(("fsdp", "rep"), None, None),
            P(("fsdp", "rep"), None, None),
            P(None, "fsdp", None),
            P("fsdp", None),
            P("fsdp", None),
            P(None, "fsdp"),
            P(None, "fsdp", None),
            P("fsdp", None),
            P("fsdp", None),
            P(None, "fsdp"),
            P(None, "fsdp", None),
            P("fsdp", None),
            P("fsdp", None),
            P(None, "fsdp"),
            P(None, "fsdp", None),
            P("fsdp", None),
            P("fsdp", None),
            P(None, "fsdp"),
        ),
        check_vma=False,
    )
```

```python
from functools import partial
import math

import jax
import jax.numpy as jnp
from jax import lax
from jax.experimental import pallas as pl
from jax.experimental.pallas import tpu as pltpu
from jax.sharding import PartitionSpec as P

HEADS = 12
HEAD_DIM = 64
STEP = 7


EPS_NORM = 1e-12
EPS_ADAM = 1e-08
DECAY = 0.5
MASK_FILL = -1e30
WEIGHT_DECAY = 0.01
ATTN_RATES = (0.04, 0.04, 0.04, 0.2, 0.04)
UP_RATE = 0.04
DOWN_RATE = 0.02
VECTOR_RATE = 0.3


def contract(left_op, right_op, left_dim, right_dim):
    return lax.dot_general(
        left_op,
        right_op,
        (((left_dim,), (right_dim,)), ((), ())),
        preferred_element_type=jnp.float32,
    )


def layer_norm(hidden, gain_row, shift_row):
    center = hidden - jnp.mean(hidden, axis=-1, keepdims=True)
    spread = jnp.mean(center * center, axis=-1, keepdims=True)
    return center * lax.rsqrt(spread + EPS_NORM) * gain_row + shift_row


def box_tables(box_rows, model_width):
    quarter = model_width // 4
    frequency = jnp.exp(jnp.arange(quarter).astype(jnp.float32) * (-math.log(10000.0) / quarter))
    angles = box_rows.astype(jnp.float32)[:, :, None] * frequency
    return (jnp.sin(angles), jnp.cos(angles))


def encode(sine_rows, cosine_rows):
    return jnp.concatenate([sine_rows[0], cosine_rows[0], sine_rows[1], cosine_rows[1]], axis=-1)


def rotate(pos_table, sine_rows, cosine_rows):
    quarter = sine_rows.shape[-1]
    pieces = []
    for coord in range(2):
        sine_part = pos_table[..., 2 * coord * quarter : (2 * coord + 1) * quarter]
        cosine_part = pos_table[..., (2 * coord + 1) * quarter : (2 * coord + 2) * quarter]
        pieces.append(cosine_part * sine_rows[coord] - sine_part * cosine_rows[coord])
        pieces.append(sine_part * sine_rows[coord] + cosine_part * cosine_rows[coord])
    return jnp.concatenate(pieces, axis=-1)


def scores(query_rows, key_rows, left_rows, encoded, page_live):
    text_part = jnp.einsum("ihd,jhd->hij", query_rows, key_rows, preferred_element_type=jnp.float32)
    place_part = jnp.einsum("hie,je->hij", left_rows, encoded, preferred_element_type=jnp.float32)
    score_rows = (text_part + place_part) * HEAD_DIM ** (-0.5)
    return jnp.where(page_live[None, None, :], score_rows, MASK_FILL)


def forward_page(weights, token_row_block, box_rows, page_length):
    attention_matrices, up_mat, down_mat, vector_rows = weights
    row_count, model_width = token_row_block.shape
    vector_f32 = vector_rows.astype(jnp.float32)
    page_live = jnp.arange(row_count) < page_length
    projected_rows = jnp.einsum(
        "tb,mby->mty", token_row_block, attention_matrices[:3], preferred_element_type=jnp.float32
    )
    query_rows = (
        (projected_rows[0] + vector_f32[4]).astype(jnp.bfloat16).reshape(row_count, HEADS, HEAD_DIM)
    )
    key_rows = projected_rows[1].astype(jnp.bfloat16).reshape(row_count, HEADS, HEAD_DIM)
    value_rows = (
        (projected_rows[2] + vector_f32[5]).astype(jnp.bfloat16).reshape(row_count, HEADS, HEAD_DIM)
    )
    sine_rows, cosine_rows = box_tables(box_rows, model_width)
    encoded = encode(sine_rows, cosine_rows).astype(jnp.bfloat16)
    rel_heads = attention_matrices[4].reshape(model_width, HEADS, HEAD_DIM)
    pos_table = jnp.einsum(
        "ihd,ehd->hie", query_rows, rel_heads, preferred_element_type=jnp.float32
    )
    left_rows = rotate(pos_table, sine_rows, cosine_rows).astype(jnp.bfloat16)
    score_rows = scores(query_rows, key_rows, left_rows, encoded, page_live)
    row_top = jnp.max(score_rows, axis=-1, keepdims=True)
    exponent = jnp.exp(score_rows - row_top)
    row_total = jnp.sum(exponent, axis=-1, keepdims=True)
    prob_low = (exponent / row_total).astype(jnp.bfloat16)
    logsum = row_top + jnp.log(row_total)
    mixed_rows = jnp.einsum(
        "hij,jhd->ihd", prob_low, value_rows, preferred_element_type=jnp.float32
    )
    context = mixed_rows.reshape(row_count, model_width).astype(jnp.bfloat16)
    attn_out = (
        jnp.dot(context, attention_matrices[3], preferred_element_type=jnp.float32) + vector_f32[6]
    )
    first_sum = token_row_block.astype(jnp.float32) + attn_out
    normed = layer_norm(first_sum, vector_f32[0], vector_f32[1])
    pre_act = jnp.dot(
        normed.astype(jnp.bfloat16), up_mat, preferred_element_type=jnp.float32
    ) + vector_f32[8:].reshape(-1)
    act_low = jax.nn.gelu(pre_act, approximate=False).astype(jnp.bfloat16)
    second_sum = normed + (
        jnp.dot(act_low, down_mat, preferred_element_type=jnp.float32) + vector_f32[7]
    )
    page_out = (layer_norm(second_sum, vector_f32[2], vector_f32[3]) * page_live[:, None]).astype(
        jnp.bfloat16
    )
    saved_state = (
        query_rows,
        key_rows,
        value_rows,
        left_rows,
        logsum,
        context,
        first_sum,
        pre_act,
        act_low,
        second_sum,
    )
    return (page_out, saved_state)


def backward_page(weights, token_row_block, box_rows, page_length, upstream, saved_state):
    attention_matrices, up_mat, down_mat, vector_rows = weights
    (
        query_rows,
        key_rows,
        value_rows,
        left_rows,
        logsum,
        context,
        first_sum,
        pre_act,
        act_low,
        second_sum,
    ) = saved_state
    row_count, model_width = token_row_block.shape
    vector_f32 = vector_rows.astype(jnp.float32)
    page_live = jnp.arange(row_count) < page_length
    sine_rows, cosine_rows = box_tables(box_rows, model_width)
    encoded = encode(sine_rows, cosine_rows).astype(jnp.bfloat16)
    out_grad = upstream.astype(jnp.float32) * page_live[:, None]
    _, pull_second = jax.vjp(layer_norm, second_sum, vector_f32[2], vector_f32[3])
    second_grad, gain_two, shift_two = pull_second(out_grad)
    ffn_grad = second_grad.astype(jnp.bfloat16)
    down_grad = contract(act_low, ffn_grad, 0, 0)
    act_grad = contract(ffn_grad, down_mat, 1, 1)
    _, pull_gelu = jax.vjp(partial(jax.nn.gelu, approximate=False), pre_act)
    pre_grad = pull_gelu(act_grad)[0].astype(jnp.bfloat16)
    normed, pull_first = jax.vjp(layer_norm, first_sum, vector_f32[0], vector_f32[1])
    up_grad = contract(normed.astype(jnp.bfloat16), pre_grad, 0, 0)
    normed_grad = contract(pre_grad, up_mat, 1, 1) + second_grad
    first_grad, gain_one, shift_one = pull_first(normed_grad)
    attn_grad = first_grad.astype(jnp.bfloat16)
    out_mat_grad = contract(context, attn_grad, 0, 0)
    context_grad = (
        contract(attn_grad, attention_matrices[3], 1, 1)
        .astype(jnp.bfloat16)
        .reshape(row_count, HEADS, HEAD_DIM)
    )
    score_rows = scores(query_rows, key_rows, left_rows, encoded, page_live)
    prob_rows = jnp.exp(score_rows - logsum)
    value_grad = jnp.einsum(
        "hij,ihd->jhd",
        prob_rows.astype(jnp.bfloat16),
        context_grad,
        preferred_element_type=jnp.float32,
    ).astype(jnp.bfloat16)
    prob_grad = jnp.einsum(
        "ihd,jhd->hij", context_grad, value_rows, preferred_element_type=jnp.float32
    )
    score_grad = (
        prob_rows * (prob_grad - jnp.sum(prob_rows * prob_grad, axis=-1, keepdims=True))
    ).astype(jnp.bfloat16)
    score_scale = HEAD_DIM ** (-0.5)
    left_grad = (
        jnp.einsum("hij,je->hie", score_grad, encoded, preferred_element_type=jnp.float32)
        * score_scale
    )
    table_grad = rotate(left_grad, sine_rows, cosine_rows).astype(jnp.bfloat16)
    rel_heads = attention_matrices[4].reshape(model_width, HEADS, HEAD_DIM)
    rel_grad = jnp.einsum(
        "hie,ihd->ehd", table_grad, query_rows, preferred_element_type=jnp.float32
    ).reshape(model_width, model_width)
    query_grad = (
        jnp.einsum("hij,jhd->ihd", score_grad, key_rows, preferred_element_type=jnp.float32)
        * score_scale
    )
    query_grad = query_grad + jnp.einsum(
        "hie,ehd->ihd", table_grad, rel_heads, preferred_element_type=jnp.float32
    )
    key_grad = (
        jnp.einsum("hij,ihd->jhd", score_grad, query_rows, preferred_element_type=jnp.float32)
        * score_scale
    )
    stacked_layers = jnp.stack(
        [
            query_grad.astype(jnp.bfloat16).reshape(row_count, model_width),
            key_grad.astype(jnp.bfloat16).reshape(row_count, model_width),
            value_grad.reshape(row_count, model_width),
        ]
    )
    projection_gradient = jnp.einsum(
        "cg,yca->yga", token_row_block, stacked_layers, preferred_element_type=jnp.float32
    )
    token_grad = first_grad + jnp.einsum(
        "skl,scl->kc", stacked_layers, attention_matrices[:3], preferred_element_type=jnp.float32
    )
    column_sums = jnp.sum(stacked_layers.astype(jnp.float32), axis=1)
    attn_grads = jnp.concatenate([projection_gradient, out_mat_grad[None], rel_grad[None]], axis=0)
    small_rows = jnp.stack(
        [
            gain_one,
            shift_one,
            gain_two,
            shift_two,
            column_sums[0],
            column_sums[2],
            jnp.sum(attn_grad.astype(jnp.float32), axis=0),
            jnp.sum(ffn_grad.astype(jnp.float32), axis=0),
        ]
    )
    up_bias_rows = jnp.sum(pre_grad.astype(jnp.float32), axis=0).reshape(-1, model_width)
    vector_grad = jnp.concatenate([small_rows, up_bias_rows], axis=0)
    return (token_grad, (attn_grads, up_grad, down_grad, vector_grad))


def adam_update(weight, first, second, grad, rate, decay_weight):
    first_new = DECAY * first + (1.0 - DECAY) * grad
    second_new = DECAY * second + (1.0 - DECAY) * grad * grad
    correction = 1.0 - DECAY**STEP
    direction = first_new / correction / (jnp.sqrt(second_new / correction) + EPS_ADAM)
    return (weight - rate * (direction + decay_weight * weight), first_new, second_new)


AXES = ("fsdp", "rep")
ORDERS = ((8, 4, 2, 1), (8, 4, 1, 2))
PLANE_FIRST = ((1, 8, 4, 2), (2, 8, 4, 1))
DEPTH_FIRST = ((8, 2, 1, 4), (8, 1, 2, 4))
PLAIN_AT, DEPTH_AT, PLANE_AT = 32, 96, 64
LOW = jnp.bfloat16
WIDE = jnp.float32
CHUNK = 256
SLAB = 128
FEED_VMEM_BYTES = 58 * 1024 * 1024
OPEN_VMEM_BYTES = 28 * 1024 * 1024
ATTN_VMEM_BYTES = 28 * 1024 * 1024
CORE_AT, LENGTH_AT = 128, 129


def mask_table(order):
    masks = [0]
    for bit in order:
        masks = masks + [bit ^ mask for mask in masks]
    return masks


CORE_PAIRS = [(chip * 2 + core, chip * 2 + 1 - core) for chip in range(16) for core in range(2)]


def place_of(mask, order):
    place = 0
    for bit_at, bit in enumerate(order):
        place = place + jnp.where((mask & bit) != 0, 1 << bit_at, 0)
    return place


def block_scalars(chip, core, length):
    rows, lane = [], jnp.arange(16, dtype=jnp.int32)
    blocks = [jnp.array(mask_table(order), jnp.int32) ^ chip for order in ORDERS]
    places = [place_of(lane ^ chip, order) for order in ORDERS]
    plane_blocks = [jnp.array(mask_table(order), jnp.int32) ^ chip for order in PLANE_FIRST]
    depth_places = [place_of(lane ^ chip, order) for order in DEPTH_FIRST]
    for pair in (blocks, places, plane_blocks, depth_places):
        rows.append(jnp.where(core == 0, pair[0], pair[1]))
        rows.append(jnp.where(core == 0, pair[1], pair[0]))
    last = jnp.where(lane == 0, core, jnp.where(lane == 1, length, 0))
    return jnp.stack(rows + [last]).astype(jnp.int32).reshape(-1)


def after(value, *others):
    return lax.optimization_barrier((value, *others))[0]


def sync(*values):
    return lax.optimization_barrier(values)


def swap_cores(block):
    return lax.ppermute(block, AXES, CORE_PAIRS)


def hop(held, step, orders=ORDERS):
    pairs = [
        (chip * 2 + core, (chip ^ orders[core][step]) * 2 + core)
        for chip in range(16)
        for core in range(2)
    ]
    return lax.ppermute(held, AXES, pairs)


def join(held, arrived):
    return jnp.concatenate([held, arrived], axis=0)


def add_up(terms):
    total_sum = terms[0].astype(WIDE)
    for term in terms[1:]:
        total_sum = total_sum + term.astype(WIDE)
    return total_sum.astype(terms[0].dtype)


def halve(terms):
    half = terms[0].shape[0] // 2
    return [term[:half] for term in terms], add_up([term[half:] for term in terms])


def by_half(core, sums):
    mine, other = sums
    first = jnp.where(core == 0, mine, other)
    second = jnp.where(core == 0, other, mine)
    return first.astype(WIDE), second.astype(WIDE)


def dot(left_op, right_op, left_dim, right_dim):
    return lax.dot_general(
        left_op,
        right_op,
        (((left_dim,), (right_dim,)), ((), ())),
        preferred_element_type=WIDE,
    )


def each(count, size, body, flat=False):
    def step(index, carry):
        body(pl.ds(pl.multiple_of(index * size, size), size))
        return carry

    if flat:
        for index in range(count // size):
            body(pl.ds(index * size, size))
    else:
        lax.fori_loop(0, count // size, step, 0)


def block_at(index):
    return pl.ds(pl.multiple_of(index * 48, 16), 48)


def turned(block):
    return (block & 3) | ((block & 4) << 1) | ((block & 8) >> 1)


def start_copies(make, count):
    def start(place, carry):
        for copy in make(place):
            copy.start()
        return carry

    lax.fori_loop(0, count, start, 0)


def wait_for(buffer, sem):
    pltpu.make_async_copy(buffer, buffer, sem).wait()


def sources(scal, pieces):
    core = scal[CORE_AT]
    bases = (0, 8, 16, 24)
    halves = (core, core, 1 - core, 1 - core)
    return [(piece, base, half) for piece, base, half in zip(pieces, bases, halves, strict=True)]


def attn_copies(scal, pieces, lanes, mats, spot, sem, place):
    copies = []
    for source, base, half in sources(scal, pieces):
        block = scal[base + place]
        for part in range(2):
            row = block if part == 0 else jnp.where(half == 1, turned(block), block)
            copies.append(
                pltpu.make_async_copy(
                    source.at[place, pl.ds(48 * part, 48), lanes],
                    mats.at[2 * half + part, block_at(row), spot],
                    sem,
                )
            )
    return copies


def head_masks(dtype):
    lane = lax.broadcasted_iota(jnp.int32, (1, 128), 1)
    first = jnp.where(lane < 64, 1.0, 0.0)
    return (first.astype(dtype), (1.0 - first).astype(dtype))


def attend_kernel(
    group,
    scal,
    tokens,
    vec,
    sines,
    cosines,
    *refs,
):
    pieces, refs = refs[:4], refs[4:] if group == 0 else refs[10:]
    q_out, k_out, v_out, ctx_out, prob_out, mats_out = refs[:6]
    mats, right, sem, sem_out = refs[6:]
    pair = pl.program_id(0)
    width = tokens.shape[1]
    rows = tokens.shape[0]

    @pl.when(pair == 0)
    def _():
        cols = mats.shape[2]
        lane_at = pl.ds(group * cols, cols)
        start_copies(partial(attn_copies, scal, pieces, lane_at, mats, pl.ds(0, cols), sem), 8)
        wait_for(mats, sem)
        pltpu.make_async_copy(mats, mats_out.at[:, :, lane_at], sem_out).start()
        right[:, : width // 2] = sines[...].astype(LOW)
        right[:, width // 2 : width] = cosines[...].astype(LOW)

        def project(at):
            x = tokens[at, :]
            q_out[at, :] = (dot(x, mats[0], 1, 0) + vec[4:5, :]).astype(LOW)
            k_out[at, :] = dot(x, mats[1], 1, 0).astype(LOW)
            v_out[at, :] = (dot(x, mats[2], 1, 0) + vec[5:6, :]).astype(LOW)

        each(rows, CHUNK, project)

    lanes = pl.ds(pl.multiple_of(pair * 128, 128), 128)
    right[:, width:] = k_out[:, lanes]
    rel = mats[3, :, lanes]
    live = lax.broadcasted_iota(jnp.int32, (1, rows), 1) < scal[LENGTH_AT]
    half = width // 2

    def score(at):
        q_pair = q_out[at, :] if q_out.shape[1] == 128 else q_out[at, lanes]
        sin, cos = sines[at, :], cosines[at, :]
        mixed = []
        for head, mask in enumerate(head_masks(LOW)):
            q_head = q_pair * mask
            table = dot(q_head, rel, 1, 1)
            us, uc = table[:, :half], table[:, half:]
            left = jnp.concatenate(
                [(uc * sin - us * cos).astype(LOW), (us * sin + uc * cos).astype(LOW), q_head], axis=1
            )
            s = dot(left, right[...], 1, 1) * HEAD_DIM ** (-0.5)
            s = jnp.where(live, s, MASK_FILL)
            top = jnp.max(s, axis=-1, keepdims=True)
            e = jnp.exp(s - top)
            prob = (e * (1.0 / jnp.sum(e, axis=-1, keepdims=True))).astype(LOW)
            prob_out[head, at, :] = prob
            mixed.append(dot(prob, v_out[:, lanes], 1, 0))
        masks = head_masks(WIDE)
        ctx_out[at, :] = (mixed[0] * masks[0] + mixed[1] * masks[1]).astype(LOW)

    each(rows, rows, score, True)

    @pl.when(pair == pl.num_programs(0) - 1)
    def _():
        wait_for(mats, sem_out)


def any_space():
    return pl.BlockSpec(memory_space=pl.ANY)


def whole(shape):
    return pl.BlockSpec(shape, lambda *_: (0,) * len(shape))


def attend(group, scal, tokens, vec, sines, cosines, pieces, before):
    rows, width = tokens.shape
    pairs, cols = PAIRS, 128 * PAIRS
    low = jax.ShapeDtypeStruct((rows, width), LOW)
    prob = pltpu.HBM((width // HEAD_DIM, rows, rows), LOW)
    mats = jax.ShapeDtypeStruct((4, width, width), LOW)
    return pl.pallas_call(
        partial(attend_kernel, group),
        out_shape=(low, low, low, low, prob, mats),
        grid_spec=pltpu.PrefetchScalarGridSpec(
            num_scalar_prefetch=1,
            grid=(pairs,),
            in_specs=[
                whole((rows, width)),
                pl.BlockSpec((vec.shape[0], cols), lambda p, _: (0, group)),
                whole((rows, width // 2)),
                whole((rows, width // 2)),
            ]
            + [any_space()] * (4 + len(before)),
            out_specs=[pl.BlockSpec((rows, cols), lambda p, _: (0, group))] * 3
            + [
                pl.BlockSpec((rows, 128), lambda p, _: (0, group * pairs + p)),
                pl.BlockSpec((2, rows, rows), lambda p, _: (group * pairs + p, 0, 0)),
                any_space(),
            ],
            scratch_shapes=[
                pltpu.VMEM((4, width, cols), LOW),
                pltpu.VMEM((rows, width + 128), LOW),
                pltpu.SemaphoreType.DMA,
                pltpu.SemaphoreType.DMA,
            ],
        ),
        compiler_params=pltpu.CompilerParams(
            dimension_semantics=("arbitrary",), vmem_limit_bytes=ATTN_VMEM_BYTES
        ),
        cost_estimate=pl.CostEstimate(
            flops=pairs * 2 * rows * width * 3072, transcendentals=0, bytes_accessed=24 * 1024 * 1024
        ),
        input_output_aliases={9 + at: at for at in range(len(before))},
        name="attend",
    )(scal, tokens, vec, sines, cosines, *pieces, *before)


CDF_POLY = (
    -0.020695917308330536,
    0.09534552693367004,
    -0.15029412508010864,
    0.07120334357023239,
    -0.011180647648870945,
    0.05997580662369728,
    0.08762594312429428,
    0.11413583159446716,
    0.12694157660007477,
    0.12694266438484192,
)
CDF_SLOPE = 0.45 / math.sqrt(2.0)


def gelu_pair(x):
    size = jnp.abs(x)
    t = 1.0 / (1.0 + CDF_SLOPE * size)
    bell = jnp.exp2(x * x * (-0.5 / math.log(2.0)))
    poly = CDF_POLY[0]
    for value in CDF_POLY[1:]:
        poly = poly * t + value
    tail = poly * t * bell
    cdf = jnp.where(x < 0.0, tail, 1.0 - tail)
    return x * cdf, cdf + x * bell * (1.0 / math.sqrt(2.0 * math.pi))


def moments(z):
    center = z - jnp.mean(z, axis=-1, keepdims=True)
    r = lax.rsqrt(jnp.mean(center * center, axis=-1, keepdims=True) + EPS_NORM)
    return center * r, r


def norm_back(grad, xh, r, gain):
    dxh = grad * gain
    return r * (
        dxh - jnp.mean(dxh, axis=-1, keepdims=True) - xh * jnp.mean(dxh * xh, axis=-1, keepdims=True)
    )


def total(values):
    return jnp.sum(values, axis=0, keepdims=True)


def out_copies(scal, pieces, out_mat, sem, place):
    return [
        pltpu.make_async_copy(
            source.at[place, :, pl.ds(0, 384)],
            out_mat.at[block_at(scal[base + place]), pl.ds(pl.multiple_of(half * 384, 128), 384)],
            sem,
        )
        for source, base, half in sources(scal, pieces)
    ]


def down_copies(scal, pieces, down_mat, sem, place):
    return [
        pltpu.make_async_copy(
            source.at[place],
            down_mat.at[pl.ds(pl.multiple_of(scal[PLANE_AT + base + place] * 192 + half * 96, 32), 96)],
            sem,
        )
        for source, base, half in sources(scal, pieces)
    ]


def per_core(scal, body):
    for core in range(2):

        @pl.when(scal[CORE_AT] == core)
        def _(core=core):
            body(core)


def send_block(scal, source, outs, side, block, cut, sem, table=PLAIN_AT):
    place = scal[table + 16 * side + block]
    if side == 0:
        pltpu.make_async_copy(source, cut(outs[0], place), sem).start()
        return
    for part in range(2):

        @pl.when(place // 8 == part)
        def _(part=part):
            pltpu.make_async_copy(source, cut(outs[1 + part], lax.rem(place, 8)), sem).start()


def block_shapes(rows, cols):
    return tuple(jax.ShapeDtypeStruct((count, rows, cols), LOW) for count in (16, 8, 8))


def up_fetch(scal, pieces, up_mat, sems, first):
    def fetch(core):
        for unit in range(4):
            near = 0 if unit // 2 == core else 2

            def start(place, carry, unit=unit, near=near):
                for index in (near, near + 1):
                    pltpu.make_async_copy(
                        pieces[index].at[place, :, pl.ds(384 + 768 * (unit % 2), 768)],
                        up_mat.at[unit, block_at(scal[8 * index + place])],
                        sems.at[first + unit],
                    ).start()
                return carry

            lax.fori_loop(0, 8, start, 0)

    per_core(scal, fetch)


def open_kernel(
    scal, tokens, vec, *refs
):
    ctx, pieces = refs[0], refs[1:5]
    norm_low, xh1, r1, act, slope, out_mat, up_mat, sem_in = refs[5:]
    step = pl.program_id(0)
    rows, width = tokens.shape

    @pl.when(step == 0)
    def _():
        start_copies(partial(out_copies, scal, pieces, out_mat, sem_in.at[0]), 8)
        up_fetch(scal, pieces, up_mat, sem_in, 1)
        wait_for(out_mat, sem_in.at[0])

        def first(at):
            attn = dot(ctx[at, :], out_mat[...], 1, 0) + vec[6:7, :]
            hat, r = moments(tokens[at, :].astype(WIDE) + attn)
            xh1[at, :] = hat
            r1[at, :] = jnp.broadcast_to(r, (r.shape[0], 128))
            norm_low[at, :] = (hat * vec[0:1, :] + vec[1:2, :]).astype(LOW)

        each(rows, CHUNK, first)

    wait_for(up_mat.at[step], sem_in.at[1 + step])

    bias = vec[pl.ds(8 + step, 1), :]
    spots = [pl.ds(CHUNK * index, CHUNK) for index in range(rows // CHUNK)]

    def front(at):
        return dot(norm_low[at, :], up_mat[step], 1, 0) + bias

    pre = front(spots[0])
    for index, at in enumerate(spots):
        ahead = front(spots[index + 1]) if index + 1 < len(spots) else None
        value, grad = gelu_pair(pre)
        act[0, at, :] = value.astype(LOW)
        slope[0, at, :] = grad
        pre = ahead


def open_ffn(scal, tokens, vec, ctx, two):
    rows, width = tokens.shape
    unit = pl.BlockSpec((1, rows, width), lambda j, _: (j, 0, 0))
    return pl.pallas_call(
        open_kernel,
        out_shape=(
            pltpu.HBM((rows, width), LOW),
            pltpu.HBM((rows, width), WIDE),
            pltpu.HBM((rows, 128), WIDE),
            pltpu.HBM((4, rows, width), LOW),
            pltpu.HBM((4, rows, width), WIDE),
        ),
        grid_spec=pltpu.PrefetchScalarGridSpec(
            num_scalar_prefetch=1,
            grid=(4,),
            in_specs=[whole((rows, width)), whole((16, width))]
            + [whole((rows, width))]
            + [any_space()] * 4,
            out_specs=[whole((rows, width))] * 2 + [whole((rows, 128)), unit, unit],
            scratch_shapes=[
                pltpu.VMEM((width, width), LOW),
                pltpu.VMEM((4, width, width), LOW),
                pltpu.SemaphoreType.DMA((5,)),
            ],
        ),
        compiler_params=pltpu.CompilerParams(
            dimension_semantics=("arbitrary",), vmem_limit_bytes=OPEN_VMEM_BYTES
        ),
        cost_estimate=pl.CostEstimate(
            flops=2 * rows * width * width * 9, transcendentals=0, bytes_accessed=18 * 1024 * 1024
        ),
        name="open_ffn",
    )(scal, tokens, vec, ctx, *two)


def feed_kernel(*refs):
    scal, cot, vec, ctx, act_in, slope_in, norm_in, xh_in, r_in = refs[:9]
    two_pieces, three_pieces = refs[9:13], refs[13:17]
    page_out, dh1_out, dctx_out, *outs = refs[17:26]
    two_outs, three_outs = outs[:3], outs[3:]
    (
        out_mat,
        up_mat,
        down_mat,
        norm_low,
        xh1,
        r1,
        act,
        slope,
        held,
        df,
        dpre,
        dattn,
        g_out,
        g_up,
        g_down,
        vec_out,
        vec_low,
        sem_in,
        sem_up,
        sem_down,
        sem_out,
        sem_page,
        sem_rows,
    ) = refs[26:]
    step = pl.program_id(0)
    rows, width = cot.shape
    length = scal[LENGTH_AT]

    @pl.when(step == 0)
    def _():
        start_copies(partial(down_copies, scal, three_pieces, down_mat, sem_in.at[0]), 8)
        for source, target, at in (
            (xh_in, xh1, 1),
            (act_in, act, 2),
            (norm_in, norm_low, 3),
            (r_in, r1, 4),
            (slope_in, slope, 5),
        ):
            pltpu.make_async_copy(source, target, sem_in.at[at]).start()
        up_fetch(scal, two_pieces, up_mat, sem_in, 6)
        start_copies(partial(out_copies, scal, two_pieces, out_mat, sem_in.at[10]), 8)
        vec_out[...] = jnp.zeros_like(vec_out)
        wait_for(xh1, sem_in.at[1])

        def prime(at):
            held[at, :] = xh1[at, :] * vec[0:1, :] + (vec[1:2, :] + vec[7:8, :])

        each(rows, SLAB, prime)
        wait_for(act, sem_in.at[2])
        wait_for(down_mat, sem_in.at[0])

    @pl.when(step < 4)
    def _():
        down_at = pl.ds(pl.multiple_of(step * width, width), width)
        held[...] += dot(act[step], down_mat[down_at, :], 1, 0)

    @pl.when(step == 3)
    def _():
        def second(at):
            hat, r = moments(held[at, :])
            place = lax.broadcasted_iota(jnp.int32, (SLAB, 1), 0) + at.start
            live = jnp.where(place < length, 1.0, 0.0)
            dattn[at, :] = ((hat * vec[2:3, :] + vec[3:4, :]) * live).astype(LOW)
            dy = cot[at, :].astype(WIDE) * live
            vec_out[2:3, :] += total(dy * hat)
            vec_out[3:4, :] += total(dy)
            dh2 = norm_back(dy, hat, r, vec[2:3, :])
            low = dh2.astype(LOW)
            df[at, :] = low
            vec_out[7:8, :] += total(low.astype(WIDE))
            held[at, :] = dh2

        each(rows, SLAB, second)
        pltpu.make_async_copy(dattn, page_out, sem_page).start()
        wait_for(slope, sem_in.at[5])
        wait_for(norm_low, sem_in.at[3])
        wait_for(r1, sem_in.at[4])
        wait_for(out_mat, sem_in.at[10])
        for unit in range(4):
            wait_for(up_mat.at[unit], sem_in.at[6 + unit])

    def send_up(slot, unit):
        at = pl.ds(pl.multiple_of(384 + 768 * lax.rem(unit, 2), 128), 768)
        for side in range(2):

            @pl.when((unit // 2 == scal[CORE_AT]) == (side == 0))
            def _(side=side):
                def body(block, carry):
                    send_block(
                        scal,
                        g_up.at[slot, block_at(block)],
                        two_outs,
                        side,
                        block,
                        lambda ref, place: ref.at[place, :, at],
                        sem_up.at[slot],
                    )
                    return carry

                lax.fori_loop(0, 16, body, 0)

    def send_down(slot, unit):
        def body(core):
            for part in range(8):
                send_block(
                    scal,
                    g_down.at[slot, pl.ds(96 * part, 96)],
                    three_outs,
                    (part % 2) ^ core,
                    4 * unit + part // 2,
                    lambda ref, place: ref.at[place, pl.ds(0, 96)],
                    sem_down.at[slot],
                    DEPTH_AT,
                )

        per_core(scal, body)

    def send_out():
        def on(core):
            def body(block, carry):
                for half in range(2):
                    send_block(
                        scal,
                        g_out.at[block_at(block), pl.ds(384 * half, 384)],
                        two_outs,
                        half ^ core,
                        block,
                        lambda ref, place: ref.at[place, :, pl.ds(0, 384)],
                        sem_out,
                    )
                return carry

            lax.fori_loop(0, 16, body, 0)

        per_core(scal, on)

    @pl.when(step >= 4)
    def _():
        unit = step - 4
        slot = lax.rem(unit, 2)
        down_at = pl.ds(pl.multiple_of(unit * width, width), width)

        @pl.when(unit >= 2)
        def _():
            wait_for(g_up.at[slot], sem_up.at[slot])
            wait_for(g_down.at[slot], sem_down.at[slot])

        def backward(at):
            grad = dot(df[at, :], down_mat[down_at, :], 1, 1) * slope[unit, at, :]
            low = grad.astype(LOW)
            dpre[at, :] = low
            vec_out[pl.ds(8 + unit, 1), :] += total(low.astype(WIDE))
            held[at, :] += dot(low, up_mat[unit], 1, 1)

        each(rows, rows, backward, True)

        def weights(at):
            g_down[slot, at, :] = dot(act[unit, :, at], df[...], 0, 0).astype(LOW)
            g_up[slot, at, :] = dot(norm_low[:, at], dpre[...], 0, 0).astype(LOW)

        each(width, width, weights, True)
        send_down(slot, unit)
        send_up(slot, unit)

    @pl.when(step == 7)
    def _():
        wait_for(dattn, sem_page)

        def last(at):
            grad, hat = held[at, :], xh1[at, :]
            vec_out[0:1, :] += total(grad * hat)
            vec_out[1:2, :] += total(grad)
            dh1 = norm_back(grad, hat, r1[at, :1], vec[0:1, :])
            held[at, :] = dh1
            pltpu.make_async_copy(held.at[at], dh1_out.at[at], sem_rows.at[0]).start()
            low = dh1.astype(LOW)
            dattn[at, :] = low
            vec_out[6:7, :] += total(low.astype(WIDE))

        each(rows, SLAB, last)
        vec_low[...] = jnp.zeros_like(vec_low)
        vec_low[0, 0:4, :] = vec_out[0:4, :].astype(LOW)
        vec_low[0, 4:5, :] = vec_out[6:7, :].astype(LOW)
        vec_low[1, 0:5, :] = vec_out[7:12, :].astype(LOW)

        def send_vectors(core):
            def body(block, carry):
                for half in range(2):
                    send_block(
                        scal,
                        vec_low.at[half],
                        three_outs,
                        half ^ core,
                        block,
                        lambda ref, place: ref.at[place, pl.ds(96, 8)],
                        sem_page,
                        DEPTH_AT,
                    )
                return carry

            lax.fori_loop(0, 16, body, 0)

        per_core(scal, send_vectors)

        def weights(at):
            g_out[at, :] = dot(ctx[:, at], dattn[...], 0, 0).astype(LOW)

        each(width, CHUNK, weights)
        send_out()

        def context(at):
            df[at, :] = dot(dattn[at, :], out_mat[...], 1, 1).astype(LOW)
            pltpu.make_async_copy(df.at[at], dctx_out.at[at], sem_rows.at[1]).start()

        each(rows, CHUNK, context)
        for slot in range(2):
            wait_for(g_up.at[slot], sem_up.at[slot])
            wait_for(g_down.at[slot], sem_down.at[slot])
        wait_for(g_out, sem_out)
        wait_for(held, sem_rows.at[0])
        wait_for(df, sem_rows.at[1])
        lax.fori_loop(0, 16, lambda _, carry: (wait_for(vec_low, sem_page), carry)[1], 0)


def feed(scal, cot, vec, ctx, opened, two, three):
    rows, width = cot.shape
    return pl.pallas_call(
        feed_kernel,
        out_shape=(
            jax.ShapeDtypeStruct((rows, width), LOW),
            jax.ShapeDtypeStruct((rows, width), WIDE),
            jax.ShapeDtypeStruct((rows, width), LOW),
        )
        + block_shapes(48, 384 + 2 * width)
        + block_shapes(104, width),
        grid_spec=pltpu.PrefetchScalarGridSpec(
            num_scalar_prefetch=1,
            grid=(8,),
            in_specs=[whole((rows, width)), whole((16, width)), whole((rows, width))]
            + [any_space()] * 13,
            out_specs=[any_space()] * 9,
            scratch_shapes=[
                pltpu.VMEM((width, width), LOW),
                pltpu.VMEM((4, width, width), LOW),
                pltpu.VMEM((4 * width, width), LOW),
                pltpu.VMEM((rows, width), LOW),
                pltpu.VMEM((rows, width), WIDE),
                pltpu.VMEM((rows, 128), WIDE),
                pltpu.VMEM((4, rows, width), LOW),
                pltpu.VMEM((4, rows, width), WIDE),
                pltpu.VMEM((rows, width), WIDE),
                pltpu.VMEM((rows, width), LOW),
                pltpu.VMEM((rows, width), LOW),
                pltpu.VMEM((rows, width), LOW),
                pltpu.VMEM((width, width), LOW),
                pltpu.VMEM((2, width, width), LOW),
                pltpu.VMEM((2, width, width), LOW),
                pltpu.VMEM((16, width), WIDE),
                pltpu.VMEM((2, 8, width), LOW),
                pltpu.SemaphoreType.DMA((11,)),
                pltpu.SemaphoreType.DMA((2,)),
                pltpu.SemaphoreType.DMA((2,)),
                pltpu.SemaphoreType.DMA,
                pltpu.SemaphoreType.DMA,
                pltpu.SemaphoreType.DMA((2,)),
            ],
        ),
        compiler_params=pltpu.CompilerParams(
            dimension_semantics=("arbitrary",), vmem_limit_bytes=FEED_VMEM_BYTES
        ),
        cost_estimate=pl.CostEstimate(
            flops=2 * rows * width * width * 27, transcendentals=0, bytes_accessed=32 * 1024 * 1024
        ),
        name="feed",
    )(scal, cot, vec, ctx, *opened, *two, *three)


def split_kernel(scal, attn, up, down, two_out, three_out):
    for core in range(2):

        @pl.when(scal[0] == core)
        def _(core=core):
            two_out[0, :, :384] = attn[3, :, 384 * core : 384 * (core + 1)].astype(LOW)
            two_out[0, :, 384:] = up[:, 1536 * core : 1536 * (core + 1)].astype(LOW)
            three_out[0] = down[96 * core : 96 * (core + 1), :].astype(LOW)


def split_weights(core, attn, up, down):
    width = attn.shape[2]
    shapes = ((1, 48, 384 + 2 * width), (1, 96, width))
    return pl.pallas_call(
        split_kernel,
        out_shape=tuple(jax.ShapeDtypeStruct(shape, LOW) for shape in shapes),
        grid_spec=pltpu.PrefetchScalarGridSpec(
            num_scalar_prefetch=1,
            grid=(1,),
            in_specs=[whole(attn.shape), whole(up.shape), whole(down.shape)],
            out_specs=[whole(shape) for shape in shapes],
        ),
        cost_estimate=pl.CostEstimate(flops=0, transcendentals=0, bytes_accessed=3 * 1024 * 1024),
        name="split_weights",
    )(core, attn, up, down)


def unattend_kernel(
    group,
    scal,
    tokens_in,
    sines,
    cosines,
    q_in,
    k_in,
    v_in,
    dctx_in,
    prob,
    *refs,
):
    mats_in, dq_out, dk_out, dv_out = refs[:4]
    outs = refs[4:7]
    (
    mats,
    right,
    ds_low,
    du_low,
    q_heads,
    d_heads,
    grads,
    sums,
    sem,
    sem_out,
    sem_sums,
    tokens,
    sem_tokens,
    ) = refs[7:]
    pair = pl.program_id(0)
    rows, width = tokens.shape
    half = width // 2
    copy_tokens = pltpu.make_async_copy(tokens_in, tokens, sem_tokens)
    scale = HEAD_DIM ** (-0.5)

    @pl.when(pair == 0)
    def _():
        cols = mats.shape[1]
        lane_at = pl.ds(group * cols, cols)
        fetch = pltpu.make_async_copy(mats_in.at[3, :, lane_at], mats, sem)
        fetch.start()
        copy_tokens.start()
        right[:, : width // 2] = sines[...].astype(LOW)
        right[:, width // 2 : width] = cosines[...].astype(LOW)
        fetch.wait()

    lanes = pl.ds(pl.multiple_of(pair * 128, 128), 128)
    right[:, width:] = k_in[...]
    rel = mats[:, lanes]
    low_masks, wide_masks = head_masks(LOW), head_masks(WIDE)

    def score(at):
        sin, cos = sines[at, :], cosines[at, :]
        dq = None
        for head in range(2):
            spot = pl.ds(pl.multiple_of(head * rows + at.start, at.size), at.size)
            dctx = dctx_in[at, :] * low_masks[head]
            d_heads[spot, :] = dctx
            q_heads[spot, :] = q_in[at, :] * low_masks[head]
            p = prob[head, at, :].astype(WIDE)
            dp = dot(dctx, v_in[...], 1, 1)
            ds = (p * (dp - jnp.sum(p * dp, axis=-1, keepdims=True))).astype(LOW)
            ds_low[spot, :] = ds
            dl = dot(ds, right[...], 1, 0) * scale
            ls, lc = dl[:, :half], dl[:, half:width]
            du = jnp.concatenate(
                [(lc * sin - ls * cos).astype(LOW), (ls * sin + lc * cos).astype(LOW)], axis=1
            )
            du_low[spot, :] = du
            part = (dl[:, width:] + dot(du, rel, 1, 0)) * wide_masks[head]
            dq = part if dq is None else dq + part
        dq_out[at, lanes] = dq.astype(LOW)

    each(rows, rows, score, True)
    dv_out[:, lanes] = dot(prob[...].reshape(2 * rows, rows), d_heads[...], 0, 0).astype(LOW)
    dk_out[:, lanes] = (dot(ds_low[...], q_heads[...], 0, 0) * scale).astype(LOW)
    grads[3, :, lanes] = dot(du_low[...], q_heads[...], 0, 0).astype(LOW)

    @pl.when(pair == pl.num_programs(0) - 1)
    def _():
        copy_tokens.wait()

        def weights(at):
            x = tokens[:, at]
            grads[0, at, :] = dot(x, dq_out[...], 0, 0).astype(LOW)
            grads[1, at, :] = dot(x, dk_out[...], 0, 0).astype(LOW)
            grads[2, at, :] = dot(x, dv_out[...], 0, 0).astype(LOW)

        each(width, CHUNK, weights)

        sums[...] = jnp.zeros_like(sums)
        sums[0, 0:1, :] = total(dq_out[...].astype(WIDE)).astype(LOW)
        sums[1, 0:1, :] = total(dv_out[...].astype(WIDE)).astype(LOW)

        def on(core):
            def body(block, carry):
                for slot in range(4):
                    row = turned(block) if slot == 3 else block
                    at = pl.ds(48 * (slot % 2), 48)
                    send_block(
                        scal,
                        grads.at[slot, block_at(row)],
                        outs,
                        (slot // 2) ^ core,
                        block,
                        lambda ref, place, at=at: ref.at[place, at],
                        sem_out,
                    )
                for half in range(2):
                    send_block(
                        scal,
                        sums.at[half],
                        outs,
                        half ^ core,
                        block,
                        lambda ref, place: ref.at[place, pl.ds(96, 8)],
                        sem_sums,
                    )
                return carry

            lax.fori_loop(0, 16, body, 0)

        per_core(scal, on)
        wait_for(grads, sem_out)
        lax.fori_loop(0, 16, lambda _, carry: (wait_for(sums, sem_sums), carry)[1], 0)


def unattend(group, scal, tokens, sines, cosines, q, k, v, dctx, prob, mats):
    rows, width = tokens.shape
    pairs, cols = BACK_PAIRS, 128 * BACK_PAIRS
    low = jax.ShapeDtypeStruct((rows, cols), LOW)
    lane_block = pl.BlockSpec((rows, 128), lambda p, _: (0, group * pairs + p))
    return pl.pallas_call(
        partial(unattend_kernel, group),
        out_shape=(low, low, low) + block_shapes(104, cols),
        grid_spec=pltpu.PrefetchScalarGridSpec(
            num_scalar_prefetch=1,
            grid=(pairs,),
            in_specs=[
                any_space(),
                whole((rows, half_of(width))),
                whole((rows, half_of(width))),
                lane_block,
                lane_block,
                lane_block,
                lane_block,
                pl.BlockSpec((2, rows, rows), lambda p, _: (group * pairs + p, 0, 0)),
            ]
            + [any_space()],
            out_specs=[whole((rows, cols))] * 3 + [any_space()] * 3,
            scratch_shapes=[
                pltpu.VMEM((width, cols), LOW),
                pltpu.VMEM((rows, width + 128), LOW),
                pltpu.VMEM((2 * rows, rows), LOW),
                pltpu.VMEM((2 * rows, width), LOW),
                pltpu.VMEM((2 * rows, 128), LOW),
                pltpu.VMEM((2 * rows, 128), LOW),
                pltpu.VMEM((4, width, cols), LOW),
                pltpu.VMEM((2, 8, cols), LOW),
                pltpu.SemaphoreType.DMA,
                pltpu.SemaphoreType.DMA,
                pltpu.SemaphoreType.DMA,
                pltpu.VMEM((rows, width), LOW),
                pltpu.SemaphoreType.DMA,
            ],
        ),
        compiler_params=pltpu.CompilerParams(
            dimension_semantics=("arbitrary",), vmem_limit_bytes=ATTN_VMEM_BYTES
        ),
        cost_estimate=pl.CostEstimate(
            flops=pairs * 2 * rows * width * 5000, transcendentals=0, bytes_accessed=24 * 1024 * 1024
        ),
        name="unattend",
    )(scal, tokens, sines, cosines, q, k, v, dctx, prob, mats)


def half_of(width):
    return width // 2


def input_grad_kernel(dh1, *refs):
    parts, (mats, out) = refs[: 3 * BACK_GROUPS], refs[3 * BACK_GROUPS :]
    slot = pl.program_id(0)

    @pl.when(slot == 0)
    def _():
        out[...] = dh1[...]

    for part in range(3):

        @pl.when(slot == part)
        def _(part=part):
            def rows_of(at):
                left = jnp.concatenate(
                    [parts[3 * g + part][at, :] for g in range(BACK_GROUPS)], axis=1
                )
                out[at, :] += dot(left, mats[0], 1, 1)

            each(dh1.shape[0], CHUNK, rows_of)


def input_grad(dh1, parts, mats):
    rows, width = dh1.shape
    slim = whole((rows, width // BACK_GROUPS))
    return pl.pallas_call(
        input_grad_kernel,
        out_shape=jax.ShapeDtypeStruct((rows, width), WIDE),
        grid=(3,),
        in_specs=[whole((rows, width))]
        + [slim] * (3 * BACK_GROUPS)
        + [pl.BlockSpec((1, width, width), lambda j: (j, 0, 0))],
        out_specs=whole((rows, width)),
        compiler_params=pltpu.CompilerParams(
            dimension_semantics=("arbitrary",), vmem_limit_bytes=ATTN_VMEM_BYTES
        ),
        cost_estimate=pl.CostEstimate(
            flops=2 * rows * width * width * 3, transcendentals=0, bytes_accessed=10 * 1024 * 1024
        ),
        name="input_grad",
    )(dh1, *parts, mats)


PAIRS = 3
BACK_PAIRS = 2
BACK_GROUPS = 3


def local(
    tokens,
    boxes,
    lengths,
    cotangent,
    attn_weight,
    up_weight,
    down_weight,
    vectors,
    attn_first,
    up_first,
    down_first,
    vector_first,
    attn_second,
    up_second,
    down_second,
    vector_second,
):
    chip, core = lax.axis_index("fsdp"), lax.axis_index("rep")
    width = tokens.shape[2]
    cols = width - width // BACK_GROUPS
    first = core == 0
    page = tokens[0]
    same = (ORDERS[0], ORDERS[0])

    near = jnp.where(first, attn_weight[:2], attn_weight[2:5:2]).astype(LOW).reshape(1, 96, width)
    near_far = hop(near, 0)
    core_at = after(core.astype(jnp.int32)[None], near)
    two, three = split_weights(core_at, attn_weight, up_weight, down_weight)
    three_far = hop(three, 0, PLANE_FIRST)
    vec = lax.dynamic_update_slice(
        jnp.zeros((vectors.shape[0], width), LOW),
        after(vectors.astype(LOW), near),
        (jnp.int32(0), chip * vectors.shape[1]),
    )
    scal = block_scalars(chip, core, lengths[0])
    near, near_far, two, vec, place, scal = sync(near, near_far, two, vec, boxes[0], scal)

    near = join(near, near_far)
    near_far = hop(near, 1)
    vec_far = hop(vec, 0, same)
    quarter = width // 4
    frequency = jnp.exp(jnp.arange(quarter).astype(WIDE) * (-math.log(10000.0) / quarter))
    place = place.astype(WIDE)
    angles = jnp.concatenate([place[0][:, None] * frequency, place[1][:, None] * frequency], axis=1)
    sines, cosines = jnp.sin(angles), jnp.cos(angles)
    near, near_far, vec, vec_far, two, three, three_far, sines, cosines = sync(
        near, near_far, vec, vec_far, two, three, three_far, sines, cosines
    )

    near = join(near, near_far)
    near_far = hop(near, 2)
    two_far = hop(two, 0)
    vec = vec + vec_far
    vec_far = hop(vec, 1, same)
    three = join(three, three_far)
    three_far = hop(after(three, vec), 1, PLANE_FIRST)
    near, near_far, vec, vec_far, two, two_far, three = sync(
        near, near_far, vec, vec_far, two, two_far, three
    )

    near = join(near, near_far)
    near_far = hop(near, 3)
    near_swap = swap_cores(near)
    vec = vec + vec_far
    vec_far = hop(vec, 2, same)
    two = join(two, two_far)
    two_far = hop(two, 1)
    near_far, near_swap, vec, vec_far, two, two_far, three, three_far = sync(
        near_far, near_swap, vec, vec_far, two, two_far, three, three_far
    )

    near_far_swap = swap_cores(near_far)
    vec = vec + vec_far
    vec_far = hop(vec, 3, same)
    two = join(two, two_far)
    two_far = hop(two, 2)
    three = join(three, three_far)
    three_far = hop(three, 2, PLANE_FIRST)
    vec, near_far_swap, two, three = sync(vec + vec_far, near_far_swap, two, three)
    vec = jnp.pad(vec.astype(WIDE), ((0, 16 - vec.shape[0]), (0, 0)))
    pieces = (near, near_far, near_swap, near_far_swap)

    def go(group, tick, before):
        return attend(
            group, after(scal, tick), page, vec, sines, cosines, pieces, before
        )

    kept = go(0, two, [])
    two, two_far, three, three_far, *kept = sync(two, two_far, three, three_far, *kept)

    two = join(two, two_far)
    two_far = hop(two, 3)
    three = join(three, three_far)
    two_swap = swap_cores(two)
    three_swap = swap_cores(three)
    kept = go(1, three, kept)
    two_far, two_swap, three_swap, *kept = sync(two_far, two_swap, three_swap, *kept)

    two_far_swap = swap_cores(two_far)
    three_far = hop(after(three, two_far), 3, PLANE_FIRST)
    two_pieces = (two, two_far, two_swap, two_far_swap)
    norm_low, xh1, r1, act, slope = open_ffn(scal, page, vec, kept[3], two_pieces)
    three_far, r1 = sync(three_far, r1)

    three_pieces = (three, three_far, three_swap, swap_cores(three_far))
    page_out, dh1, dctx, *sent = feed(
        scal,
        cotangent[0],
        vec,
        kept[3],
        (act, slope, norm_low, xh1, r1),
        two_pieces,
        three_pieces,
    )
    two_sent, three_sent = sent[:3], sent[3:]

    three_swap, two_swap, three_low, two_low, mark = sync(
        swap_cores(three_sent[2]), swap_cores(two_sent[2]), three_sent[1], two_sent[1], scal
    )
    three_high = add_up([three_sent[0][8:], three_swap])
    three_far = hop(three_high, 3, DEPTH_FIRST)
    two_high = add_up([two_sent[0][8:], two_swap])
    two_far = hop(two_high, 3)
    three_low = swap_cores(three_low)
    two_low = swap_cores(two_low)

    def undo(group, tick):
        return unattend(
            group,
            after(scal, tick),
            page,
            sines,
            cosines,
            *kept[:3],
            dctx,
            pltpu.with_memory_space_constraint(kept[4], pltpu.HBM),
            kept[5],
        )

    def beside(left, right):
        return jnp.concatenate([left, right], axis=2)

    back = [undo(0, mark)]
    two_far, three_low, two_low, mark, *one_sent = sync(
        two_far, three_low, two_low, back[0][0], *back[0][3:]
    )

    two_terms, two_high = halve([two_sent[0][:8], two_low, two_far])
    two_far = hop(two_high, 2)
    one_swap = swap_cores(one_sent[2])
    one_low = swap_cores(one_sent[1])
    back.append(undo(1, mark))
    two_far, three_far, one_swap, one_low, mark, *next_sent = sync(
        two_far, three_far, one_swap, one_low, back[1][0], *back[1][3:]
    )

    next_swap = swap_cores(next_sent[2])
    three_terms, three_high = halve([three_sent[0][:8], three_low, three_far])
    three_far = hop(three_high, 2, DEPTH_FIRST)
    two_terms, two_high = halve(two_terms + [two_far])
    two_far = hop(two_high, 1)
    next_swap, next_low, mark, three_high, two_high = sync(
        next_swap, next_sent[1], mark, three_high, two_high
    )
    one_high = beside(
        add_up([one_sent[0][8:], one_swap]), add_up([next_sent[0][8:], next_swap])
    )
    one_far = hop(one_high, 3)
    next_low = swap_cores(next_low)
    back.append(undo(2, mark))
    two_far, three_far, one_far, next_low, *end_sent = sync(
        two_far, three_far, one_far, next_low, *back[2][3:]
    )

    end_high = add_up([end_sent[0][8:], swap_cores(end_sent[2])])
    end_far = hop(end_high, 3)
    end_low, one_far, three_far, two_far, mark = sync(
        end_sent[1], one_far, three_far, two_far, end_high
    )
    end_low = swap_cores(end_low)
    two_terms, two_high = halve(two_terms + [two_far])
    two_far = hop(two_high, 0)
    one_terms = [beside(one_sent[0][:8], next_sent[0][:8]), beside(one_low, next_low), one_far]
    one_terms, one_high = halve(one_terms)
    one_far = hop(one_high, 2)
    three_terms, three_high = halve(three_terms + [three_far])
    three_far = hop(three_high, 1, DEPTH_FIRST)
    end_far, end_low, one_far, three_far, two_far, mark = sync(
        end_far, end_low, one_far, three_far, two_far, mark
    )

    end_terms, end_high = halve([end_sent[0][:8], end_low, end_far])
    end_far = hop(end_high, 2)
    one_terms, one_high = halve(one_terms + [one_far])
    one_far = hop(one_high, 1)
    three_terms, three_high = halve(three_terms + [three_far])
    three_far = hop(three_high, 0, DEPTH_FIRST)
    two_mine = add_up(two_terms + [two_far])[0]
    two_other = swap_cores(two_mine)
    token_grad = input_grad(
        after(dh1, mark, two_mine), [part for b in back for part in b[:3]], kept[5]
    )
    end_far, one_far, three_far, two_other, token_grad = sync(
        end_far, one_far, three_far, two_other, token_grad
    )

    end_terms, end_high = halve(end_terms + [end_far])
    end_far = hop(end_high, 1)
    one_terms, one_high = halve(one_terms + [one_far])
    one_far = hop(one_high, 0)
    three_mine = add_up(three_terms + [three_far])[0]
    three_other = swap_cores(three_mine)
    two_sum = by_half(core, (two_mine, two_other))
    up_sum = jnp.concatenate([two_sum[0][:, 384:], two_sum[1][:, 384:]], axis=1)
    up_next = adam_update(up_weight, up_first, up_second, up_sum, UP_RATE, WEIGHT_DECAY)
    end_far, one_far, three_other, up_copy, up_new, up_first_new, up_second_new = sync(
        end_far, one_far, three_other, up_next[0].astype(LOW), *up_next
    )

    end_terms, end_high = halve(end_terms + [end_far])
    end_far = hop(end_high, 0)
    three_sum = by_half(core, (three_mine, three_other))
    down_next = adam_update(
        down_weight,
        down_first,
        down_second,
        jnp.concatenate([part[:96] for part in three_sum]),
        DOWN_RATE,
        WEIGHT_DECAY,
    )
    one_mine = add_up(one_terms + [one_far])[0]
    end_far, one_mine, down_copy, down_new, down_first_new, down_second_new = sync(
        end_far, one_mine, down_next[0].astype(LOW), *down_next
    )

    one_mine = jnp.concatenate([one_mine, add_up(end_terms + [end_far])[0]], axis=1)
    one_sum = by_half(core, (one_mine, swap_cores(one_mine)))
    vec_grad = jnp.concatenate(
        [
            three_sum[0][96:100],
            one_sum[0][96:97],
            one_sum[1][96:97],
            three_sum[0][100:101],
            three_sum[1][96:101],
        ]
    )
    vec_sum = lax.dynamic_slice(
        vec_grad, (jnp.int32(0), chip * vectors.shape[1]), vectors.shape
    )
    attn_sum = jnp.stack(
        [
            one_sum[0][:48],
            one_sum[0][48:96],
            one_sum[1][:48],
            jnp.concatenate([two_sum[0][:, :384], two_sum[1][:, :384]], axis=1),
            one_sum[1][48:96],
        ]
    )
    layer_out, token_grad = page_out[None], token_grad[None]
    attn_rates = jnp.array(ATTN_RATES, jnp.float32)[:, None, None]
    attn_new, attn_first_new, attn_second_new = adam_update(
        attn_weight, attn_first, attn_second, attn_sum, attn_rates, WEIGHT_DECAY
    )
    vectors_new, vector_first_new, vector_second_new = adam_update(
        vectors, vector_first, vector_second, vec_sum, VECTOR_RATE, 0.0
    )
    return (
        layer_out,
        token_grad,
        attn_new,
        up_new,
        down_new,
        vectors_new,
        attn_first_new,
        up_first_new,
        down_first_new,
        vector_first_new,
        attn_second_new,
        up_second_new,
        down_second_new,
        vector_second_new,
        attn_new.astype(jnp.bfloat16),
        up_copy,
        down_copy,
        vectors_new.astype(jnp.bfloat16),
    )


def local_general(
    tokens,
    boxes,
    lengths,
    cotangent,
    attn_weight,
    up_weight,
    down_weight,
    vectors,
    attn_first,
    up_first,
    down_first,
    vector_first,
    attn_second,
    up_second,
    down_second,
    vector_second,
):
    lowered = (
        attn_weight.astype(jnp.bfloat16),
        up_weight.astype(jnp.bfloat16),
        down_weight.astype(jnp.bfloat16),
        vectors.astype(jnp.bfloat16),
    )
    gathered = (
        lax.all_gather(lowered[0], "fsdp", axis=1, tiled=True),
        lax.all_gather(lowered[1], "fsdp", axis=0, tiled=True),
        lax.all_gather(lowered[2], "fsdp", axis=0, tiled=True),
        lax.all_gather(lowered[3], "fsdp", axis=1, tiled=True),
    )

    def forward_step(carry, page):
        token_row_block, box_rows, page_length = page
        return (carry, forward_page(gathered, token_row_block, box_rows, page_length))

    _, (layer_out, saved_all) = lax.scan(forward_step, None, (tokens, boxes, lengths))
    backward_weights = (
        lax.all_gather(lowered[0], "fsdp", axis=1, tiled=True),
        lax.all_gather(lowered[1], "fsdp", axis=0, tiled=True),
        lax.all_gather(lowered[2], "fsdp", axis=0, tiled=True),
        lax.all_gather(lowered[3], "fsdp", axis=1, tiled=True),
    )
    model_width = gathered[0].shape[2]
    ffn_width = gathered[1].shape[1]
    zero_grads = (
        jnp.zeros((5, model_width, model_width), jnp.float32),
        jnp.zeros((model_width, ffn_width), jnp.float32),
        jnp.zeros((ffn_width, model_width), jnp.float32),
        jnp.zeros(gathered[3].shape, jnp.float32),
    )

    def backward_step(totals, page):
        token_row_block, box_rows, page_length, upstream, saved_state = page
        token_grad, grads = backward_page(
            backward_weights, token_row_block, box_rows, page_length, upstream, saved_state
        )
        return (jax.tree.map(jnp.add, totals, grads), token_grad)

    totals, token_grad = lax.scan(
        backward_step, zero_grads, (tokens, boxes, lengths, cotangent, saved_all)
    )
    shards = (
        lax.psum_scatter(totals[0], "fsdp", scatter_dimension=1, tiled=True),
        lax.psum_scatter(totals[1], "fsdp", scatter_dimension=0, tiled=True),
        lax.psum_scatter(totals[2], "fsdp", scatter_dimension=0, tiled=True),
        lax.psum_scatter(totals[3], "fsdp", scatter_dimension=1, tiled=True),
    )
    reduced = (
        lax.psum(shards[0].astype(jnp.bfloat16), "rep").astype(jnp.float32),
        lax.psum(shards[1].astype(jnp.bfloat16), "rep").astype(jnp.float32),
        lax.psum(shards[2].astype(jnp.bfloat16), "rep").astype(jnp.float32),
        lax.psum(shards[3].astype(jnp.bfloat16), "rep").astype(jnp.float32),
    )
    attn_rates = jnp.array(ATTN_RATES, jnp.float32)[:, None, None]
    attn_new, attn_first_new, attn_second_new = adam_update(
        attn_weight, attn_first, attn_second, reduced[0], attn_rates, WEIGHT_DECAY
    )
    up_new, up_first_new, up_second_new = adam_update(
        up_weight, up_first, up_second, reduced[1], UP_RATE, WEIGHT_DECAY
    )
    down_new, down_first_new, down_second_new = adam_update(
        down_weight, down_first, down_second, reduced[2], DOWN_RATE, WEIGHT_DECAY
    )
    vectors_new, vector_first_new, vector_second_new = adam_update(
        vectors, vector_first, vector_second, reduced[3], VECTOR_RATE, 0.0
    )
    return (
        layer_out,
        token_grad,
        attn_new,
        up_new,
        down_new,
        vectors_new,
        attn_first_new,
        up_first_new,
        down_first_new,
        vector_first_new,
        attn_second_new,
        up_second_new,
        down_second_new,
        vector_second_new,
        attn_new.astype(jnp.bfloat16),
        up_new.astype(jnp.bfloat16),
        down_new.astype(jnp.bfloat16),
        vectors_new.astype(jnp.bfloat16),
    )


def solution(mesh):
    blocked = mesh.shape["fsdp"] == 16 and mesh.shape["rep"] == 2
    return jax.shard_map(
        local if blocked else local_general,
        mesh=mesh,
        in_specs=(
            P(("fsdp", "rep"), None, None),
            P(("fsdp", "rep"), None, None),
            P(("fsdp", "rep")),
            P(("fsdp", "rep"), None, None),
            P(None, "fsdp", None),
            P("fsdp", None),
            P("fsdp", None),
            P(None, "fsdp"),
            P(None, "fsdp", None),
            P("fsdp", None),
            P("fsdp", None),
            P(None, "fsdp"),
            P(None, "fsdp", None),
            P("fsdp", None),
            P("fsdp", None),
            P(None, "fsdp"),
        ),
        out_specs=(
            P(("fsdp", "rep"), None, None),
            P(("fsdp", "rep"), None, None),
            P(None, "fsdp", None),
            P("fsdp", None),
            P("fsdp", None),
            P(None, "fsdp"),
            P(None, "fsdp", None),
            P("fsdp", None),
            P("fsdp", None),
            P(None, "fsdp"),
            P(None, "fsdp", None),
            P("fsdp", None),
            P("fsdp", None),
            P(None, "fsdp"),
            P(None, "fsdp", None),
            P("fsdp", None),
            P("fsdp", None),
            P(None, "fsdp"),
        ),
        check_vma=False,
    )
```

```python
from functools import partial
import math

import jax
import jax.numpy as jnp
from jax import lax
from jax.experimental import pallas as pl
from jax.experimental.pallas import tpu as pltpu
from jax.sharding import PartitionSpec as P

HEADS = 12
HEAD_DIM = 64
STEP = 7


EPS_NORM = 1e-12
EPS_ADAM = 1e-08
DECAY = 0.5
MASK_FILL = -1e30
WEIGHT_DECAY = 0.01
ATTN_RATES = (0.04, 0.04, 0.04, 0.2, 0.04)
UP_RATE = 0.04
DOWN_RATE = 0.02
VECTOR_RATE = 0.3


def contract(left_op, right_op, left_dim, right_dim):
    return lax.dot_general(
        left_op,
        right_op,
        (((left_dim,), (right_dim,)), ((), ())),
        preferred_element_type=jnp.float32,
    )


def layer_norm(hidden, gain_row, shift_row):
    center = hidden - jnp.mean(hidden, axis=-1, keepdims=True)
    spread = jnp.mean(center * center, axis=-1, keepdims=True)
    return center * lax.rsqrt(spread + EPS_NORM) * gain_row + shift_row


def box_tables(box_rows, model_width):
    quarter = model_width // 4
    frequency = jnp.exp(jnp.arange(quarter).astype(jnp.float32) * (-math.log(10000.0) / quarter))
    angles = box_rows.astype(jnp.float32)[:, :, None] * frequency
    return (jnp.sin(angles), jnp.cos(angles))


def encode(sine_rows, cosine_rows):
    return jnp.concatenate([sine_rows[0], cosine_rows[0], sine_rows[1], cosine_rows[1]], axis=-1)


def rotate(pos_table, sine_rows, cosine_rows):
    quarter = sine_rows.shape[-1]
    pieces = []
    for coord in range(2):
        sine_part = pos_table[..., 2 * coord * quarter : (2 * coord + 1) * quarter]
        cosine_part = pos_table[..., (2 * coord + 1) * quarter : (2 * coord + 2) * quarter]
        pieces.append(cosine_part * sine_rows[coord] - sine_part * cosine_rows[coord])
        pieces.append(sine_part * sine_rows[coord] + cosine_part * cosine_rows[coord])
    return jnp.concatenate(pieces, axis=-1)


def scores(query_rows, key_rows, left_rows, encoded, page_live):
    text_part = jnp.einsum("ihd,jhd->hij", query_rows, key_rows, preferred_element_type=jnp.float32)
    place_part = jnp.einsum("hie,je->hij", left_rows, encoded, preferred_element_type=jnp.float32)
    score_rows = (text_part + place_part) * HEAD_DIM ** (-0.5)
    return jnp.where(page_live[None, None, :], score_rows, MASK_FILL)


def forward_page(weights, token_row_block, box_rows, page_length):
    attention_matrices, up_mat, down_mat, vector_rows = weights
    row_count, model_width = token_row_block.shape
    vector_f32 = vector_rows.astype(jnp.float32)
    page_live = jnp.arange(row_count) < page_length
    projected_rows = jnp.einsum(
        "tb,mby->mty", token_row_block, attention_matrices[:3], preferred_element_type=jnp.float32
    )
    query_rows = (
        (projected_rows[0] + vector_f32[4]).astype(jnp.bfloat16).reshape(row_count, HEADS, HEAD_DIM)
    )
    key_rows = projected_rows[1].astype(jnp.bfloat16).reshape(row_count, HEADS, HEAD_DIM)
    value_rows = (
        (projected_rows[2] + vector_f32[5]).astype(jnp.bfloat16).reshape(row_count, HEADS, HEAD_DIM)
    )
    sine_rows, cosine_rows = box_tables(box_rows, model_width)
    encoded = encode(sine_rows, cosine_rows).astype(jnp.bfloat16)
    rel_heads = attention_matrices[4].reshape(model_width, HEADS, HEAD_DIM)
    pos_table = jnp.einsum(
        "ihd,ehd->hie", query_rows, rel_heads, preferred_element_type=jnp.float32
    )
    left_rows = rotate(pos_table, sine_rows, cosine_rows).astype(jnp.bfloat16)
    score_rows = scores(query_rows, key_rows, left_rows, encoded, page_live)
    row_top = jnp.max(score_rows, axis=-1, keepdims=True)
    exponent = jnp.exp(score_rows - row_top)
    row_total = jnp.sum(exponent, axis=-1, keepdims=True)
    prob_low = (exponent / row_total).astype(jnp.bfloat16)
    logsum = row_top + jnp.log(row_total)
    mixed_rows = jnp.einsum(
        "hij,jhd->ihd", prob_low, value_rows, preferred_element_type=jnp.float32
    )
    context = mixed_rows.reshape(row_count, model_width).astype(jnp.bfloat16)
    attn_out = (
        jnp.dot(context, attention_matrices[3], preferred_element_type=jnp.float32) + vector_f32[6]
    )
    first_sum = token_row_block.astype(jnp.float32) + attn_out
    normed = layer_norm(first_sum, vector_f32[0], vector_f32[1])
    pre_act = jnp.dot(
        normed.astype(jnp.bfloat16), up_mat, preferred_element_type=jnp.float32
    ) + vector_f32[8:].reshape(-1)
    act_low = jax.nn.gelu(pre_act, approximate=False).astype(jnp.bfloat16)
    second_sum = normed + (
        jnp.dot(act_low, down_mat, preferred_element_type=jnp.float32) + vector_f32[7]
    )
    page_out = (layer_norm(second_sum, vector_f32[2], vector_f32[3]) * page_live[:, None]).astype(
        jnp.bfloat16
    )
    saved_state = (
        query_rows,
        key_rows,
        value_rows,
        left_rows,
        logsum,
        context,
        first_sum,
        pre_act,
        act_low,
        second_sum,
    )
    return (page_out, saved_state)


def backward_page(weights, token_row_block, box_rows, page_length, upstream, saved_state):
    attention_matrices, up_mat, down_mat, vector_rows = weights
    (
        query_rows,
        key_rows,
        value_rows,
        left_rows,
        logsum,
        context,
        first_sum,
        pre_act,
        act_low,
        second_sum,
    ) = saved_state
    row_count, model_width = token_row_block.shape
    vector_f32 = vector_rows.astype(jnp.float32)
    page_live = jnp.arange(row_count) < page_length
    sine_rows, cosine_rows = box_tables(box_rows, model_width)
    encoded = encode(sine_rows, cosine_rows).astype(jnp.bfloat16)
    out_grad = upstream.astype(jnp.float32) * page_live[:, None]
    _, pull_second = jax.vjp(layer_norm, second_sum, vector_f32[2], vector_f32[3])
    second_grad, gain_two, shift_two = pull_second(out_grad)
    ffn_grad = second_grad.astype(jnp.bfloat16)
    down_grad = contract(act_low, ffn_grad, 0, 0)
    act_grad = contract(ffn_grad, down_mat, 1, 1)
    _, pull_gelu = jax.vjp(partial(jax.nn.gelu, approximate=False), pre_act)
    pre_grad = pull_gelu(act_grad)[0].astype(jnp.bfloat16)
    normed, pull_first = jax.vjp(layer_norm, first_sum, vector_f32[0], vector_f32[1])
    up_grad = contract(normed.astype(jnp.bfloat16), pre_grad, 0, 0)
    normed_grad = contract(pre_grad, up_mat, 1, 1) + second_grad
    first_grad, gain_one, shift_one = pull_first(normed_grad)
    attn_grad = first_grad.astype(jnp.bfloat16)
    out_mat_grad = contract(context, attn_grad, 0, 0)
    context_grad = (
        contract(attn_grad, attention_matrices[3], 1, 1)
        .astype(jnp.bfloat16)
        .reshape(row_count, HEADS, HEAD_DIM)
    )
    score_rows = scores(query_rows, key_rows, left_rows, encoded, page_live)
    prob_rows = jnp.exp(score_rows - logsum)
    value_grad = jnp.einsum(
        "hij,ihd->jhd",
        prob_rows.astype(jnp.bfloat16),
        context_grad,
        preferred_element_type=jnp.float32,
    ).astype(jnp.bfloat16)
    prob_grad = jnp.einsum(
        "ihd,jhd->hij", context_grad, value_rows, preferred_element_type=jnp.float32
    )
    score_grad = (
        prob_rows * (prob_grad - jnp.sum(prob_rows * prob_grad, axis=-1, keepdims=True))
    ).astype(jnp.bfloat16)
    score_scale = HEAD_DIM ** (-0.5)
    left_grad = (
        jnp.einsum("hij,je->hie", score_grad, encoded, preferred_element_type=jnp.float32)
        * score_scale
    )
    table_grad = rotate(left_grad, sine_rows, cosine_rows).astype(jnp.bfloat16)
    rel_heads = attention_matrices[4].reshape(model_width, HEADS, HEAD_DIM)
    rel_grad = jnp.einsum(
        "hie,ihd->ehd", table_grad, query_rows, preferred_element_type=jnp.float32
    ).reshape(model_width, model_width)
    query_grad = (
        jnp.einsum("hij,jhd->ihd", score_grad, key_rows, preferred_element_type=jnp.float32)
        * score_scale
    )
    query_grad = query_grad + jnp.einsum(
        "hie,ehd->ihd", table_grad, rel_heads, preferred_element_type=jnp.float32
    )
    key_grad = (
        jnp.einsum("hij,ihd->jhd", score_grad, query_rows, preferred_element_type=jnp.float32)
        * score_scale
    )
    stacked_layers = jnp.stack(
        [
            query_grad.astype(jnp.bfloat16).reshape(row_count, model_width),
            key_grad.astype(jnp.bfloat16).reshape(row_count, model_width),
            value_grad.reshape(row_count, model_width),
        ]
    )
    projection_gradient = jnp.einsum(
        "cg,yca->yga", token_row_block, stacked_layers, preferred_element_type=jnp.float32
    )
    token_grad = first_grad + jnp.einsum(
        "skl,scl->kc", stacked_layers, attention_matrices[:3], preferred_element_type=jnp.float32
    )
    column_sums = jnp.sum(stacked_layers.astype(jnp.float32), axis=1)
    attn_grads = jnp.concatenate([projection_gradient, out_mat_grad[None], rel_grad[None]], axis=0)
    small_rows = jnp.stack(
        [
            gain_one,
            shift_one,
            gain_two,
            shift_two,
            column_sums[0],
            column_sums[2],
            jnp.sum(attn_grad.astype(jnp.float32), axis=0),
            jnp.sum(ffn_grad.astype(jnp.float32), axis=0),
        ]
    )
    up_bias_rows = jnp.sum(pre_grad.astype(jnp.float32), axis=0).reshape(-1, model_width)
    vector_grad = jnp.concatenate([small_rows, up_bias_rows], axis=0)
    return (token_grad, (attn_grads, up_grad, down_grad, vector_grad))


def adam_update(weight, first, second, grad, rate, decay_weight):
    first_new = DECAY * first + (1.0 - DECAY) * grad
    second_new = DECAY * second + (1.0 - DECAY) * grad * grad
    correction = 1.0 - DECAY**STEP
    direction = first_new / correction / (jnp.sqrt(second_new / correction) + EPS_ADAM)
    return (weight - rate * (direction + decay_weight * weight), first_new, second_new)


AXES = ("fsdp", "rep")
ORDERS = ((8, 4, 2, 1), (8, 4, 1, 2))
PLANE_FIRST = ((1, 8, 4, 2), (2, 8, 4, 1))
DEPTH_FIRST = ((8, 2, 1, 4), (8, 1, 2, 4))
PLAIN_AT, DEPTH_AT, PLANE_AT = 32, 96, 64
LOW = jnp.bfloat16
WIDE = jnp.float32
CHUNK = 256
SLAB = 128
FEED_VMEM_BYTES = 58 * 1024 * 1024
OPEN_VMEM_BYTES = 28 * 1024 * 1024
ATTN_VMEM_BYTES = 28 * 1024 * 1024
CORE_AT, LENGTH_AT = 128, 129


def mask_table(order):
    masks = [0]
    for bit in order:
        masks = masks + [bit ^ mask for mask in masks]
    return masks


CORE_PAIRS = [(chip * 2 + core, chip * 2 + 1 - core) for chip in range(16) for core in range(2)]


def place_of(mask, order):
    place = 0
    for bit_at, bit in enumerate(order):
        place = place + jnp.where((mask & bit) != 0, 1 << bit_at, 0)
    return place


def block_scalars(chip, core, length):
    rows, lane = [], jnp.arange(16, dtype=jnp.int32)
    blocks = [jnp.array(mask_table(order), jnp.int32) ^ chip for order in ORDERS]
    places = [place_of(lane ^ chip, order) for order in ORDERS]
    plane_blocks = [jnp.array(mask_table(order), jnp.int32) ^ chip for order in PLANE_FIRST]
    depth_places = [place_of(lane ^ chip, order) for order in DEPTH_FIRST]
    for pair in (blocks, places, plane_blocks, depth_places):
        rows.append(jnp.where(core == 0, pair[0], pair[1]))
        rows.append(jnp.where(core == 0, pair[1], pair[0]))
    last = jnp.where(lane == 0, core, jnp.where(lane == 1, length, 0))
    return jnp.stack(rows + [last]).astype(jnp.int32).reshape(-1)


def after(value, *others):
    return lax.optimization_barrier((value, *others))[0]


def sync(*values):
    return lax.optimization_barrier(values)


def swap_cores(block):
    return lax.ppermute(block, AXES, CORE_PAIRS)


def hop(held, step, orders=ORDERS):
    pairs = [
        (chip * 2 + core, (chip ^ orders[core][step]) * 2 + core)
        for chip in range(16)
        for core in range(2)
    ]
    return lax.ppermute(held, AXES, pairs)


def join(held, arrived):
    return jnp.concatenate([held, arrived], axis=0)


def add_up(terms):
    total_sum = terms[0].astype(WIDE)
    for term in terms[1:]:
        total_sum = total_sum + term.astype(WIDE)
    return total_sum.astype(terms[0].dtype)


def halve(terms):
    half = terms[0].shape[0] // 2
    return [term[:half] for term in terms], add_up([term[half:] for term in terms])


def by_half(core, sums):
    mine, other = sums
    first = jnp.where(core == 0, mine, other)
    second = jnp.where(core == 0, other, mine)
    return first.astype(WIDE), second.astype(WIDE)


def dot(left_op, right_op, left_dim, right_dim):
    return lax.dot_general(
        left_op,
        right_op,
        (((left_dim,), (right_dim,)), ((), ())),
        preferred_element_type=WIDE,
    )


def each(count, size, body, flat=False):
    def step(index, carry):
        body(pl.ds(pl.multiple_of(index * size, size), size))
        return carry

    if flat:
        for index in range(count // size):
            body(pl.ds(index * size, size))
    else:
        lax.fori_loop(0, count // size, step, 0)


def block_at(index):
    return pl.ds(pl.multiple_of(index * 48, 16), 48)


def turned(block):
    return (block & 3) | ((block & 4) << 1) | ((block & 8) >> 1)


def start_copies(make, count):
    def start(place, carry):
        for copy in make(place):
            copy.start()
        return carry

    lax.fori_loop(0, count, start, 0)


def wait_for(buffer, sem):
    pltpu.make_async_copy(buffer, buffer, sem).wait()


def sources(scal, pieces):
    core = scal[CORE_AT]
    bases = (0, 8, 16, 24)
    halves = (core, core, 1 - core, 1 - core)
    return [(piece, base, half) for piece, base, half in zip(pieces, bases, halves, strict=True)]


def attn_copies(scal, pieces, lanes, mats, spot, sem, place):
    copies = []
    for source, base, half in sources(scal, pieces):
        block = scal[base + place]
        for part in range(2):
            row = block if part == 0 else jnp.where(half == 1, turned(block), block)
            copies.append(
                pltpu.make_async_copy(
                    source.at[place, pl.ds(48 * part, 48), lanes],
                    mats.at[2 * half + part, block_at(row), spot],
                    sem,
                )
            )
    return copies


def head_masks(dtype):
    lane = lax.broadcasted_iota(jnp.int32, (1, 128), 1)
    first = jnp.where(lane < 64, 1.0, 0.0)
    return (first.astype(dtype), (1.0 - first).astype(dtype))


def attend_kernel(
    group,
    scal,
    tokens,
    vec,
    sines,
    cosines,
    *refs,
):
    pieces, refs = refs[:4], refs[4:] if group == 0 else refs[10:]
    q_out, k_out, v_out, ctx_out, prob_out, mats_out = refs[:6]
    mats, right, sem, sem_out = refs[6:]
    pair = pl.program_id(0)
    width = tokens.shape[1]
    rows = tokens.shape[0]

    @pl.when(pair == 0)
    def _():
        cols = mats.shape[2]
        lane_at = pl.ds(group * cols, cols)
        start_copies(partial(attn_copies, scal, pieces, lane_at, mats, pl.ds(0, cols), sem), 8)
        wait_for(mats, sem)
        pltpu.make_async_copy(mats, mats_out.at[:, :, lane_at], sem_out).start()
        right[:, : width // 2] = sines[...].astype(LOW)
        right[:, width // 2 : width] = cosines[...].astype(LOW)

        def project(at):
            x = tokens[at, :]
            q_out[at, :] = (dot(x, mats[0], 1, 0) + vec[4:5, :]).astype(LOW)
            k_out[at, :] = dot(x, mats[1], 1, 0).astype(LOW)
            v_out[at, :] = (dot(x, mats[2], 1, 0) + vec[5:6, :]).astype(LOW)

        each(rows, CHUNK, project)

    lanes = pl.ds(pl.multiple_of(pair * 128, 128), 128)
    right[:, width:] = k_out[:, lanes]
    rel = mats[3, :, lanes]
    live = lax.broadcasted_iota(jnp.int32, (1, rows), 1) < scal[LENGTH_AT]
    half = width // 2

    def score(at):
        q_pair = q_out[at, :] if q_out.shape[1] == 128 else q_out[at, lanes]
        sin, cos = sines[at, :], cosines[at, :]
        mixed = []
        for head, mask in enumerate(head_masks(LOW)):
            q_head = q_pair * mask
            table = dot(q_head, rel, 1, 1)
            us, uc = table[:, :half], table[:, half:]
            left = jnp.concatenate(
                [(uc * sin - us * cos).astype(LOW), (us * sin + uc * cos).astype(LOW), q_head], axis=1
            )
            s = dot(left, right[...], 1, 1) * HEAD_DIM ** (-0.5)
            s = jnp.where(live, s, MASK_FILL)
            top = jnp.max(s, axis=-1, keepdims=True)
            e = jnp.exp(s - top)
            prob = (e * (1.0 / jnp.sum(e, axis=-1, keepdims=True))).astype(LOW)
            prob_out[head, at, :] = prob
            mixed.append(dot(prob, v_out[:, lanes], 1, 0))
        masks = head_masks(WIDE)
        ctx_out[at, :] = (mixed[0] * masks[0] + mixed[1] * masks[1]).astype(LOW)

    each(rows, rows, score, True)

    @pl.when(pair == pl.num_programs(0) - 1)
    def _():
        wait_for(mats, sem_out)


def any_space():
    return pl.BlockSpec(memory_space=pl.ANY)


def whole(shape):
    return pl.BlockSpec(shape, lambda *_: (0,) * len(shape))


def attend(group, scal, tokens, vec, sines, cosines, pieces, before):
    rows, width = tokens.shape
    pairs, cols = PAIRS, 128 * PAIRS
    low = jax.ShapeDtypeStruct((rows, width), LOW)
    prob = pltpu.HBM((width // HEAD_DIM, rows, rows), LOW)
    mats = jax.ShapeDtypeStruct((4, width, width), LOW)
    return pl.pallas_call(
        partial(attend_kernel, group),
        out_shape=(low, low, low, low, prob, mats),
        grid_spec=pltpu.PrefetchScalarGridSpec(
            num_scalar_prefetch=1,
            grid=(pairs,),
            in_specs=[
                whole((rows, width)),
                pl.BlockSpec((vec.shape[0], cols), lambda p, _: (0, group)),
                whole((rows, width // 2)),
                whole((rows, width // 2)),
            ]
            + [any_space()] * (4 + len(before)),
            out_specs=[pl.BlockSpec((rows, cols), lambda p, _: (0, group))] * 3
            + [
                pl.BlockSpec((rows, 128), lambda p, _: (0, group * pairs + p)),
                pl.BlockSpec((2, rows, rows), lambda p, _: (group * pairs + p, 0, 0)),
                any_space(),
            ],
            scratch_shapes=[
                pltpu.VMEM((4, width, cols), LOW),
                pltpu.VMEM((rows, width + 128), LOW),
                pltpu.SemaphoreType.DMA,
                pltpu.SemaphoreType.DMA,
            ],
        ),
        compiler_params=pltpu.CompilerParams(
            dimension_semantics=("arbitrary",), vmem_limit_bytes=ATTN_VMEM_BYTES
        ),
        cost_estimate=pl.CostEstimate(
            flops=pairs * 2 * rows * width * 3072, transcendentals=0, bytes_accessed=24 * 1024 * 1024
        ),
        input_output_aliases={9 + at: at for at in range(len(before))},
        name="attend",
    )(scal, tokens, vec, sines, cosines, *pieces, *before)


CDF_POLY = (
    -0.020695917308330536,
    0.09534552693367004,
    -0.15029412508010864,
    0.07120334357023239,
    -0.011180647648870945,
    0.05997580662369728,
    0.08762594312429428,
    0.11413583159446716,
    0.12694157660007477,
    0.12694266438484192,
)
CDF_SLOPE = 0.45 / math.sqrt(2.0)


def gelu_pair(x):
    size = jnp.abs(x)
    t = 1.0 / (1.0 + CDF_SLOPE * size)
    bell = jnp.exp2(x * x * (-0.5 / math.log(2.0)))
    poly = CDF_POLY[0]
    for value in CDF_POLY[1:]:
        poly = poly * t + value
    tail = poly * t * bell
    cdf = jnp.where(x < 0.0, tail, 1.0 - tail)
    return x * cdf, cdf + x * bell * (1.0 / math.sqrt(2.0 * math.pi))


def moments(z):
    center = z - jnp.mean(z, axis=-1, keepdims=True)
    r = lax.rsqrt(jnp.mean(center * center, axis=-1, keepdims=True) + EPS_NORM)
    return center * r, r


def norm_back(grad, xh, r, gain):
    dxh = grad * gain
    return r * (
        dxh - jnp.mean(dxh, axis=-1, keepdims=True) - xh * jnp.mean(dxh * xh, axis=-1, keepdims=True)
    )


def total(values):
    return jnp.sum(values, axis=0, keepdims=True)


def out_copies(scal, pieces, out_mat, sem, place):
    return [
        pltpu.make_async_copy(
            source.at[place, :, pl.ds(0, 384)],
            out_mat.at[block_at(scal[base + place]), pl.ds(pl.multiple_of(half * 384, 128), 384)],
            sem,
        )
        for source, base, half in sources(scal, pieces)
    ]


def down_copies(scal, pieces, down_mat, sem, place):
    return [
        pltpu.make_async_copy(
            source.at[place],
            down_mat.at[pl.ds(pl.multiple_of(scal[PLANE_AT + base + place] * 192 + half * 96, 32), 96)],
            sem,
        )
        for source, base, half in sources(scal, pieces)
    ]


def per_core(scal, body):
    for core in range(2):

        @pl.when(scal[CORE_AT] == core)
        def _(core=core):
            body(core)


def send_block(scal, source, outs, side, block, cut, sem, table=PLAIN_AT):
    place = scal[table + 16 * side + block]
    if side == 0:
        pltpu.make_async_copy(source, cut(outs[0], place), sem).start()
        return
    for part in range(2):

        @pl.when(place // 8 == part)
        def _(part=part):
            pltpu.make_async_copy(source, cut(outs[1 + part], lax.rem(place, 8)), sem).start()


def block_shapes(rows, cols):
    return tuple(jax.ShapeDtypeStruct((count, rows, cols), LOW) for count in (16, 8, 8))


def up_fetch(scal, pieces, up_mat, sems, first):
    def fetch(core):
        for unit in range(4):
            near = 0 if unit // 2 == core else 2

            def start(place, carry, unit=unit, near=near):
                for index in (near, near + 1):
                    pltpu.make_async_copy(
                        pieces[index].at[place, :, pl.ds(384 + 768 * (unit % 2), 768)],
                        up_mat.at[unit, block_at(scal[8 * index + place])],
                        sems.at[first + unit],
                    ).start()
                return carry

            lax.fori_loop(0, 8, start, 0)

    per_core(scal, fetch)


def open_kernel(
    scal, tokens, vec, *refs
):
    ctx, pieces = refs[0], refs[1:5]
    norm_low, xh1, r1, act, slope, out_mat, up_mat, sem_in = refs[5:]
    step = pl.program_id(0)
    rows, width = tokens.shape

    @pl.when(step == 0)
    def _():
        start_copies(partial(out_copies, scal, pieces, out_mat, sem_in.at[0]), 8)
        up_fetch(scal, pieces, up_mat, sem_in, 1)
        wait_for(out_mat, sem_in.at[0])

        def first(at):
            attn = dot(ctx[at, :], out_mat[...], 1, 0) + vec[6:7, :]
            hat, r = moments(tokens[at, :].astype(WIDE) + attn)
            xh1[at, :] = hat
            r1[at, :] = jnp.broadcast_to(r, (r.shape[0], 128))
            norm_low[at, :] = (hat * vec[0:1, :] + vec[1:2, :]).astype(LOW)

        each(rows, CHUNK, first)

    wait_for(up_mat.at[step], sem_in.at[1 + step])

    bias = vec[pl.ds(8 + step, 1), :]
    spots = [pl.ds(CHUNK * index, CHUNK) for index in range(rows // CHUNK)]

    def front(at):
        return dot(norm_low[at, :], up_mat[step], 1, 0) + bias

    pre = front(spots[0])
    for index, at in enumerate(spots):
        ahead = front(spots[index + 1]) if index + 1 < len(spots) else None
        value, grad = gelu_pair(pre)
        act[0, at, :] = value.astype(LOW)
        slope[0, at, :] = grad
        pre = ahead


def open_ffn(scal, tokens, vec, ctx, two):
    rows, width = tokens.shape
    unit = pl.BlockSpec((1, rows, width), lambda j, _: (j, 0, 0))
    return pl.pallas_call(
        open_kernel,
        out_shape=(
            pltpu.HBM((rows, width), LOW),
            pltpu.HBM((rows, width), WIDE),
            pltpu.HBM((rows, 128), WIDE),
            pltpu.HBM((4, rows, width), LOW),
            pltpu.HBM((4, rows, width), WIDE),
        ),
        grid_spec=pltpu.PrefetchScalarGridSpec(
            num_scalar_prefetch=1,
            grid=(4,),
            in_specs=[whole((rows, width)), whole((16, width))]
            + [whole((rows, width))]
            + [any_space()] * 4,
            out_specs=[whole((rows, width))] * 2 + [whole((rows, 128)), unit, unit],
            scratch_shapes=[
                pltpu.VMEM((width, width), LOW),
                pltpu.VMEM((4, width, width), LOW),
                pltpu.SemaphoreType.DMA((5,)),
            ],
        ),
        compiler_params=pltpu.CompilerParams(
            dimension_semantics=("arbitrary",), vmem_limit_bytes=OPEN_VMEM_BYTES
        ),
        cost_estimate=pl.CostEstimate(
            flops=2 * rows * width * width * 9, transcendentals=0, bytes_accessed=18 * 1024 * 1024
        ),
        name="open_ffn",
    )(scal, tokens, vec, ctx, *two)


def feed_kernel(*refs):
    scal, cot, vec, ctx, act_in, slope_in, norm_in, xh_in, r_in = refs[:9]
    two_pieces, three_pieces = refs[9:13], refs[13:17]
    page_out, dh1_out, dctx_out, *outs = refs[17:26]
    two_outs, three_outs = outs[:3], outs[3:]
    (
        out_mat,
        up_mat,
        down_mat,
        norm_low,
        xh1,
        r1,
        act,
        slope,
        held,
        df,
        dpre,
        dattn,
        g_out,
        g_up,
        g_down,
        vec_out,
        vec_low,
        sem_in,
        sem_up,
        sem_down,
        sem_out,
        sem_page,
        sem_rows,
    ) = refs[26:]
    step = pl.program_id(0)
    rows, width = cot.shape
    length = scal[LENGTH_AT]

    @pl.when(step == 0)
    def _():
        start_copies(partial(down_copies, scal, three_pieces, down_mat, sem_in.at[0]), 8)
        for source, target, at in (
            (xh_in, xh1, 1),
            (act_in, act, 2),
            (norm_in, norm_low, 3),
            (r_in, r1, 4),
            (slope_in, slope, 5),
        ):
            pltpu.make_async_copy(source, target, sem_in.at[at]).start()
        up_fetch(scal, two_pieces, up_mat, sem_in, 6)
        start_copies(partial(out_copies, scal, two_pieces, out_mat, sem_in.at[10]), 8)
        vec_out[...] = jnp.zeros_like(vec_out)
        wait_for(xh1, sem_in.at[1])

        def prime(at):
            held[at, :] = xh1[at, :] * vec[0:1, :] + (vec[1:2, :] + vec[7:8, :])

        each(rows, SLAB, prime)
        wait_for(act, sem_in.at[2])
        wait_for(down_mat, sem_in.at[0])

    @pl.when(step < 4)
    def _():
        down_at = pl.ds(pl.multiple_of(step * width, width), width)
        held[...] += dot(act[step], down_mat[down_at, :], 1, 0)

    @pl.when(step == 3)
    def _():
        def second(at):
            hat, r = moments(held[at, :])
            place = lax.broadcasted_iota(jnp.int32, (SLAB, 1), 0) + at.start
            live = jnp.where(place < length, 1.0, 0.0)
            dattn[at, :] = ((hat * vec[2:3, :] + vec[3:4, :]) * live).astype(LOW)
            dy = cot[at, :].astype(WIDE) * live
            vec_out[2:3, :] += total(dy * hat)
            vec_out[3:4, :] += total(dy)
            dh2 = norm_back(dy, hat, r, vec[2:3, :])
            low = dh2.astype(LOW)
            df[at, :] = low
            vec_out[7:8, :] += total(low.astype(WIDE))
            held[at, :] = dh2

        each(rows, SLAB, second)
        pltpu.make_async_copy(dattn, page_out, sem_page).start()
        wait_for(slope, sem_in.at[5])
        wait_for(norm_low, sem_in.at[3])
        wait_for(r1, sem_in.at[4])
        wait_for(out_mat, sem_in.at[10])
        for unit in range(4):
            wait_for(up_mat.at[unit], sem_in.at[6 + unit])

    def send_up(slot, unit):
        at = pl.ds(pl.multiple_of(384 + 768 * lax.rem(unit, 2), 128), 768)
        for side in range(2):

            @pl.when((unit // 2 == scal[CORE_AT]) == (side == 0))
            def _(side=side):
                def body(block, carry):
                    send_block(
                        scal,
                        g_up.at[slot, block_at(block)],
                        two_outs,
                        side,
                        block,
                        lambda ref, place: ref.at[place, :, at],
                        sem_up.at[slot],
                    )
                    return carry

                lax.fori_loop(0, 16, body, 0)

    def send_down(slot, unit):
        def body(core):
            for part in range(8):
                send_block(
                    scal,
                    g_down.at[slot, pl.ds(96 * part, 96)],
                    three_outs,
                    (part % 2) ^ core,
                    4 * unit + part // 2,
                    lambda ref, place: ref.at[place, pl.ds(0, 96)],
                    sem_down.at[slot],
                    DEPTH_AT,
                )

        per_core(scal, body)

    def send_out():
        def on(core):
            def body(block, carry):
                for half in range(2):
                    send_block(
                        scal,
                        g_out.at[block_at(block), pl.ds(384 * half, 384)],
                        two_outs,
                        half ^ core,
                        block,
                        lambda ref, place: ref.at[place, :, pl.ds(0, 384)],
                        sem_out,
                    )
                return carry

            lax.fori_loop(0, 16, body, 0)

        per_core(scal, on)

    @pl.when(step >= 4)
    def _():
        unit = step - 4
        slot = lax.rem(unit, 2)
        down_at = pl.ds(pl.multiple_of(unit * width, width), width)

        @pl.when(unit >= 2)
        def _():
            wait_for(g_up.at[slot], sem_up.at[slot])
            wait_for(g_down.at[slot], sem_down.at[slot])

        def backward(at):
            grad = dot(df[at, :], down_mat[down_at, :], 1, 1) * slope[unit, at, :]
            low = grad.astype(LOW)
            dpre[at, :] = low
            vec_out[pl.ds(8 + unit, 1), :] += total(low.astype(WIDE))
            held[at, :] += dot(low, up_mat[unit], 1, 1)

        each(rows, rows, backward, True)

        def weights(at):
            g_down[slot, at, :] = dot(act[unit, :, at], df[...], 0, 0).astype(LOW)
            g_up[slot, at, :] = dot(norm_low[:, at], dpre[...], 0, 0).astype(LOW)

        each(width, width, weights, True)
        send_down(slot, unit)
        send_up(slot, unit)

    @pl.when(step == 7)
    def _():
        wait_for(dattn, sem_page)

        def last(at):
            grad, hat = held[at, :], xh1[at, :]
            vec_out[0:1, :] += total(grad * hat)
            vec_out[1:2, :] += total(grad)
            dh1 = norm_back(grad, hat, r1[at, :1], vec[0:1, :])
            held[at, :] = dh1
            pltpu.make_async_copy(held.at[at], dh1_out.at[at], sem_rows.at[0]).start()
            low = dh1.astype(LOW)
            dattn[at, :] = low
            vec_out[6:7, :] += total(low.astype(WIDE))

        each(rows, SLAB, last)
        vec_low[...] = jnp.zeros_like(vec_low)
        vec_low[0, 0:4, :] = vec_out[0:4, :].astype(LOW)
        vec_low[0, 4:5, :] = vec_out[6:7, :].astype(LOW)
        vec_low[1, 0:5, :] = vec_out[7:12, :].astype(LOW)

        def send_vectors(core):
            def body(block, carry):
                for half in range(2):
                    send_block(
                        scal,
                        vec_low.at[half],
                        three_outs,
                        half ^ core,
                        block,
                        lambda ref, place: ref.at[place, pl.ds(96, 8)],
                        sem_page,
                        DEPTH_AT,
                    )
                return carry

            lax.fori_loop(0, 16, body, 0)

        per_core(scal, send_vectors)

        def weights(at):
            g_out[at, :] = dot(ctx[:, at], dattn[...], 0, 0).astype(LOW)

        each(width, CHUNK, weights)
        send_out()

        def context(at):
            df[at, :] = dot(dattn[at, :], out_mat[...], 1, 1).astype(LOW)
            pltpu.make_async_copy(df.at[at], dctx_out.at[at], sem_rows.at[1]).start()

        each(rows, CHUNK, context)
        for slot in range(2):
            wait_for(g_up.at[slot], sem_up.at[slot])
            wait_for(g_down.at[slot], sem_down.at[slot])
        wait_for(g_out, sem_out)
        wait_for(held, sem_rows.at[0])
        wait_for(df, sem_rows.at[1])
        lax.fori_loop(0, 16, lambda _, carry: (wait_for(vec_low, sem_page), carry)[1], 0)


def feed(scal, cot, vec, ctx, opened, two, three):
    rows, width = cot.shape
    return pl.pallas_call(
        feed_kernel,
        out_shape=(
            jax.ShapeDtypeStruct((rows, width), LOW),
            jax.ShapeDtypeStruct((rows, width), WIDE),
            jax.ShapeDtypeStruct((rows, width), LOW),
        )
        + block_shapes(48, 384 + 2 * width)
        + block_shapes(104, width),
        grid_spec=pltpu.PrefetchScalarGridSpec(
            num_scalar_prefetch=1,
            grid=(8,),
            in_specs=[whole((rows, width)), whole((16, width)), whole((rows, width))]
            + [any_space()] * 13,
            out_specs=[any_space()] * 9,
            scratch_shapes=[
                pltpu.VMEM((width, width), LOW),
                pltpu.VMEM((4, width, width), LOW),
                pltpu.VMEM((4 * width, width), LOW),
                pltpu.VMEM((rows, width), LOW),
                pltpu.VMEM((rows, width), WIDE),
                pltpu.VMEM((rows, 128), WIDE),
                pltpu.VMEM((4, rows, width), LOW),
                pltpu.VMEM((4, rows, width), WIDE),
                pltpu.VMEM((rows, width), WIDE),
                pltpu.VMEM((rows, width), LOW),
                pltpu.VMEM((rows, width), LOW),
                pltpu.VMEM((rows, width), LOW),
                pltpu.VMEM((width, width), LOW),
                pltpu.VMEM((2, width, width), LOW),
                pltpu.VMEM((2, width, width), LOW),
                pltpu.VMEM((16, width), WIDE),
                pltpu.VMEM((2, 8, width), LOW),
                pltpu.SemaphoreType.DMA((11,)),
                pltpu.SemaphoreType.DMA((2,)),
                pltpu.SemaphoreType.DMA((2,)),
                pltpu.SemaphoreType.DMA,
                pltpu.SemaphoreType.DMA,
                pltpu.SemaphoreType.DMA((2,)),
            ],
        ),
        compiler_params=pltpu.CompilerParams(
            dimension_semantics=("arbitrary",), vmem_limit_bytes=FEED_VMEM_BYTES
        ),
        cost_estimate=pl.CostEstimate(
            flops=2 * rows * width * width * 27, transcendentals=0, bytes_accessed=32 * 1024 * 1024
        ),
        name="feed",
    )(scal, cot, vec, ctx, *opened, *two, *three)


def split_kernel(scal, attn, up, down, two_out, three_out):
    for core in range(2):

        @pl.when(scal[0] == core)
        def _(core=core):
            two_out[0, :, :384] = attn[3, :, 384 * core : 384 * (core + 1)].astype(LOW)
            two_out[0, :, 384:] = up[:, 1536 * core : 1536 * (core + 1)].astype(LOW)
            three_out[0] = down[96 * core : 96 * (core + 1), :].astype(LOW)


def split_weights(core, attn, up, down):
    width = attn.shape[2]
    shapes = ((1, 48, 384 + 2 * width), (1, 96, width))
    return pl.pallas_call(
        split_kernel,
        out_shape=tuple(jax.ShapeDtypeStruct(shape, LOW) for shape in shapes),
        grid_spec=pltpu.PrefetchScalarGridSpec(
            num_scalar_prefetch=1,
            grid=(1,),
            in_specs=[whole(attn.shape), whole(up.shape), whole(down.shape)],
            out_specs=[whole(shape) for shape in shapes],
        ),
        cost_estimate=pl.CostEstimate(flops=0, transcendentals=0, bytes_accessed=3 * 1024 * 1024),
        name="split_weights",
    )(core, attn, up, down)


def unattend_kernel(
    group,
    scal,
    tokens_in,
    sines,
    cosines,
    q_in,
    k_in,
    v_in,
    dctx_in,
    prob,
    *refs,
):
    mats_in, dq_out, dk_out, dv_out = refs[:4]
    outs = refs[4:7]
    (
    mats,
    right,
    ds_low,
    du_low,
    q_heads,
    d_heads,
    grads,
    sums,
    sem,
    sem_out,
    sem_sums,
    tokens,
    sem_tokens,
    ) = refs[7:]
    pair = pl.program_id(0)
    rows, width = tokens.shape
    half = width // 2
    copy_tokens = pltpu.make_async_copy(tokens_in, tokens, sem_tokens)
    scale = HEAD_DIM ** (-0.5)

    @pl.when(pair == 0)
    def _():
        cols = mats.shape[1]
        lane_at = pl.ds(group * cols, cols)
        fetch = pltpu.make_async_copy(mats_in.at[3, :, lane_at], mats, sem)
        fetch.start()
        copy_tokens.start()
        right[:, : width // 2] = sines[...].astype(LOW)
        right[:, width // 2 : width] = cosines[...].astype(LOW)
        fetch.wait()

    lanes = pl.ds(pl.multiple_of(pair * 128, 128), 128)
    right[:, width:] = k_in[...]
    rel = mats[:, lanes]
    low_masks, wide_masks = head_masks(LOW), head_masks(WIDE)

    def score(at):
        sin, cos = sines[at, :], cosines[at, :]
        dq = None
        for head in range(2):
            spot = pl.ds(pl.multiple_of(head * rows + at.start, at.size), at.size)
            dctx = dctx_in[at, :] * low_masks[head]
            d_heads[spot, :] = dctx
            q_heads[spot, :] = q_in[at, :] * low_masks[head]
            p = prob[head, at, :].astype(WIDE)
            dp = dot(dctx, v_in[...], 1, 1)
            ds = (p * (dp - jnp.sum(p * dp, axis=-1, keepdims=True))).astype(LOW)
            ds_low[spot, :] = ds
            dl = dot(ds, right[...], 1, 0) * scale
            ls, lc = dl[:, :half], dl[:, half:width]
            du = jnp.concatenate(
                [(lc * sin - ls * cos).astype(LOW), (ls * sin + lc * cos).astype(LOW)], axis=1
            )
            du_low[spot, :] = du
            part = (dl[:, width:] + dot(du, rel, 1, 0)) * wide_masks[head]
            dq = part if dq is None else dq + part
        dq_out[at, lanes] = dq.astype(LOW)

    each(rows, rows, score, True)
    dv_out[:, lanes] = dot(prob[...].reshape(2 * rows, rows), d_heads[...], 0, 0).astype(LOW)
    dk_out[:, lanes] = (dot(ds_low[...], q_heads[...], 0, 0) * scale).astype(LOW)
    grads[3, :, lanes] = dot(du_low[...], q_heads[...], 0, 0).astype(LOW)

    @pl.when(pair == pl.num_programs(0) - 1)
    def _():
        copy_tokens.wait()

        def weights(at):
            x = tokens[:, at]
            grads[0, at, :] = dot(x, dq_out[...], 0, 0).astype(LOW)
            grads[1, at, :] = dot(x, dk_out[...], 0, 0).astype(LOW)
            grads[2, at, :] = dot(x, dv_out[...], 0, 0).astype(LOW)

        each(width, CHUNK, weights)

        sums[...] = jnp.zeros_like(sums)
        sums[0, 0:1, :] = total(dq_out[...].astype(WIDE)).astype(LOW)
        sums[1, 0:1, :] = total(dv_out[...].astype(WIDE)).astype(LOW)

        def on(core):
            def body(block, carry):
                for slot in range(4):
                    row = turned(block) if slot == 3 else block
                    at = pl.ds(48 * (slot % 2), 48)
                    send_block(
                        scal,
                        grads.at[slot, block_at(row)],
                        outs,
                        (slot // 2) ^ core,
                        block,
                        lambda ref, place, at=at: ref.at[place, at],
                        sem_out,
                    )
                for half in range(2):
                    send_block(
                        scal,
                        sums.at[half],
                        outs,
                        half ^ core,
                        block,
                        lambda ref, place: ref.at[place, pl.ds(96, 8)],
                        sem_sums,
                    )
                return carry

            lax.fori_loop(0, 16, body, 0)

        per_core(scal, on)
        wait_for(grads, sem_out)
        lax.fori_loop(0, 16, lambda _, carry: (wait_for(sums, sem_sums), carry)[1], 0)


def unattend(group, scal, tokens, sines, cosines, q, k, v, dctx, prob, mats):
    rows, width = tokens.shape
    pairs, cols = BACK_PAIRS, 128 * BACK_PAIRS
    low = jax.ShapeDtypeStruct((rows, cols), LOW)
    lane_block = pl.BlockSpec((rows, 128), lambda p, _: (0, group * pairs + p))
    return pl.pallas_call(
        partial(unattend_kernel, group),
        out_shape=(low, low, low) + block_shapes(104, cols),
        grid_spec=pltpu.PrefetchScalarGridSpec(
            num_scalar_prefetch=1,
            grid=(pairs,),
            in_specs=[
                any_space(),
                whole((rows, half_of(width))),
                whole((rows, half_of(width))),
                lane_block,
                lane_block,
                lane_block,
                lane_block,
                pl.BlockSpec((2, rows, rows), lambda p, _: (group * pairs + p, 0, 0)),
            ]
            + [any_space()],
            out_specs=[whole((rows, cols))] * 3 + [any_space()] * 3,
            scratch_shapes=[
                pltpu.VMEM((width, cols), LOW),
                pltpu.VMEM((rows, width + 128), LOW),
                pltpu.VMEM((2 * rows, rows), LOW),
                pltpu.VMEM((2 * rows, width), LOW),
                pltpu.VMEM((2 * rows, 128), LOW),
                pltpu.VMEM((2 * rows, 128), LOW),
                pltpu.VMEM((4, width, cols), LOW),
                pltpu.VMEM((2, 8, cols), LOW),
                pltpu.SemaphoreType.DMA,
                pltpu.SemaphoreType.DMA,
                pltpu.SemaphoreType.DMA,
                pltpu.VMEM((rows, width), LOW),
                pltpu.SemaphoreType.DMA,
            ],
        ),
        compiler_params=pltpu.CompilerParams(
            dimension_semantics=("arbitrary",), vmem_limit_bytes=ATTN_VMEM_BYTES
        ),
        cost_estimate=pl.CostEstimate(
            flops=pairs * 2 * rows * width * 5000, transcendentals=0, bytes_accessed=24 * 1024 * 1024
        ),
        name="unattend",
    )(scal, tokens, sines, cosines, q, k, v, dctx, prob, mats)


def half_of(width):
    return width // 2


def input_grad_kernel(dh1, *refs):
    parts, (mats, out) = refs[: 3 * BACK_GROUPS], refs[3 * BACK_GROUPS :]
    slot = pl.program_id(0)

    @pl.when(slot == 0)
    def _():
        out[...] = dh1[...]

    for part in range(3):

        @pl.when(slot == part)
        def _(part=part):
            def rows_of(at):
                left = jnp.concatenate(
                    [parts[3 * g + part][at, :] for g in range(BACK_GROUPS)], axis=1
                )
                out[at, :] += dot(left, mats[0], 1, 1)

            each(dh1.shape[0], CHUNK, rows_of)


def input_grad(dh1, parts, mats):
    rows, width = dh1.shape
    slim = whole((rows, width // BACK_GROUPS))
    return pl.pallas_call(
        input_grad_kernel,
        out_shape=jax.ShapeDtypeStruct((rows, width), WIDE),
        grid=(3,),
        in_specs=[whole((rows, width))]
        + [slim] * (3 * BACK_GROUPS)
        + [pl.BlockSpec((1, width, width), lambda j: (j, 0, 0))],
        out_specs=whole((rows, width)),
        compiler_params=pltpu.CompilerParams(
            dimension_semantics=("arbitrary",), vmem_limit_bytes=ATTN_VMEM_BYTES
        ),
        cost_estimate=pl.CostEstimate(
            flops=2 * rows * width * width * 3, transcendentals=0, bytes_accessed=10 * 1024 * 1024
        ),
        name="input_grad",
    )(dh1, *parts, mats)


PAIRS = 3
BACK_PAIRS = 2
BACK_GROUPS = 3


def local(
    tokens,
    boxes,
    lengths,
    cotangent,
    attn_weight,
    up_weight,
    down_weight,
    vectors,
    attn_first,
    up_first,
    down_first,
    vector_first,
    attn_second,
    up_second,
    down_second,
    vector_second,
):
    chip, core = lax.axis_index("fsdp"), lax.axis_index("rep")
    width = tokens.shape[2]
    cols = width - width // BACK_GROUPS
    first = core == 0
    page = tokens[0]
    same = (ORDERS[0], ORDERS[0])

    near = jnp.where(first, attn_weight[:2], attn_weight[2:5:2]).astype(LOW).reshape(1, 96, width)
    near_far = hop(near, 0)
    core_at = after(core.astype(jnp.int32)[None], near)
    two, three = split_weights(core_at, attn_weight, up_weight, down_weight)
    three_far = hop(three, 0, PLANE_FIRST)
    vec = lax.dynamic_update_slice(
        jnp.zeros((vectors.shape[0], width), LOW),
        after(vectors.astype(LOW), near),
        (jnp.int32(0), chip * vectors.shape[1]),
    )
    scal = block_scalars(chip, core, lengths[0])
    near, near_far, two, vec, place, scal = sync(near, near_far, two, vec, boxes[0], scal)

    near = join(near, near_far)
    near_far = hop(near, 1)
    vec_far = hop(vec, 0, same)
    quarter = width // 4
    frequency = jnp.exp(jnp.arange(quarter).astype(WIDE) * (-math.log(10000.0) / quarter))
    place = place.astype(WIDE)
    angles = jnp.concatenate([place[0][:, None] * frequency, place[1][:, None] * frequency], axis=1)
    sines, cosines = jnp.sin(angles), jnp.cos(angles)
    near, near_far, vec, vec_far, two, three, three_far, sines, cosines = sync(
        near, near_far, vec, vec_far, two, three, three_far, sines, cosines
    )

    near = join(near, near_far)
    near_far = hop(near, 2)
    two_far = hop(two, 0)
    vec = vec + vec_far
    vec_far = hop(vec, 1, same)
    three = join(three, three_far)
    three_far = hop(after(three, vec), 1, PLANE_FIRST)
    near, near_far, vec, vec_far, two, two_far, three = sync(
        near, near_far, vec, vec_far, two, two_far, three
    )

    near = join(near, near_far)
    near_far = hop(near, 3)
    near_swap = swap_cores(near)
    vec = vec + vec_far
    vec_far = hop(vec, 2, same)
    two = join(two, two_far)
    two_far = hop(two, 1)
    near_far, near_swap, vec, vec_far, two, two_far, three, three_far = sync(
        near_far, near_swap, vec, vec_far, two, two_far, three, three_far
    )

    near_far_swap = swap_cores(near_far)
    vec = vec + vec_far
    vec_far = hop(vec, 3, same)
    two = join(two, two_far)
    two_far = hop(two, 2)
    three = join(three, three_far)
    three_far = hop(three, 2, PLANE_FIRST)
    vec, near_far_swap, two, three = sync(vec + vec_far, near_far_swap, two, three)
    vec = jnp.pad(vec.astype(WIDE), ((0, 16 - vec.shape[0]), (0, 0)))
    pieces = (near, near_far, near_swap, near_far_swap)

    def go(group, tick, before):
        return attend(
            group, after(scal, tick), page, vec, sines, cosines, pieces, before
        )

    kept = go(0, two, [])
    two, two_far, three, three_far, *kept = sync(two, two_far, three, three_far, *kept)

    two = join(two, two_far)
    two_far = hop(two, 3)
    three = join(three, three_far)
    two_swap = swap_cores(two)
    three_swap = swap_cores(three)
    kept = go(1, three, kept)
    two_far, two_swap, three_swap, *kept = sync(two_far, two_swap, three_swap, *kept)

    two_far_swap = swap_cores(two_far)
    three_far = hop(after(three, two_far), 3, PLANE_FIRST)
    two_pieces = (two, two_far, two_swap, two_far_swap)
    norm_low, xh1, r1, act, slope = open_ffn(scal, page, vec, kept[3], two_pieces)
    three_far, r1 = sync(three_far, r1)

    three_pieces = (three, three_far, three_swap, swap_cores(three_far))
    page_out, dh1, dctx, *sent = feed(
        scal,
        cotangent[0],
        vec,
        kept[3],
        (act, slope, norm_low, xh1, r1),
        two_pieces,
        three_pieces,
    )
    two_sent, three_sent = sent[:3], sent[3:]

    three_swap, two_swap, three_low, two_low, mark = sync(
        swap_cores(three_sent[2]), two_sent[2], three_sent[1], two_sent[1], scal
    )
    two_swap = swap_cores(two_swap)
    three_high = add_up([three_sent[0][8:], three_swap])
    three_far = hop(three_high, 3, DEPTH_FIRST)
    two_swap, three_low, two_low, mark = sync(
        after(two_swap, three_high), three_low, two_low, mark
    )
    two_high = add_up([two_sent[0][8:], two_swap])
    two_far = hop(two_high, 3)
    three_low = swap_cores(three_low)
    two_low = swap_cores(two_low)

    def undo(group, tick):
        return unattend(
            group,
            after(scal, tick),
            page,
            sines,
            cosines,
            *kept[:3],
            dctx,
            pltpu.with_memory_space_constraint(kept[4], pltpu.HBM),
            kept[5],
        )

    def beside(left, right):
        return jnp.concatenate([left, right], axis=2)

    back = [undo(0, mark)]
    two_far, three_low, two_low, mark, *one_sent = sync(
        two_far, three_low, two_low, back[0][0], *back[0][3:]
    )

    two_terms, two_high = halve([two_sent[0][:8], two_low, two_far])
    two_far = hop(two_high, 2)
    one_swap = swap_cores(one_sent[2])
    one_low = swap_cores(one_sent[1])
    back.append(undo(1, mark))
    two_far, three_far, one_swap, one_low, mark, *next_sent = sync(
        two_far, three_far, one_swap, one_low, back[1][0], *back[1][3:]
    )

    next_swap = swap_cores(next_sent[2])
    three_terms, three_high = halve([three_sent[0][:8], three_low, three_far])
    three_far = hop(three_high, 2, DEPTH_FIRST)
    two_terms, two_high = halve(two_terms + [two_far])
    two_far = hop(two_high, 1)
    next_swap, next_low, mark, three_high, two_high = sync(
        next_swap, next_sent[1], mark, three_high, two_high
    )
    one_high = beside(
        add_up([one_sent[0][8:], one_swap]), add_up([next_sent[0][8:], next_swap])
    )
    one_far = hop(one_high, 3)
    next_low = swap_cores(next_low)
    back.append(undo(2, mark))
    two_far, three_far, one_far, next_low, *end_sent = sync(
        two_far, three_far, one_far, next_low, *back[2][3:]
    )

    end_high = add_up([end_sent[0][8:], swap_cores(end_sent[2])])
    end_far = hop(end_high, 3)
    end_low, one_far, three_far, two_far, mark = sync(
        end_sent[1], one_far, three_far, two_far, end_high
    )
    end_low = swap_cores(end_low)
    two_terms, two_high = halve(two_terms + [two_far])
    two_far = hop(two_high, 0)
    one_terms = [beside(one_sent[0][:8], next_sent[0][:8]), beside(one_low, next_low), one_far]
    one_terms, one_high = halve(one_terms)
    one_far = hop(one_high, 2)
    three_terms, three_high = halve(three_terms + [three_far])
    three_far = hop(three_high, 1, DEPTH_FIRST)
    end_far, end_low, one_far, three_far, two_far, mark = sync(
        end_far, end_low, one_far, three_far, two_far, mark
    )

    end_terms, end_high = halve([end_sent[0][:8], end_low, end_far])
    end_far = hop(end_high, 2)
    one_terms, one_high = halve(one_terms + [one_far])
    one_far = hop(one_high, 1)
    three_terms, three_high = halve(three_terms + [three_far])
    three_far = hop(three_high, 0, DEPTH_FIRST)
    two_mine = add_up(two_terms + [two_far])[0]
    two_other = swap_cores(two_mine)
    token_grad = input_grad(
        after(dh1, mark, two_mine), [part for b in back for part in b[:3]], kept[5]
    )
    end_far, one_far, three_far, two_other, token_grad = sync(
        end_far, one_far, three_far, two_other, token_grad
    )

    end_terms, end_high = halve(end_terms + [end_far])
    end_far = hop(end_high, 1)
    one_terms, one_high = halve(one_terms + [one_far])
    one_far = hop(one_high, 0)
    three_mine = add_up(three_terms + [three_far])[0]
    three_other = swap_cores(three_mine)
    two_sum = by_half(core, (two_mine, two_other))
    up_sum = jnp.concatenate([two_sum[0][:, 384:], two_sum[1][:, 384:]], axis=1)
    up_next = adam_update(up_weight, up_first, up_second, up_sum, UP_RATE, WEIGHT_DECAY)
    end_far, one_far, three_other, up_copy, up_new, up_first_new, up_second_new = sync(
        end_far, one_far, three_other, up_next[0].astype(LOW), *up_next
    )

    end_terms, end_high = halve(end_terms + [end_far])
    end_far = hop(end_high, 0)
    three_sum = by_half(core, (three_mine, three_other))
    down_next = adam_update(
        down_weight,
        down_first,
        down_second,
        jnp.concatenate([part[:96] for part in three_sum]),
        DOWN_RATE,
        WEIGHT_DECAY,
    )
    one_mine = add_up(one_terms + [one_far])[0]
    end_far, one_mine, down_copy, down_new, down_first_new, down_second_new = sync(
        end_far, one_mine, down_next[0].astype(LOW), *down_next
    )

    one_mine = jnp.concatenate([one_mine, add_up(end_terms + [end_far])[0]], axis=1)
    one_sum = by_half(core, (one_mine, swap_cores(one_mine)))
    vec_grad = jnp.concatenate(
        [
            three_sum[0][96:100],
            one_sum[0][96:97],
            one_sum[1][96:97],
            three_sum[0][100:101],
            three_sum[1][96:101],
        ]
    )
    vec_sum = lax.dynamic_slice(
        vec_grad, (jnp.int32(0), chip * vectors.shape[1]), vectors.shape
    )
    attn_sum = jnp.stack(
        [
            one_sum[0][:48],
            one_sum[0][48:96],
            one_sum[1][:48],
            jnp.concatenate([two_sum[0][:, :384], two_sum[1][:, :384]], axis=1),
            one_sum[1][48:96],
        ]
    )
    layer_out, token_grad = page_out[None], token_grad[None]
    attn_rates = jnp.array(ATTN_RATES, jnp.float32)[:, None, None]
    attn_new, attn_first_new, attn_second_new = adam_update(
        attn_weight, attn_first, attn_second, attn_sum, attn_rates, WEIGHT_DECAY
    )
    vectors_new, vector_first_new, vector_second_new = adam_update(
        vectors, vector_first, vector_second, vec_sum, VECTOR_RATE, 0.0
    )
    return (
        layer_out,
        token_grad,
        attn_new,
        up_new,
        down_new,
        vectors_new,
        attn_first_new,
        up_first_new,
        down_first_new,
        vector_first_new,
        attn_second_new,
        up_second_new,
        down_second_new,
        vector_second_new,
        attn_new.astype(jnp.bfloat16),
        up_copy,
        down_copy,
        vectors_new.astype(jnp.bfloat16),
    )


def local_general(
    tokens,
    boxes,
    lengths,
    cotangent,
    attn_weight,
    up_weight,
    down_weight,
    vectors,
    attn_first,
    up_first,
    down_first,
    vector_first,
    attn_second,
    up_second,
    down_second,
    vector_second,
):
    lowered = (
        attn_weight.astype(jnp.bfloat16),
        up_weight.astype(jnp.bfloat16),
        down_weight.astype(jnp.bfloat16),
        vectors.astype(jnp.bfloat16),
    )
    gathered = (
        lax.all_gather(lowered[0], "fsdp", axis=1, tiled=True),
        lax.all_gather(lowered[1], "fsdp", axis=0, tiled=True),
        lax.all_gather(lowered[2], "fsdp", axis=0, tiled=True),
        lax.all_gather(lowered[3], "fsdp", axis=1, tiled=True),
    )

    def forward_step(carry, page):
        token_row_block, box_rows, page_length = page
        return (carry, forward_page(gathered, token_row_block, box_rows, page_length))

    _, (layer_out, saved_all) = lax.scan(forward_step, None, (tokens, boxes, lengths))
    backward_weights = (
        lax.all_gather(lowered[0], "fsdp", axis=1, tiled=True),
        lax.all_gather(lowered[1], "fsdp", axis=0, tiled=True),
        lax.all_gather(lowered[2], "fsdp", axis=0, tiled=True),
        lax.all_gather(lowered[3], "fsdp", axis=1, tiled=True),
    )
    model_width = gathered[0].shape[2]
    ffn_width = gathered[1].shape[1]
    zero_grads = (
        jnp.zeros((5, model_width, model_width), jnp.float32),
        jnp.zeros((model_width, ffn_width), jnp.float32),
        jnp.zeros((ffn_width, model_width), jnp.float32),
        jnp.zeros(gathered[3].shape, jnp.float32),
    )

    def backward_step(totals, page):
        token_row_block, box_rows, page_length, upstream, saved_state = page
        token_grad, grads = backward_page(
            backward_weights, token_row_block, box_rows, page_length, upstream, saved_state
        )
        return (jax.tree.map(jnp.add, totals, grads), token_grad)

    totals, token_grad = lax.scan(
        backward_step, zero_grads, (tokens, boxes, lengths, cotangent, saved_all)
    )
    shards = (
        lax.psum_scatter(totals[0], "fsdp", scatter_dimension=1, tiled=True),
        lax.psum_scatter(totals[1], "fsdp", scatter_dimension=0, tiled=True),
        lax.psum_scatter(totals[2], "fsdp", scatter_dimension=0, tiled=True),
        lax.psum_scatter(totals[3], "fsdp", scatter_dimension=1, tiled=True),
    )
    reduced = (
        lax.psum(shards[0].astype(jnp.bfloat16), "rep").astype(jnp.float32),
        lax.psum(shards[1].astype(jnp.bfloat16), "rep").astype(jnp.float32),
        lax.psum(shards[2].astype(jnp.bfloat16), "rep").astype(jnp.float32),
        lax.psum(shards[3].astype(jnp.bfloat16), "rep").astype(jnp.float32),
    )
    attn_rates = jnp.array(ATTN_RATES, jnp.float32)[:, None, None]
    attn_new, attn_first_new, attn_second_new = adam_update(
        attn_weight, attn_first, attn_second, reduced[0], attn_rates, WEIGHT_DECAY
    )
    up_new, up_first_new, up_second_new = adam_update(
        up_weight, up_first, up_second, reduced[1], UP_RATE, WEIGHT_DECAY
    )
    down_new, down_first_new, down_second_new = adam_update(
        down_weight, down_first, down_second, reduced[2], DOWN_RATE, WEIGHT_DECAY
    )
    vectors_new, vector_first_new, vector_second_new = adam_update(
        vectors, vector_first, vector_second, reduced[3], VECTOR_RATE, 0.0
    )
    return (
        layer_out,
        token_grad,
        attn_new,
        up_new,
        down_new,
        vectors_new,
        attn_first_new,
        up_first_new,
        down_first_new,
        vector_first_new,
        attn_second_new,
        up_second_new,
        down_second_new,
        vector_second_new,
        attn_new.astype(jnp.bfloat16),
        up_new.astype(jnp.bfloat16),
        down_new.astype(jnp.bfloat16),
        vectors_new.astype(jnp.bfloat16),
    )


def solution(mesh):
    blocked = mesh.shape["fsdp"] == 16 and mesh.shape["rep"] == 2
    return jax.shard_map(
        local if blocked else local_general,
        mesh=mesh,
        in_specs=(
            P(("fsdp", "rep"), None, None),
            P(("fsdp", "rep"), None, None),
            P(("fsdp", "rep")),
            P(("fsdp", "rep"), None, None),
            P(None, "fsdp", None),
            P("fsdp", None),
            P("fsdp", None),
            P(None, "fsdp"),
            P(None, "fsdp", None),
            P("fsdp", None),
            P("fsdp", None),
            P(None, "fsdp"),
            P(None, "fsdp", None),
            P("fsdp", None),
            P("fsdp", None),
            P(None, "fsdp"),
        ),
        out_specs=(
            P(("fsdp", "rep"), None, None),
            P(("fsdp", "rep"), None, None),
            P(None, "fsdp", None),
            P("fsdp", None),
            P("fsdp", None),
            P(None, "fsdp"),
            P(None, "fsdp", None),
            P("fsdp", None),
            P("fsdp", None),
            P(None, "fsdp"),
            P(None, "fsdp", None),
            P("fsdp", None),
            P("fsdp", None),
            P(None, "fsdp"),
            P(None, "fsdp", None),
            P("fsdp", None),
            P("fsdp", None),
            P(None, "fsdp"),
        ),
        check_vma=False,
    )
```
